32 devices in a mesh: dp: 16 (over z, y, x), tensor: 2 (over core).
Axes of the slice: x: 2, y: 2, z: 4, core: 2. Of those that a mesh axis runs over, the one named last changes fastest.
Arguments:
- inputs: bfloat16 [8192, 768], P(('dp', 'tensor')), may hold values from -6 to 6
- gain_attn: bfloat16 [768], P('dp'), may hold values from 0.5 to 1.5
- w_qkv: bfloat16 [3, 768, 768], P(None, 'dp', 'tensor')
- w_out: bfloat16 [768, 768], P('tensor', 'dp'), may hold values from -1.75 to 1.75
- gain_ffn: bfloat16 [768], P('dp'), may hold values from 0.5 to 1.5
- w_in: bfloat16 [768, 2, 1152], P('dp', None, 'tensor'), may hold values from -0.21875 to 0.21875
- w_down: bfloat16 [1152, 768], P('tensor', 'dp'), may hold values from -0.1875 to 0.1875
- cotangent: bfloat16 [8192, 768], P(('dp', 'tensor')), may hold values from -6 to 6
- segments: int32 [32, 256], P('dp'), may hold values from 0 to 2, never falling along the last dimension, each value on 1 to 160 neighbouring positions
- lengths: int32 [32], P('dp'), may hold values from 192 to 256
- counts: int32 [16], P('dp'), may hold values from 1 to 2, as said below
Outputs:
- output: bfloat16 [8192, 768], P(('dp', 'tensor'))
- grad_inputs: float32 [8192, 768], P(('dp', 'tensor'))
- grad_gain_attn: float32 [768], P('dp')
- grad_qkv: float32 [3, 768, 768], P(None, 'dp', 'tensor')
- grad_out: float32 [768, 768], P('tensor', 'dp')
- grad_gain_ffn: float32 [768], P('dp')
- grad_in: float32 [768, 2, 1152], P('dp', None, 'tensor')
- grad_down: float32 [1152, 768], P('tensor', 'dp')
The draws below stay inside these ranges and needn't reach their ends.
Inputs may be any that keep to these rules, and one draw needn't show every extreme that they name: `counts`: each group uses 1 to 2 of its block slots; some group uses all 2 and some exactly 1. `segments`: along each block the ids start at 0, never fall and end at 2 or below; a sequence holds at most 256 * 5 // 8 slots.
All inputs are finite; a program needn't handle non-finite values.
Results may differ from the reference program's by a relative error of at most 0.019.
Values may be sent and summed in bfloat16 or wider, within the bound.
No kernel may reach another device: no remote copies, remote signals or barrier semaphores. Data moves between devices by JAX's collectives and lax.ppermute only.
A program may use at most 128 MiB of HBM per device.

```python
import math
import jax
import jax.numpy as jnp
import numpy as np
from jax import lax

D = 768
HD = 64
FF = 1152
SEQ = 256
BLK_DEV = 2
GROUPS = 16
BLOCKS = 32
TOKENS = 8192


def draw_w_qkv(key, part):
    weights = jax.random.normal(key, (3, D, D), jnp.float32) * D ** (-0.5)
    return weights.astype(jnp.bfloat16)


def draw_counts(key, part):
    first_key = jax.random.fold_in(key, 11)
    second_key = jax.random.fold_in(key, 12)
    third_key = jax.random.fold_in(key, 13)
    fourth_key = jax.random.fold_in(key, 14)
    first_draw = jax.random.randint(first_key, (GROUPS,), 1, BLK_DEV + 1)
    second_draw = jax.random.randint(second_key, (GROUPS,), 1, BLK_DEV + 1)
    group_counts = jnp.minimum(first_draw, second_draw)
    full_at = jax.random.randint(third_key, (), 0, GROUPS)
    low_at = (full_at + jax.random.randint(fourth_key, (), 1, GROUPS)) % GROUPS
    index_row = jnp.arange(GROUPS, dtype=jnp.int32)
    group_counts = jnp.where(index_row == full_at, BLK_DEV, group_counts)
    group_counts = jnp.where(index_row == low_at, 1, group_counts)
    return group_counts.astype(jnp.int32)


def with_ends(array, rng, smallest, largest):
    dims = array.shape
    index_at = [jax.random.randint(jax.random.fold_in(rng, axis), (), 0, dims[axis]) for axis in range(len(dims))]
    array = array.at[tuple(index_at)].set(smallest)
    longest = dims.index(max(dims))
    index_at[longest] = (index_at[longest] + 1) % dims[longest]
    return array.at[tuple(index_at)].set(largest)


def block_scale(stream_key, extent, shards, low, top_value):
    factor_of = 1.0
    for axis_at, parts in shards:
        steps = jax.random.uniform(jax.random.fold_in(jax.random.fold_in(stream_key, 6), axis_at), (parts,), jnp.float32, low / len(shards), top_value / len(shards))
        factor_of = factor_of * jnp.repeat(jnp.exp(steps), extent[axis_at] // parts).reshape((-1,) + (1,) * (len(extent) - 1 - axis_at))
    return factor_of


def profile(amount, total, reach, slope):
    portions = [(1 << 20) // math.isqrt(standing ** slope) + 1 for standing in range(2, amount + 1)]
    rest, given = total - reach - (amount - 1), [1] * (amount - 1)
    while rest > 0:
        candidates = [i for i in range(amount - 1) if given[i] < reach]
        whole, remaining = sum([portions[i] for i in candidates]), rest
        for i in candidates:
            more = min(reach - given[i], max(1, remaining * portions[i] // whole), rest)
            given[i] = given[i] + more
            rest = rest - more
    return np.array([reach] + given)


def uneven_parts(stream_key, count, total, most, slope):
    if count == 2:
        one = jax.random.randint(stream_key, (), max(1, total - most), min(most, total - 1) + 1)
        return jnp.stack([one, total - one])
    sizes = jnp.asarray(profile(count, total, most, slope), jnp.int32)
    pairs = (count - 1) // 2
    giver, taker = sizes[1:1 + 2 * pairs:2], sizes[2:2 + 2 * pairs:2]
    margin = jnp.minimum(giver - 1, most - taker)
    shifted = jax.random.randint(jax.random.fold_in(stream_key, 1), (pairs,), 0, 1 << 20) % (margin + 1)
    sizes = sizes.at[1:1 + 2 * pairs:2].set(giver - shifted).at[2:2 + 2 * pairs:2].set(taker + shifted)
    return sizes[jax.random.permutation(jax.random.fold_in(stream_key, 2), count)]


def gaussian(own_key, extent, spread, limit, pieces=(), held_as=jnp.bfloat16):
    entries = spread * jax.random.normal(own_key, extent, jnp.float32)
    if pieces:
        entries = entries * block_scale(own_key, extent, pieces, -0.22, 0.18)
    return jnp.clip(entries, -limit, limit).astype(held_as)


def setup_inputs(seed: int = 0) -> dict:
    arg_keys = jax.random.split(jax.random.key(seed), 12)
    inputs = gaussian(arg_keys[0], (TOKENS, D), 1.0, 6.0, ((0, 32),))
    gain_attn = jnp.clip(1.0 + 0.1 * jax.random.normal(arg_keys[1], (D,), jnp.float32), 0.5, 1.5).astype(jnp.bfloat16)
    w_qkv = draw_w_qkv(jax.random.fold_in(arg_keys[11], 71), 0)
    w_out = gaussian(arg_keys[3], (D, D), (D // 64) ** -0.5, 1.75, ((0, 2), (1, 16)))
    gain_ffn = jnp.clip(1.0 + 0.1 * jax.random.normal(arg_keys[4], (D,), jnp.float32), 0.5, 1.5).astype(jnp.bfloat16)
    w_in = gaussian(arg_keys[5], (D, 2, FF), D ** -0.5, 0.21875, ((0, 16), (2, 2)))
    w_down = gaussian(arg_keys[6], (FF, D), FF ** -0.5, 0.1875, ((0, 2), (1, 16)))
    cotangent = gaussian(arg_keys[7], (TOKENS, D), 1.0, 6.0, ((0, 32),))
    segments = jax.vmap(lambda own: jnp.searchsorted(jnp.cumsum(uneven_parts(own, 3, SEQ, SEQ * 5 // 8, 0)), jnp.arange(SEQ), side="right"))(jax.random.split(arg_keys[8], BLOCKS)).reshape((BLOCKS, SEQ)).astype(jnp.int32)
    lengths = with_ends(jax.random.randint(arg_keys[9], (BLOCKS,), 3 * SEQ // 4, SEQ + 1), jax.random.fold_in(arg_keys[9], 1), 3 * SEQ // 4, SEQ).astype(jnp.int32)
    counts = draw_counts(jax.random.fold_in(arg_keys[11], 71), 0)
    return dict(inputs=inputs, gain_attn=gain_attn, w_qkv=w_qkv, w_out=w_out, gain_ffn=gain_ffn, w_in=w_in, w_down=w_down, cotangent=cotangent, segments=segments, lengths=lengths, counts=counts)


THETA_BASE = 160000.0
EPSILON = 1e-05
SQRT_HALF = 0.7071067811865476
INV_ROOT_TWO_PI = 0.3989422804014327
MASKED_SCORE = -1e+30

def norm_rows(rows_in, gain_vec):
    centre = rows_in - lax.optimization_barrier(jnp.mean(rows_in, axis=-1, keepdims=True))
    inv_std = lax.rsqrt(lax.optimization_barrier(jnp.mean(centre * centre, axis=-1, keepdims=True)) + EPSILON)
    normed = centre * inv_std
    return (normed, inv_std, (normed * gain_vec.astype(jnp.float32)).astype(jnp.bfloat16))

def norm_back(grad_normed, normed, inv_std, gain_vec):
    scaled = grad_normed * gain_vec.astype(jnp.float32)
    inner_mean = lax.optimization_barrier(jnp.mean(scaled * normed, axis=-1, keepdims=True))
    grad_rows = inv_std * (scaled - lax.optimization_barrier(jnp.mean(scaled, axis=-1, keepdims=True)) - normed * inner_mean)
    return (grad_rows, lax.optimization_barrier(jnp.sum(grad_normed * normed, axis=0)))

def gelu_exact(values):
    return 0.5 * values * (1.0 + jax.scipy.special.erf(values * SQRT_HALF))

def gelu_slope(values):
    return 0.5 * (1.0 + jax.scipy.special.erf(values * SQRT_HALF)) + values * INV_ROOT_TWO_PI * jnp.exp(-0.5 * values * values)

def rotary_tables(segments, head_width):
    seq_len = segments.shape[-1]
    earlier = lax.optimization_barrier(jnp.sum((segments[:, None, :] < segments[:, :, None]).astype(jnp.int32), axis=-1))
    position = (jnp.arange(seq_len, dtype=jnp.int32)[None, :] - earlier).astype(jnp.float32)
    half_width = head_width // 2
    frequency = jnp.power(jnp.float32(THETA_BASE), -(jnp.arange(half_width, dtype=jnp.float32) * (2.0 / head_width)))
    angle = position[:, :, None] * frequency[None, None, :]
    return (jnp.cos(angle)[:, :, None, :], jnp.sin(angle)[:, :, None, :])

def rotate(vectors, cosine_table, sine_table, direction_sign):
    half_width = vectors.shape[-1] // 2
    first_half = vectors[..., :half_width]
    second_half = vectors[..., half_width:]
    return jnp.concatenate([first_half * cosine_table - direction_sign * second_half * sine_table, second_half * cosine_table + direction_sign * first_half * sine_table], axis=-1)

def block_masks(segments, lengths, count_live):
    block_count, seq_len = segments.shape
    live_slots = (jnp.arange(block_count, dtype=jnp.int32)[:, None] < count_live) & (jnp.arange(seq_len, dtype=jnp.int32)[None, :] < lengths[:, None])
    same_doc = segments[:, :, None] == segments[:, None, :]
    diagonal = jnp.eye(seq_len, dtype=bool)[None]
    key_mask = same_doc & live_slots[:, None, :] | diagonal
    return (live_slots, key_mask)

def masked_scores(queries, key_rows, key_mask, scale):
    scores = jnp.einsum('bqhd,bkhd->bhqk', queries.astype(jnp.float32), key_rows.astype(jnp.float32)) * scale
    return jnp.where(key_mask[:, None], scores, MASKED_SCORE)

def attend(queries, key_rows, value_rows, key_mask, scale):
    scores = masked_scores(queries, key_rows, key_mask, scale)
    row_max = lax.optimization_barrier(jnp.max(scores, axis=-1, keepdims=True))
    log_total = row_max + jnp.log(lax.optimization_barrier(jnp.sum(jnp.exp(scores - row_max), axis=-1, keepdims=True)))
    attn_prob = jnp.exp(scores - log_total).astype(jnp.bfloat16)
    attended = jnp.einsum('bhqk,bkhd->bqhd', attn_prob.astype(jnp.float32), value_rows.astype(jnp.float32)).astype(jnp.bfloat16)
    return (attended, log_total)

def attend_back(queries, key_rows, value_rows, attended, log_total, key_mask, grad_att, scale):
    scores = masked_scores(queries, key_rows, key_mask, scale)
    attn_prob = jnp.exp(scores - log_total)
    prob_bf = attn_prob.astype(jnp.bfloat16)
    grad_values = jnp.einsum('bhqk,bqhd->bkhd', prob_bf.astype(jnp.float32), grad_att.astype(jnp.float32))
    grad_prob = jnp.einsum('bqhd,bkhd->bhqk', grad_att.astype(jnp.float32), value_rows.astype(jnp.float32))
    row_inner = lax.optimization_barrier(jnp.sum(grad_att.astype(jnp.float32) * attended.astype(jnp.float32), axis=-1))
    row_inner = jnp.transpose(row_inner, (0, 2, 1))[..., None]
    grad_scores = (attn_prob * (grad_prob - row_inner)).astype(jnp.bfloat16)
    grad_queries = jnp.einsum('bhqk,bkhd->bqhd', grad_scores.astype(jnp.float32), key_rows.astype(jnp.float32)) * scale
    grad_keys = jnp.einsum('bhqk,bqhd->bkhd', grad_scores.astype(jnp.float32), queries.astype(jnp.float32)) * scale
    return (grad_queries, grad_keys, grad_values)

def reference(inputs, gain_attn, w_qkv, w_out, gain_ffn, w_in, w_down, cotangent, segments, lengths, counts):
    model_width = inputs.shape[1]
    head_width = HD
    head_count = model_width // head_width
    scale = head_width ** (-0.5)
    group_count = counts.shape[0]
    block_count = segments.shape[0] // group_count
    seq_len = segments.shape[1]
    group_rows = block_count * seq_len
    unit_count = w_down.shape[0]

    def heads_of(matrix):
        return matrix.reshape(block_count, seq_len, head_count, head_width)

    def group_pass(totals, items):
        rows_in, cot_rows, group_segs, group_lens, group_live = items
        live_slots, key_mask = block_masks(group_segs, group_lens, group_live)
        live_rows = live_slots.reshape(group_rows, 1).astype(jnp.float32)
        cosine_table, sine_table = rotary_tables(group_segs, head_width)
        rows_f = rows_in.astype(jnp.float32)
        normed1, inv_std1, normed1_bf = norm_rows(rows_f, gain_attn)
        projected = [jnp.dot(normed1_bf, w_qkv[which_one], preferred_element_type=jnp.float32) for which_one in range(3)]
        queries = rotate(heads_of(projected[0]), cosine_table, sine_table, 1.0).astype(jnp.bfloat16)
        key_rows = rotate(heads_of(projected[1]), cosine_table, sine_table, 1.0).astype(jnp.bfloat16)
        value_rows = heads_of(projected[2]).astype(jnp.bfloat16)
        attended, log_total = attend(queries, key_rows, value_rows, key_mask, scale)
        attended_rows = attended.reshape(group_rows, model_width)
        hidden = rows_f + jnp.dot(attended_rows, w_out, preferred_element_type=jnp.float32)
        normed2, inv_std2, normed2_bf = norm_rows(hidden, gain_ffn)
        unit_in = jnp.dot(normed2_bf, w_in[:, 0, :], preferred_element_type=jnp.float32)
        unit_gate = jnp.dot(normed2_bf, w_in[:, 1, :], preferred_element_type=jnp.float32)
        activated = (gelu_exact(unit_in) * unit_gate).astype(jnp.bfloat16)
        mixed = hidden + jnp.dot(activated, w_down, preferred_element_type=jnp.float32)
        out_rows = (live_rows * mixed).astype(jnp.bfloat16)
        grad_mixed = live_rows * cot_rows.astype(jnp.float32)
        grad_mixed_bf = grad_mixed.astype(jnp.bfloat16)
        grad_act = jnp.dot(grad_mixed_bf, w_down.T, preferred_element_type=jnp.float32)
        grad_down = jnp.dot(activated.T, grad_mixed_bf, preferred_element_type=jnp.float32)
        grad_in_bf = (grad_act * unit_gate * gelu_slope(unit_in)).astype(jnp.bfloat16)
        grad_gate_bf = (grad_act * gelu_exact(unit_in)).astype(jnp.bfloat16)
        grad_w_in = jnp.stack([jnp.dot(normed2_bf.T, grad_in_bf, preferred_element_type=jnp.float32), jnp.dot(normed2_bf.T, grad_gate_bf, preferred_element_type=jnp.float32)], axis=1)
        grad_normed2 = jnp.dot(grad_in_bf, w_in[:, 0, :].T, preferred_element_type=jnp.float32) + jnp.dot(grad_gate_bf, w_in[:, 1, :].T, preferred_element_type=jnp.float32)
        grad_ln2, gain2_term = norm_back(grad_normed2, normed2, inv_std2, gain_ffn)
        grad_hidden = grad_mixed + grad_ln2
        grad_hidden_bf = grad_hidden.astype(jnp.bfloat16)
        grad_att = jnp.dot(grad_hidden_bf, w_out.T, preferred_element_type=jnp.float32).astype(jnp.bfloat16)
        grad_w_out = jnp.dot(attended_rows.T, grad_hidden_bf, preferred_element_type=jnp.float32)
        grad_queries, grad_keys, grad_values = attend_back(queries, key_rows, value_rows, attended, log_total, key_mask, heads_of(grad_att), scale)
        grad_pieces = [rotate(grad_queries, cosine_table, sine_table, -1.0), rotate(grad_keys, cosine_table, sine_table, -1.0), grad_values]
        grad_pieces = [grad_piece.reshape(group_rows, model_width).astype(jnp.bfloat16) for grad_piece in grad_pieces]
        grad_w_qkv = jnp.stack([jnp.dot(normed1_bf.T, grad_piece, preferred_element_type=jnp.float32) for grad_piece in grad_pieces])
        grad_normed1 = jnp.dot(grad_pieces[0], w_qkv[0].T, preferred_element_type=jnp.float32)
        grad_normed1 = grad_normed1 + jnp.dot(grad_pieces[1], w_qkv[1].T, preferred_element_type=jnp.float32)
        grad_normed1 = grad_normed1 + jnp.dot(grad_pieces[2], w_qkv[2].T, preferred_element_type=jnp.float32)
        grad_ln1, gain1_term = norm_back(grad_normed1, normed1, inv_std1, gain_attn)
        grad_rows = grad_hidden + grad_ln1
        terms = (gain1_term, grad_w_qkv, grad_w_out, gain2_term, grad_w_in, grad_down)
        totals = tuple((total + term for total, term in zip(totals, terms)))
        return (totals, (out_rows, grad_rows))
    start_totals = (jnp.zeros((model_width,), jnp.float32), jnp.zeros((3, model_width, model_width), jnp.float32), jnp.zeros((model_width, model_width), jnp.float32), jnp.zeros((model_width,), jnp.float32), jnp.zeros((model_width, 2, unit_count), jnp.float32), jnp.zeros((unit_count, model_width), jnp.float32))
    items = (inputs.reshape(group_count, group_rows, model_width), cotangent.reshape(group_count, group_rows, model_width), segments.reshape(group_count, block_count, seq_len), lengths.reshape(group_count, block_count), counts)
    totals, stacked = lax.scan(group_pass, start_totals, items)
    output = stacked[0].reshape(group_count * group_rows, model_width)
    grad_inputs = stacked[1].reshape(group_count * group_rows, model_width)
    return (output, grad_inputs, totals[0], totals[1], totals[2], totals[3], totals[4], totals[5])
```

```python
import functools

import jax
import jax.numpy as jnp
from jax import lax
from jax.experimental import pallas as pl
from jax.experimental.pallas import tpu as pltpu
from jax.sharding import PartitionSpec as P

HD = 64
LANES = 128

THETA_BASE = 160000.0
EPSILON = 1e-05
SQRT_HALF = 0.7071067811865476
INV_ROOT_TWO_PI = 0.3989422804014327
MASKED_SCORE = -1e30

F32 = jnp.float32
BF16 = jnp.bfloat16


NN = (((1,), (0,)), ((), ()))
NT = (((1,), (1,)), ((), ()))
TN = (((0,), (0,)), ((), ()))

Z_STEPS = (4, 8, 12)
FIRST_A = tuple(b * 2 + z for b in (0, 1) for z in (0, 4, 8, 12))
FIRST_B = tuple(b + z for b in (0, 1) for z in (0, 4, 8, 12))
ORDER = ((FIRST_A, 1), (FIRST_B, 2))


def mm(left, right, dims):
    return lax.dot_general(left, right, dims, preferred_element_type=F32)


def norm_parts(rows_in):
    centre = rows_in - jnp.mean(rows_in, axis=-1, keepdims=True)
    inv_std = lax.rsqrt(jnp.mean(centre * centre, axis=-1, keepdims=True) + EPSILON)
    return centre * inv_std, inv_std


def norm_back(grad_normed, normed, inv_std, gain_row):
    scaled = grad_normed * gain_row
    inner_mean = jnp.mean(scaled * normed, axis=-1, keepdims=True)
    grad_rows = inv_std * (scaled - jnp.mean(scaled, axis=-1, keepdims=True) - normed * inner_mean)
    return grad_rows, jnp.sum(grad_normed * normed, axis=0, keepdims=True)


def lane_index(shape):
    return lax.broadcasted_iota(jnp.int32, shape, 1)


def swap_halves(chunk):
    half = HD // 2
    return jnp.where(
        lane_index(chunk.shape) % HD < half,
        pltpu.roll(chunk, LANES - half, 1),
        pltpu.roll(chunk, half, 1),
    )


def column_to_row(columns, lane):
    pick = (lane_index((8, LANES)) == lane).astype(BF16)
    return mm(pick, columns, NT)[0:1]


def row_to_columns(row):
    return jnp.transpose(jnp.broadcast_to(row, (LANES, row.shape[1])), (1, 0))


class Pieces:
    def __init__(self, me, refs, rows, split):
        self.me, self.refs, self.rows, self.split = me, refs, rows, split

    def copy(self, dst, dst_col, src_col, width):
        if len(self.refs) == 1:
            dst[:, dst_col : dst_col + width] = self.refs[0][:, src_col : src_col + width]
            return
        spans = []
        low, high = src_col, src_col + width
        if low < self.split:
            spans.append((0, low, min(high, self.split), dst_col))
        if high > self.split:
            start = max(low, self.split)
            spans.append((1, start - self.split, high - self.split, dst_col + start - low))
        for colour, begin, end, at in spans:
            order, bit = ORDER[colour]
            for which in (0, 1):
                ref = self.refs[2 * colour + which]
                for i, distance in enumerate(order):
                    base = (self.me ^ (distance ^ (bit * which))) * self.rows
                    base = pl.multiple_of(base, self.rows)
                    dst[pl.ds(base, self.rows), at : at + end - begin] = ref[i, :, begin:end]


def attn_mask(seg_row, seg_col, live_row):
    same = seg_col == seg_row
    shape = same.shape
    diagonal = lax.broadcasted_iota(jnp.int32, shape, 0) == lane_index(shape)
    return (same & (live_row > 0)) | diagonal


def attn_forward_kernel(cfg, n_pieces, *refs):
    me_ref, x_ref = refs[:2]
    own = refs[2 : 2 + n_pieces]
    other = refs[2 + n_pieces : 2 + 2 * n_pieces]
    seg_row, seg_col, live_row, cos_ref, sin_ref = refs[2 + 2 * n_pieces : 7 + 2 * n_pieces]
    w_ref, qkv_ref, att_ref, logt_ref, n1_ref, gain_ref, gcol = refs[7 + 2 * n_pieces :]
    me = me_ref[0]
    half, width = cfg["half"], 2 * cfg["half"]
    for which, pieces in enumerate((own, other)):
        part = Pieces(me, pieces, cfg["rows"], cfg["split"])
        for c in range(3):
            part.copy(w_ref, c * width + which * half, c * half, half)
        if which == 0:
            part.copy(gcol, 0, 3 * half, LANES)
    gain_row = column_to_row(gcol[...], 0)
    gain_ref[...] = jnp.broadcast_to(gain_row, gain_ref.shape)
    normed, _ = norm_parts(x_ref[...].astype(F32))
    n1 = (normed * gain_row).astype(BF16)
    n1_ref[...] = n1
    cosine, sine = cos_ref[...], sin_ref[...]
    step = 2 * LANES
    for at in range(0, 3 * width, step):
        product = mm(n1, w_ref[:, at : at + step], NN)
        for sub in range(0, step, LANES):
            chunk = product[:, sub : sub + LANES]
            if at < 2 * width:
                chunk = chunk * cosine + swap_halves(chunk) * sine
            qkv_ref[:, at + sub : at + sub + LANES] = chunk.astype(BF16)
    mask = attn_mask(seg_row[...], seg_col[...], live_row[...])
    scale = HD ** (-0.5)
    rows = x_ref.shape[0]
    low = lane_index((rows, LANES)) < HD
    lanes = lane_index((rows, LANES))
    totals = jnp.zeros((rows, LANES), F32)
    for pair in range(width // LANES):
        at = pair * LANES
        queries = qkv_ref[:, at : at + LANES]
        keys = qkv_ref[:, width + at : width + at + LANES]
        values = qkv_ref[:, 2 * width + at : 2 * width + at + LANES]
        outs = []
        for side in range(2):
            picked = jnp.where(low if side == 0 else ~low, queries, jnp.zeros_like(queries))
            scores = jnp.where(mask, mm(picked, keys, NT) * scale, MASKED_SCORE)
            row_max = jnp.max(scores, axis=-1, keepdims=True)
            weights = jnp.exp(scores - row_max)
            total = jnp.sum(weights, axis=-1, keepdims=True)
            prob = (weights * (1.0 / total)).astype(BF16)
            outs.append(mm(prob, values, NN))
            totals = jnp.where(lanes == 2 * pair + side, row_max + jnp.log(total), totals)
        att_ref[:, at : at + LANES] = jnp.where(low, outs[0], outs[1]).astype(BF16)
    logt_ref[...] = totals


def ffn_kernel(cfg, n_pieces, *refs):
    me_ref, x_ref, att_ref, cot_ref, live_ref = refs[:5]
    own = refs[5 : 5 + n_pieces]
    other = refs[5 + n_pieces : 5 + 2 * n_pieces]
    rest = refs[5 + 2 * n_pieces :]
    out_ref, gh_ref, wo_ref, swap_ref, keep_ref = rest[:5]
    win_ref, wgate_ref, wdown_ref, gcol = rest[5:]
    me = me_ref[0]
    half, units, main = cfg["half"], cfg["units"], cfg["main"]
    tail = units - main
    model = x_ref.shape[1]
    out_at = 2 * units
    for which, pieces in enumerate((own, other)):
        part = Pieces(me, pieces, cfg["rows"], cfg["split"])
        part.copy(win_ref, which * main, 0, main)
        part.copy(wgate_ref, which * main, main, main)
        part.copy(win_ref, 2 * main + which * tail, 2 * main, tail)
        part.copy(wgate_ref, 2 * main + which * tail, 2 * main + tail, tail)
        part.copy(wo_ref, which * half, out_at, half)
        part.copy(wdown_ref, which * main, out_at + half, main)
        part.copy(wdown_ref, 2 * main + which * tail, out_at + half + main, tail)
        if which == 0:
            part.copy(gcol, 0, out_at + half + main, LANES)
    lanes8 = lane_index((8, LANES))
    pick = (lanes8 == tail).astype(BF16)
    gain_row = mm(pick, gcol[...], NT)[0:1]
    att = att_ref[...]
    hidden = x_ref[...].astype(F32) + mm(att, wo_ref[...], NT)
    normed, inv_std = norm_parts(hidden)
    n2 = (normed * gain_row).astype(BF16)
    live = live_ref[...]
    grad_mixed = live * cot_ref[...].astype(F32)
    grad_mixed_bf = grad_mixed.astype(BF16)
    rows = x_ref.shape[0]
    swap_ref[0:rows, 0:model] = n2
    swap_ref[0:rows, model : 2 * model] = grad_mixed_bf
    base = 3 * model
    step = 3 * LANES
    mixed = hidden
    grad_normed = jnp.zeros((rows, model), F32)
    for at in range(0, 2 * units, step):
        unit_in = mm(n2, win_ref[:, at : at + step], NN)
        unit_gate = mm(n2, wgate_ref[:, at : at + step], NN)
        grad_act = mm(grad_mixed_bf, wdown_ref[:, at : at + step], NN)
        cdf = 0.5 * (1.0 + lax.erf(unit_in * SQRT_HALF))
        gelu = unit_in * cdf
        slope = cdf + unit_in * INV_ROOT_TWO_PI * jnp.exp(-0.5 * unit_in * unit_in)
        activated = (gelu * unit_gate).astype(BF16)
        grad_in = (grad_act * unit_gate * slope).astype(BF16)
        grad_gate = (grad_act * gelu).astype(BF16)
        mixed = mixed + mm(activated, wdown_ref[:, at : at + step], NT)
        grad_normed = (
            grad_normed
            + mm(grad_in, win_ref[:, at : at + step], NT)
            + mm(grad_gate, wgate_ref[:, at : at + step], NT)
        )
        for sub in range(0, step, LANES):
            lo = at + sub
            a, gi, gg = (v[:, sub : sub + LANES] for v in (activated, grad_in, grad_gate))
            if lo < 2 * main:
                which, col = divmod(lo, main)
                ref, off = (keep_ref, 0) if which == 0 else (swap_ref, base)
                ref[0:rows, off + col : off + col + LANES] = gi
                ref[0:rows, off + main + col : off + main + col + LANES] = gg
                col = off + 2 * units + half + col
                ref[0:rows, col : col + LANES] = a
            else:
                low = lane_index((rows, LANES)) < tail
                gi, gg, a = gi.astype(F32), gg.astype(F32), a.astype(F32)
                mine = jnp.where(low, gi, pltpu.roll(gg, tail, 1)).astype(BF16)
                theirs = jnp.where(low, pltpu.roll(gi, tail, 1), gg).astype(BF16)
                at_tail = 2 * main
                keep_ref[0:rows, at_tail : at_tail + LANES] = mine
                swap_ref[0:rows, base + at_tail : base + at_tail + LANES] = theirs
                at_tail = 2 * units + half + main
                keep_ref[0:rows, at_tail : at_tail + LANES] = a.astype(BF16)
                swap_ref[0:rows, base + at_tail : base + at_tail + LANES] = pltpu.roll(
                    a, tail, 1
                ).astype(BF16)
    out_ref[...] = (live * mixed).astype(BF16)
    grad_rows, gain_term = norm_back(grad_normed, normed, inv_std, gain_row)
    grad_hidden = grad_mixed + grad_rows
    gh_ref[...] = grad_hidden
    swap_ref[0:rows, 2 * model : base] = grad_hidden.astype(BF16)
    keep_ref[0:rows, 2 * units : 2 * units + half] = att[:, 0:half]
    swap_ref[0:rows, base + 2 * units : base + 2 * units + half] = att[:, half:]
    put_gain(swap_ref, gain_term, rows)


def put_gain(ref, gain_term, rows):
    model = gain_term.shape[1]
    extra = ref.shape[0] - rows
    high = gain_term.astype(BF16).astype(F32)
    first = lax.broadcasted_iota(jnp.int32, (extra, model), 0)
    block = jnp.where(first == 0, high, jnp.where(first == 1, gain_term - high, 0.0))
    ref[rows:, 0:model] = block.astype(BF16)
    ref[rows:, model:] = jnp.zeros((extra, ref.shape[1] - model), BF16)


def attn_backward_kernel(cfg, *refs):
    (x_ref, gh_ref, wo_ref, w_ref, qkv_ref, att_ref, logt_ref, gain_ref) = refs[:8]
    seg_row, seg_col, live_row, cos_ref, sin_ref, n1_ref = refs[8:14]
    gin_ref, swap_ref, keep_ref, gatt_ref, gqkv_ref = refs[14:]
    half, width = cfg["half"], 2 * cfg["half"]
    rows, model = x_ref.shape
    gatt_ref[...] = mm(gh_ref[...].astype(BF16), wo_ref[...], NN).astype(BF16)
    mask = attn_mask(seg_row[...], seg_col[...], live_row[...])
    scale = HD ** (-0.5)
    low = lane_index((rows, LANES)) < HD
    cosine, sine = cos_ref[...], sin_ref[...]
    for pair in range(width // LANES):
        at = pair * LANES
        queries = qkv_ref[:, at : at + LANES]
        keys = qkv_ref[:, width + at : width + at + LANES]
        values = qkv_ref[:, 2 * width + at : 2 * width + at + LANES]
        grad_att = gatt_ref[:, at : at + LANES]
        products = grad_att.astype(F32) * att_ref[:, at : at + LANES].astype(F32)
        grads_q, grad_k, grad_v = [], 0.0, 0.0
        for side in range(2):
            on = low if side == 0 else ~low
            q_side = jnp.where(on, queries, jnp.zeros_like(queries))
            g_side = jnp.where(on, grad_att, jnp.zeros_like(grad_att))
            head = 2 * pair + side
            scores = jnp.where(mask, mm(q_side, keys, NT) * scale, MASKED_SCORE)
            prob = jnp.exp(scores - logt_ref[:, head : head + 1])
            row_inner = jnp.sum(jnp.where(on, products, 0.0), axis=-1, keepdims=True)
            grad_prob = mm(g_side, values, NT)
            grad_scores = (prob * (grad_prob - row_inner)).astype(BF16)
            grad_v = grad_v + mm(prob.astype(BF16), g_side, TN)
            grads_q.append(mm(grad_scores, keys, NN))
            grad_k = grad_k + mm(grad_scores, q_side, TN)
        grad_q = jnp.where(low, grads_q[0], grads_q[1]) * scale
        grad_k = grad_k * scale
        grad_q = grad_q * cosine - swap_halves(grad_q) * sine
        grad_k = grad_k * cosine - swap_halves(grad_k) * sine
        for c, value in enumerate((grad_q, grad_k, grad_v)):
            value = value.astype(BF16)
            gqkv_ref[:, c * width + at : c * width + at + LANES] = value
            if at < half:
                keep_ref[0:rows, c * half + at : c * half + at + LANES] = value
            else:
                col = model + c * half + at - half
                swap_ref[0:rows, col : col + LANES] = value
    swap_ref[0:rows, 0:model] = n1_ref[...]
    grad_normed = mm(gqkv_ref[...], w_ref[...], NT)
    normed, inv_std = norm_parts(x_ref[...].astype(F32))
    grad_rows, gain_term = norm_back(grad_normed, normed, inv_std, gain_ref[0:1])
    gin_ref[...] = gh_ref[...] + grad_rows
    put_gain(swap_ref, gain_term, rows)


def grads_kernel(cfg, sections, fast, me_ref, mine, keep, theirs, *refs):
    grad_ref = refs[-1]
    outs = refs[:-1]
    tokens = keep.shape[0]
    base = cfg["base"]
    for left, at, size in sections:
        l_mine = mine[0:tokens, left : left + cfg["model"]]
        l_theirs = theirs[0:tokens, left : left + cfg["model"]]
        grad_ref[:, at : at + size] = mm(l_mine, keep[:, at : at + size], TN) + mm(
            l_theirs, theirs[0:tokens, base + at : base + at + size], TN
        )
    gain = jnp.zeros((1, cfg["model"]), F32)
    for ref in (mine, theirs):
        block = ref[tokens:, 0 : cfg["model"]].astype(F32)
        gain = gain + block[0:1] + block[1:2]
    columns = row_to_columns(gain)
    total = grad_ref.shape[1]
    last = slice(total - LANES, total)
    if cfg["gain_lane"]:
        keep_low = lane_index(columns.shape) < cfg["gain_lane"]
        columns = jnp.where(keep_low, grad_ref[:, last], columns)
    grad_ref[:, last] = columns
    if not fast:
        outs[0][...] = grad_ref[...]
        return
    me, rows, split = me_ref[0], cfg["rows"], cfg["split"]
    for colour, (order, bit) in enumerate(ORDER):
        cols = slice(0, split) if colour == 0 else slice(split, total)
        for which in (0, 1):
            for i, distance in enumerate(order):
                start = pl.multiple_of((me ^ (distance ^ (bit * which))) * rows, rows)
                outs[2 * colour + which][i] = grad_ref[pl.ds(start, rows), cols].astype(BF16)


VMEM = pl.BlockSpec(memory_space=pltpu.VMEM)
SMEM = pl.BlockSpec(memory_space=pltpu.SMEM)


def call(kernel, operands, outs, scratch, scalars=1, flops=0):
    moved = sum(o.size * o.dtype.itemsize for o in operands)
    moved += sum(s.size * s.dtype.itemsize for s in outs)
    return pl.pallas_call(
        kernel,
        out_shape=outs,
        in_specs=[SMEM] * scalars + [VMEM] * (len(operands) - scalars),
        out_specs=[VMEM] * len(outs),
        scratch_shapes=scratch,
        cost_estimate=pl.CostEstimate(flops=flops, bytes_accessed=moved, transcendentals=0),
        compiler_params=pltpu.CompilerParams(vmem_limit_bytes=60 * 1024 * 1024),
    )(*operands)


def shards(
    inputs, gain_attn, w_qkv, w_out, gain_ffn, w_in, w_down, cotangent, segments, lengths, counts
):
    dp, cores = lax.axis_size("dp"), lax.axis_size("tensor")
    me, core = lax.axis_index("dp"), lax.axis_index("tensor")
    seq = segments.shape[1]
    tokens, model = inputs.shape
    rows, half, units = gain_attn.shape[0], w_qkv.shape[2], w_in.shape[2]
    main = units // LANES * LANES
    tail = units - main
    if cores != 2 or tokens != seq or segments.shape[0] != cores or 2 * tail != LANES:
        raise ValueError("unsupported shapes")
    fast = dp == 16 and rows % 16 == 0

    def swap_cores(value):
        return lax.ppermute(value, "tensor", [(0, 1), (1, 0)])

    def exchange(value, distance):
        return lax.ppermute(value, "dp", [(i, i ^ distance) for i in range(dp)])

    def gather(packed, split):
        if not fast:
            full = lax.all_gather(packed, "dp", axis=0, tiled=True)
            return [full], [swap_cores(full)]
        planes = [packed] + [exchange(packed, z) for z in Z_STEPS]
        a4 = jnp.stack([p[:, :split] for p in planes])
        b4 = jnp.stack([p[:, split:] for p in planes])
        a8 = jnp.concatenate([a4, exchange(a4, 2)])
        b8 = jnp.concatenate([b4, exchange(b4, 1)])
        own = [a8, exchange(a8, 1), b8, exchange(b8, 2)]
        return own, [swap_cores(piece) for piece in own]

    def scatter(pieces, split):
        if not fast:
            return lax.psum_scatter(pieces[0], "dp", scatter_dimension=0, tiled=True)
        keep_a, send_a, keep_b, send_b = pieces

        def add(left, right):
            return left.astype(F32) + right.astype(F32)

        sum_a = add(keep_a, exchange(send_a, 1))
        sum_b = add(keep_b, exchange(send_b, 2))
        sum_a = add(sum_a[:4], exchange(sum_a[4:].astype(BF16), 2))
        sum_b = add(sum_b[:4], exchange(sum_b[4:].astype(BF16), 1))
        blocks = [jnp.concatenate([sum_a[z], sum_b[z]], axis=1) for z in range(4)]
        total = blocks[0]
        for block, z in zip(blocks[1:], Z_STEPS):
            total = total + exchange(block.astype(BF16), z).astype(F32)
        return total

    pack_qkv = jnp.concatenate(
        [w_qkv[0], w_qkv[1], w_qkv[2], jnp.pad(gain_attn[:, None], ((0, 0), (0, LANES - 1)))],
        axis=1,
    )
    out_t, down_t = w_out.T, w_down.T
    pack_ffn = jnp.concatenate(
        [
            w_in[:, 0, :main],
            w_in[:, 1, :main],
            w_in[:, 0, main:],
            w_in[:, 1, main:],
            out_t,
            down_t,
            jnp.pad(gain_ffn[:, None], ((0, 0), (0, tail - 1))),
        ],
        axis=1,
    )
    split_qkv = pack_qkv.shape[1] // 2
    split_ffn = 2 * units
    own_qkv, other_qkv = gather(pack_qkv, split_qkv)
    own_ffn, other_ffn = gather(pack_ffn, split_ffn)

    seg = lax.dynamic_slice_in_dim(segments, core, 1, axis=0)
    length = lax.dynamic_slice_in_dim(lengths, core, 1, axis=0)
    live = ((jnp.arange(seq, dtype=jnp.int32) < length) & (core < counts[0])).astype(F32)
    seg_row, seg_col = seg, seg.reshape(seq, 1)
    live_row, live_col = live.reshape(1, seq), live.reshape(seq, 1)
    earlier = jnp.sum((seg_row < seg_col).astype(jnp.int32), axis=1)
    position = (jnp.arange(seq, dtype=jnp.int32) - earlier).astype(F32)
    frequency = jnp.power(F32(THETA_BASE), -(jnp.arange(HD // 2, dtype=F32) * (2.0 / HD)))
    angle = position[:, None] * frequency[None, :]
    cosine, sine = jnp.cos(angle), jnp.sin(angle)
    repeats = LANES // HD
    cosine = jnp.concatenate([cosine, cosine] * repeats, axis=1)
    sine = jnp.concatenate([-sine, sine] * repeats, axis=1)
    me_vec = me.astype(jnp.int32).reshape(1)

    def shape(*dims, dtype=BF16):
        return jax.ShapeDtypeStruct(dims, dtype)

    n_pieces = len(own_qkv)
    cfg = dict(half=half, rows=rows, split=split_qkv, units=units, main=main, model=model)
    width = 2 * half
    w_full, qkv, att, logt, n1, gain1 = call(
        functools.partial(attn_forward_kernel, cfg, n_pieces),
        [me_vec, inputs, *own_qkv, *other_qkv, seg_row, seg_col, live_row, cosine, sine],
        [
            shape(model, 3 * width),
            shape(tokens, 3 * width),
            shape(tokens, width),
            shape(tokens, LANES, dtype=F32),
            shape(tokens, model),
            shape(8, model, dtype=F32),
        ],
        [pltpu.VMEM((model, LANES), BF16)],
        flops=2 * tokens * model * 3 * width,
    )
    ffn_cfg = dict(cfg, split=split_ffn)
    side = 2 * units + half + main + LANES
    output, grad_hidden, wo_full, swap1, keep1 = call(
        functools.partial(ffn_kernel, ffn_cfg, n_pieces),
        [me_vec, inputs, att, cotangent, live_col, *own_ffn, *other_ffn],
        [
            shape(tokens, model),
            shape(tokens, model, dtype=F32),
            shape(model, width),
            shape(tokens + 16, 3 * model + side),
            shape(tokens, side),
        ],
        [pltpu.VMEM((model, 2 * units), BF16)] * 3 + [pltpu.VMEM((model, LANES), BF16)],
        flops=2 * tokens * model * 12 * units,
    )

    def grads(sections, swap_mine, keep, cfg):
        total = cfg["total"]
        if fast:
            outs = [shape(8, rows, cfg["split"])] * 2 + [shape(8, rows, total - cfg["split"])] * 2
        else:
            outs = [shape(model, total, dtype=F32)]
        return call(
            functools.partial(grads_kernel, cfg, sections, fast),
            [me_vec, swap_mine, keep, swap_cores(swap_mine)],
            outs,
            [pltpu.VMEM((model, total), F32)],
            flops=4 * tokens * model * total,
        )

    sections1 = [
        (0, 0, 2 * units),
        (2 * model, 2 * units, half),
        (model, 2 * units + half, main + LANES),
    ]
    pieces1 = grads(
        sections1, swap1, keep1, dict(ffn_cfg, base=3 * model, total=side, gain_lane=tail)
    )
    share1 = scatter(pieces1, split_ffn)
    grad_inputs, swap2, keep2 = call(
        functools.partial(attn_backward_kernel, cfg),
        [
            inputs, grad_hidden, wo_full, w_full, qkv, att, logt, gain1,
            seg_row, seg_col, live_row, cosine, sine, n1,
        ],
        [
            shape(tokens, model, dtype=F32),
            shape(tokens + 16, model + 3 * half),
            shape(tokens, 3 * half),
        ],
        [pltpu.VMEM((tokens, width), BF16), pltpu.VMEM((tokens, 3 * width), BF16)],
        scalars=0,
        flops=2 * tokens * model * 5 * width,
    )
    sections2 = [(0, 0, 3 * half)]
    pieces2 = grads(
        sections2, swap2, keep2, dict(cfg, base=model, total=3 * half + LANES, gain_lane=0)
    )
    share2 = scatter(pieces2, split_qkv)

    grad_qkv = jnp.stack([share2[:, c * half : (c + 1) * half] for c in range(3)])
    grad_gain1 = share2[:, 3 * half]
    heads = share1[:, : 2 * main].reshape(rows, 2, main)
    tails = share1[:, 2 * main : 2 * units].reshape(rows, 2, tail)
    grad_in = jnp.concatenate([heads, tails], axis=2)
    grad_out = share1[:, 2 * units : 2 * units + half].T
    grad_down = share1[:, 2 * units + half : 2 * units + half + units].T
    grad_gain2 = share1[:, 2 * units + half + units]
    return (
        output,
        grad_inputs,
        grad_gain1,
        grad_qkv,
        grad_out,
        grad_gain2,
        grad_in,
        grad_down,
    )


def solution(mesh):
    in_specs = (
        P(("dp", "tensor"), None),
        P("dp"),
        P(None, "dp", "tensor"),
        P("tensor", "dp"),
        P("dp"),
        P("dp", None, "tensor"),
        P("tensor", "dp"),
        P(("dp", "tensor"), None),
        P("dp", None),
        P("dp"),
        P("dp"),
    )
    out_specs = (
        P(("dp", "tensor"), None),
        P(("dp", "tensor"), None),
        P("dp"),
        P(None, "dp", "tensor"),
        P("tensor", "dp"),
        P("dp"),
        P("dp", None, "tensor"),
        P("tensor", "dp"),
    )
    return jax.shard_map(shards, mesh=mesh, in_specs=in_specs, out_specs=out_specs, check_vma=False)
```

```python
import functools

import jax
import jax.numpy as jnp
from jax import lax
from jax.experimental import pallas as pl
from jax.experimental.pallas import tpu as pltpu
from jax.sharding import PartitionSpec as P


HD = 64
LANES = 128

THETA_BASE = 160000.0
EPSILON = 1e-05
SQRT_HALF = 0.7071067811865476
INV_ROOT_TWO_PI = 0.3989422804014327
MASKED_SCORE = -1e30

F32 = jnp.float32
BF16 = jnp.bfloat16


NN = (((1,), (0,)), ((), ()))
NT = (((1,), (1,)), ((), ()))
TN = (((0,), (0,)), ((), ()))

X, Y, Z, ZZ = 1, 2, 4, 8
Z_ALL = (0, Z, ZZ, Z | ZZ)
Z_HALVES = (0, ZZ, Z, Z | ZZ)
XY_ALL = (0, X, Y, X | Y)
XY_HALVES = (0, Y, X, X | Y)


def shift(distances, by):
    return tuple(d ^ by for d in distances)


PLANE_PIECES = (Z_ALL, shift(Z_ALL, X), shift(Z_ALL, Y), (3, 7), (11, 15))
LINE_PIECES = tuple(shift(XY_ALL, z) for z in Z_ALL)

GRAD_A = (tuple(y + z for y in (0, Y) for z in Z_HALVES), X)
GRAD_B = (tuple(x + z for x in (0, X) for z in Z_HALVES), Y)
GRAD_C = (tuple(z + xy for z in (0, ZZ) for xy in XY_HALVES), Z)


def mm(left, right, dims):
    return lax.dot_general(left, right, dims, preferred_element_type=F32)


def norm_parts(rows_in):
    centre = rows_in - jnp.mean(rows_in, axis=-1, keepdims=True)
    inv_std = lax.rsqrt(jnp.mean(centre * centre, axis=-1, keepdims=True) + EPSILON)
    return centre * inv_std, inv_std


def norm_back(grad_normed, normed, inv_std, gain_row):
    scaled = grad_normed * gain_row
    inner_mean = jnp.mean(scaled * normed, axis=-1, keepdims=True)
    grad_rows = inv_std * (scaled - jnp.mean(scaled, axis=-1, keepdims=True) - normed * inner_mean)
    return grad_rows, jnp.sum(grad_normed * normed, axis=0, keepdims=True)


def lane_index(shape):
    return lax.broadcasted_iota(jnp.int32, shape, 1)


def swap_halves(chunk):
    half = HD // 2
    return jnp.where(
        lane_index(chunk.shape) % HD < half,
        pltpu.roll(chunk, LANES - half, 1),
        pltpu.roll(chunk, half, 1),
    )


def column_to_row(columns, lane):
    pick = (lane_index((8, LANES)) == lane).astype(BF16)
    return mm(pick, columns, NT)[0:1]


def row_to_columns(row):
    return jnp.transpose(jnp.broadcast_to(row, (LANES, row.shape[1])), (1, 0))


class Pieces:
    def __init__(self, me, refs, rows, layout):
        self.me, self.refs, self.rows, self.layout = me, refs, rows, layout

    def copy(self, dst, dst_col, src_col, width):
        for ref, (distances, first, last) in zip(self.refs, self.layout):
            low, high = max(first, src_col), min(last, src_col + width)
            if low >= high:
                continue
            at = slice(dst_col + low - src_col, dst_col + high - src_col)
            cols = slice(low - first, high - first)
            if distances is None:
                dst[:, at] = ref[:, cols]
                continue
            for i, distance in enumerate(distances):
                base = pl.multiple_of((self.me ^ distance) * self.rows, self.rows)
                dst[pl.ds(base, self.rows), at] = ref[i, :, cols]


def attn_mask(seg_row, seg_col, live_row):
    same = seg_col == seg_row
    shape = same.shape
    diagonal = lax.broadcasted_iota(jnp.int32, shape, 0) == lane_index(shape)
    return (same & (live_row > 0)) | diagonal


def attn_forward_kernel(cfg, n_pieces, *refs):
    me_ref, x_ref = refs[:2]
    own = refs[2 : 2 + n_pieces]
    other = refs[2 + n_pieces : 2 + 2 * n_pieces]
    seg_row, seg_col, live_row, cos_ref, sin_ref = refs[2 + 2 * n_pieces : 7 + 2 * n_pieces]
    w_ref, qkv_ref, att_ref, logt_ref, n1_ref, gain_ref, gcol = refs[7 + 2 * n_pieces :]
    me = me_ref[0]
    half, width = cfg["half"], 2 * cfg["half"]
    for which, pieces in enumerate((own, other)):
        part = Pieces(me, pieces, cfg["rows"], cfg["layout"])
        for c in range(3):
            part.copy(w_ref, c * width + which * half, c * half, half)
        if which == 0:
            part.copy(gcol, 0, 3 * half, LANES)
    gain_row = column_to_row(gcol[...], 0)
    gain_ref[...] = jnp.broadcast_to(gain_row, gain_ref.shape)
    normed, _ = norm_parts(x_ref[...].astype(F32))
    n1 = (normed * gain_row).astype(BF16)
    n1_ref[...] = n1
    cosine, sine = cos_ref[...], sin_ref[...]
    step = 2 * LANES
    for at in range(0, 3 * width, step):
        product = mm(n1, w_ref[:, at : at + step], NN)
        for sub in range(0, step, LANES):
            chunk = product[:, sub : sub + LANES]
            if at < 2 * width:
                chunk = chunk * cosine + swap_halves(chunk) * sine
            qkv_ref[:, at + sub : at + sub + LANES] = chunk.astype(BF16)
    mask = attn_mask(seg_row[...], seg_col[...], live_row[...])
    scale = HD ** (-0.5)
    rows = x_ref.shape[0]
    low = lane_index((rows, LANES)) < HD
    lanes = lane_index((rows, LANES))
    totals = jnp.zeros((rows, LANES), F32)
    for pair in range(width // LANES):
        at = pair * LANES
        queries = qkv_ref[:, at : at + LANES]
        keys = qkv_ref[:, width + at : width + at + LANES]
        values = qkv_ref[:, 2 * width + at : 2 * width + at + LANES]
        outs = []
        for side in range(2):
            picked = jnp.where(low if side == 0 else ~low, queries, jnp.zeros_like(queries))
            scores = jnp.where(mask, mm(picked, keys, NT) * scale, MASKED_SCORE)
            row_max = jnp.max(scores, axis=-1, keepdims=True)
            weights = jnp.exp(scores - row_max)
            total = jnp.sum(weights, axis=-1, keepdims=True)
            prob = (weights * (1.0 / total)).astype(BF16)
            outs.append(mm(prob, values, NN))
            totals = jnp.where(lanes == 2 * pair + side, row_max + jnp.log(total), totals)
        att_ref[:, at : at + LANES] = jnp.where(low, outs[0], outs[1]).astype(BF16)
    logt_ref[...] = totals


def ffn_kernel(cfg, n_pieces, *refs):
    me_ref, x_ref, att_ref, cot_ref, live_ref = refs[:5]
    own = refs[5 : 5 + n_pieces]
    other = refs[5 + n_pieces : 5 + 2 * n_pieces]
    rest = refs[5 + 2 * n_pieces :]
    out_ref, gh_ref, wo_ref, swap_ref, keep_ref = rest[:5]
    win_ref, wgate_ref, wdown_ref, gcol = rest[5:]
    me = me_ref[0]
    half, units, main = cfg["half"], cfg["units"], cfg["main"]
    tail = units - main
    model = x_ref.shape[1]
    out_at = 2 * units
    for which, pieces in enumerate((own, other)):
        part = Pieces(me, pieces, cfg["rows"], cfg["layout"])
        part.copy(win_ref, which * main, 0, main)
        part.copy(wgate_ref, which * main, main, main)
        part.copy(win_ref, 2 * main + which * tail, 2 * main, tail)
        part.copy(wgate_ref, 2 * main + which * tail, 2 * main + tail, tail)
        part.copy(wo_ref, which * half, out_at, half)
        part.copy(wdown_ref, which * main, out_at + half, main)
        part.copy(wdown_ref, 2 * main + which * tail, out_at + half + main, tail)
        if which == 0:
            part.copy(gcol, 0, out_at + half + main, LANES)
    lanes8 = lane_index((8, LANES))
    pick = (lanes8 == tail).astype(BF16)
    gain_row = mm(pick, gcol[...], NT)[0:1]
    att = att_ref[...]
    hidden = x_ref[...].astype(F32) + mm(att, wo_ref[...], NT)
    normed, inv_std = norm_parts(hidden)
    n2 = (normed * gain_row).astype(BF16)
    live = live_ref[...]
    grad_mixed = live * cot_ref[...].astype(F32)
    grad_mixed_bf = grad_mixed.astype(BF16)
    rows = x_ref.shape[0]
    swap_ref[0:rows, 0:model] = n2
    swap_ref[0:rows, model : 2 * model] = grad_mixed_bf
    base = 3 * model
    step = 3 * LANES
    mixed = hidden
    grad_normed = jnp.zeros((rows, model), F32)
    for at in range(0, 2 * units, step):
        unit_in = mm(n2, win_ref[:, at : at + step], NN)
        unit_gate = mm(n2, wgate_ref[:, at : at + step], NN)
        grad_act = mm(grad_mixed_bf, wdown_ref[:, at : at + step], NN)
        cdf = 0.5 * (1.0 + lax.erf(unit_in * SQRT_HALF))
        gelu = unit_in * cdf
        slope = cdf + unit_in * INV_ROOT_TWO_PI * jnp.exp(-0.5 * unit_in * unit_in)
        activated = (gelu * unit_gate).astype(BF16)
        grad_in = (grad_act * unit_gate * slope).astype(BF16)
        grad_gate = (grad_act * gelu).astype(BF16)
        mixed = mixed + mm(activated, wdown_ref[:, at : at + step], NT)
        grad_normed = (
            grad_normed
            + mm(grad_in, win_ref[:, at : at + step], NT)
            + mm(grad_gate, wgate_ref[:, at : at + step], NT)
        )
        for sub in range(0, step, LANES):
            lo = at + sub
            a, gi, gg = (v[:, sub : sub + LANES] for v in (activated, grad_in, grad_gate))
            if lo < 2 * main:
                which, col = divmod(lo, main)
                ref, off = (keep_ref, 0) if which == 0 else (swap_ref, base)
                ref[0:rows, off + col : off + col + LANES] = gi
                ref[0:rows, off + main + col : off + main + col + LANES] = gg
                col = off + 2 * units + half + col
                ref[0:rows, col : col + LANES] = a
            else:
                low = lane_index((rows, LANES)) < tail
                gi, gg, a = gi.astype(F32), gg.astype(F32), a.astype(F32)
                mine = jnp.where(low, gi, pltpu.roll(gg, tail, 1)).astype(BF16)
                theirs = jnp.where(low, pltpu.roll(gi, tail, 1), gg).astype(BF16)
                at_tail = 2 * main
                keep_ref[0:rows, at_tail : at_tail + LANES] = mine
                swap_ref[0:rows, base + at_tail : base + at_tail + LANES] = theirs
                at_tail = 2 * units + half + main
                keep_ref[0:rows, at_tail : at_tail + LANES] = a.astype(BF16)
                swap_ref[0:rows, base + at_tail : base + at_tail + LANES] = pltpu.roll(
                    a, tail, 1
                ).astype(BF16)
    out_ref[...] = (live * mixed).astype(BF16)
    grad_rows, gain_term = norm_back(grad_normed, normed, inv_std, gain_row)
    grad_hidden = grad_mixed + grad_rows
    gh_ref[...] = grad_hidden
    swap_ref[0:rows, 2 * model : base] = grad_hidden.astype(BF16)
    keep_ref[0:rows, 2 * units : 2 * units + half] = att[:, 0:half]
    swap_ref[0:rows, base + 2 * units : base + 2 * units + half] = att[:, half:]
    put_gain(swap_ref, gain_term, rows)


def put_gain(ref, gain_term, rows):
    model = gain_term.shape[1]
    extra = ref.shape[0] - rows
    high = gain_term.astype(BF16).astype(F32)
    first = lax.broadcasted_iota(jnp.int32, (extra, model), 0)
    block = jnp.where(first == 0, high, jnp.where(first == 1, gain_term - high, 0.0))
    ref[rows:, 0:model] = block.astype(BF16)
    ref[rows:, model:] = jnp.zeros((extra, ref.shape[1] - model), BF16)


def attn_backward_kernel(cfg, *refs):
    (x_ref, gh_ref, wo_ref, w_ref, qkv_ref, att_ref, logt_ref, gain_ref) = refs[:8]
    seg_row, seg_col, live_row, cos_ref, sin_ref, n1_ref = refs[8:14]
    gin_ref, swap_ref, keep_ref, gatt_ref, gqkv_ref = refs[14:]
    half, width = cfg["half"], 2 * cfg["half"]
    rows, model = x_ref.shape
    gatt_ref[...] = mm(gh_ref[...].astype(BF16), wo_ref[...], NN).astype(BF16)
    mask = attn_mask(seg_row[...], seg_col[...], live_row[...])
    scale = HD ** (-0.5)
    low = lane_index((rows, LANES)) < HD
    cosine, sine = cos_ref[...], sin_ref[...]
    for pair in range(width // LANES):
        at = pair * LANES
        queries = qkv_ref[:, at : at + LANES]
        keys = qkv_ref[:, width + at : width + at + LANES]
        values = qkv_ref[:, 2 * width + at : 2 * width + at + LANES]
        grad_att = gatt_ref[:, at : at + LANES]
        products = grad_att.astype(F32) * att_ref[:, at : at + LANES].astype(F32)
        grads_q, grad_k, grad_v = [], 0.0, 0.0
        for side in range(2):
            on = low if side == 0 else ~low
            q_side = jnp.where(on, queries, jnp.zeros_like(queries))
            g_side = jnp.where(on, grad_att, jnp.zeros_like(grad_att))
            head = 2 * pair + side
            scores = jnp.where(mask, mm(q_side, keys, NT) * scale, MASKED_SCORE)
            prob = jnp.exp(scores - logt_ref[:, head : head + 1])
            row_inner = jnp.sum(jnp.where(on, products, 0.0), axis=-1, keepdims=True)
            grad_prob = mm(g_side, values, NT)
            grad_scores = (prob * (grad_prob - row_inner)).astype(BF16)
            grad_v = grad_v + mm(prob.astype(BF16), g_side, TN)
            grads_q.append(mm(grad_scores, keys, NN))
            grad_k = grad_k + mm(grad_scores, q_side, TN)
        grad_q = jnp.where(low, grads_q[0], grads_q[1]) * scale
        grad_k = grad_k * scale
        grad_q = grad_q * cosine - swap_halves(grad_q) * sine
        grad_k = grad_k * cosine - swap_halves(grad_k) * sine
        for c, value in enumerate((grad_q, grad_k, grad_v)):
            value = value.astype(BF16)
            gqkv_ref[:, c * width + at : c * width + at + LANES] = value
            if at < half:
                keep_ref[0:rows, c * half + at : c * half + at + LANES] = value
            else:
                col = model + c * half + at - half
                swap_ref[0:rows, col : col + LANES] = value
    swap_ref[0:rows, 0:model] = n1_ref[...]
    grad_normed = mm(gqkv_ref[...], w_ref[...], NT)
    normed, inv_std = norm_parts(x_ref[...].astype(F32))
    grad_rows, gain_term = norm_back(grad_normed, normed, inv_std, gain_ref[0:1])
    gin_ref[...] = gh_ref[...] + grad_rows
    put_gain(swap_ref, gain_term, rows)


def grads_kernel(cfg, sections, fast, me_ref, mine, keep, theirs, *refs):
    grad_ref = refs[-1]
    outs = refs[:-1]
    tokens = keep.shape[0]
    base = cfg["base"]
    for left, at, size in sections:
        l_mine = mine[0:tokens, left : left + cfg["model"]]
        l_theirs = theirs[0:tokens, left : left + cfg["model"]]
        grad_ref[:, at : at + size] = mm(l_mine, keep[:, at : at + size], TN) + mm(
            l_theirs, theirs[0:tokens, base + at : base + at + size], TN
        )
    gain = jnp.zeros((1, cfg["model"]), F32)
    for ref in (mine, theirs):
        block = ref[tokens:, 0 : cfg["model"]].astype(F32)
        gain = gain + block[0:1] + block[1:2]
    columns = row_to_columns(gain)
    total = grad_ref.shape[1]
    last = slice(total - LANES, total)
    if cfg["gain_lane"]:
        keep_low = lane_index(columns.shape) < cfg["gain_lane"]
        columns = jnp.where(keep_low, grad_ref[:, last], columns)
    grad_ref[:, last] = columns
    if not fast:
        outs[0][...] = grad_ref[...]
        return
    me, rows = me_ref[0], cfg["rows"]
    at = 0
    for (order, bit), (first, last) in cfg["emit"]:
        for which in (0, 1):
            for i, distance in enumerate(order):
                start = pl.multiple_of((me ^ distance ^ (bit * which)) * rows, rows)
                outs[at + which][i] = grad_ref[pl.ds(start, rows), first:last].astype(BF16)
        at += 2


def stack_kernel(*refs):
    for i, ref in enumerate(refs[:-1]):
        refs[-1][i] = ref[...]


def combine_kernel(joined, *refs):
    n = (len(refs) - 2) // 2 if joined else len(refs) // 4
    ins, outs = refs[: 2 * n], refs[2 * n :]
    at = 0
    for i in range(n):
        kept, came = ins[2 * i], ins[2 * i + 1]
        blocks, _, cols = kept.shape
        keep, send = (outs[0], outs[1]) if joined else (outs[2 * i], outs[2 * i + 1])
        for j in range(blocks):
            total = kept[j].astype(F32) + came[j].astype(F32)
            ref, k = (keep, j) if j < blocks // 2 else (send, j - blocks // 2)
            ref[k, :, at : at + cols] = total.astype(ref.dtype)
        at += cols if joined else 0


def final_ffn_kernel(kept_c, came_c, kept_ab, came_ab, share):
    cut = kept_c.shape[2]
    share[:, :cut] = kept_c[0] + came_c[0].astype(F32)
    share[:, cut:] = kept_ab[0] + came_ab[0].astype(F32)


def final_qkv_kernel(kept, came, grad, gain):
    half = grad.shape[2]
    for c in range(3):
        cols = slice(c * half, (c + 1) * half)
        grad[c] = kept[0, :, cols] + came[0, :, cols].astype(F32)
    gain[...] = kept[0, :, 3 * half :] + came[0, :, 3 * half :].astype(F32)


VMEM = pl.BlockSpec(memory_space=pltpu.VMEM)
SMEM = pl.BlockSpec(memory_space=pltpu.SMEM)


def call(kernel, operands, outs, scratch, scalars=1, flops=0):
    moved = sum(o.size * o.dtype.itemsize for o in operands)
    moved += sum(s.size * s.dtype.itemsize for s in outs)
    return pl.pallas_call(
        kernel,
        out_shape=outs,
        in_specs=[SMEM] * scalars + [VMEM] * (len(operands) - scalars),
        out_specs=[VMEM] * len(outs),
        scratch_shapes=scratch,
        cost_estimate=pl.CostEstimate(flops=flops, bytes_accessed=moved, transcendentals=0),
        compiler_params=pltpu.CompilerParams(vmem_limit_bytes=60 * 1024 * 1024),
    )(*operands)


def shape(*dims, dtype=BF16):
    return jax.ShapeDtypeStruct(dims, dtype)


def stack(planes):
    outs = [shape(len(planes), *planes[0].shape)]
    return call(stack_kernel, list(planes), outs, [], scalars=0)[0]


def combine(joined, *arrays):
    outs = []
    for kept in arrays[::2]:
        blocks, rows, cols = kept.shape
        outs += [shape(blocks // 2, rows, cols, dtype=F32), shape(blocks // 2, rows, cols)]
    if joined:
        blocks, rows = outs[0].shape[:2]
        cols = sum(o.shape[2] for o in outs[::2])
        outs = [shape(blocks, rows, cols, dtype=F32), shape(blocks, rows, cols)]
    kernel = functools.partial(combine_kernel, joined)
    return call(kernel, list(arrays), outs, [], scalars=0)


def shards(
    inputs, gain_attn, w_qkv, w_out, gain_ffn, w_in, w_down, cotangent, segments, lengths, counts
):
    dp, cores = lax.axis_size("dp"), lax.axis_size("tensor")
    me, core = lax.axis_index("dp"), lax.axis_index("tensor")
    seq = segments.shape[1]
    tokens, model = inputs.shape
    rows, half, units = gain_attn.shape[0], w_qkv.shape[2], w_in.shape[2]
    main = units // LANES * LANES
    tail = units - main
    if cores != 2 or tokens != seq or segments.shape[0] != cores or 2 * tail != LANES:
        raise ValueError("unsupported shapes")
    fast = fast_path(dp) and rows % 16 == 0

    def swap_cores(value):
        return lax.ppermute(value, "tensor", [(0, 1), (1, 0)])

    def exchange(value, distance):
        pairs = [(i, i ^ distance) for i in range(dp)]
        return lax.ppermute(value, "dp", pairs)

    def across_z(value):
        return [value] + [exchange(value, z) for z in Z_ALL[1:]]

    def plane(stacked):
        came_x = exchange(stacked, X)
        came_y = exchange(stacked, Y)
        far_a = exchange(came_y[:2], X)
        far_b = exchange(came_x[2:], Y)
        return [stacked, came_x, came_y, far_a, far_b]

    def both_cores(pieces):
        return [swap_cores(piece) for piece in pieces]

    pack_qkv = jnp.concatenate(
        [w_qkv[0], w_qkv[1], w_qkv[2], jnp.pad(gain_attn[:, None], ((0, 0), (0, LANES - 1)))],
        axis=1,
    )
    out_t, down_t = w_out.T, w_down.T
    pack_ffn = jnp.concatenate(
        [
            w_in[:, 0, :main],
            w_in[:, 1, :main],
            w_in[:, 0, main:],
            w_in[:, 1, main:],
            out_t,
            down_t,
            jnp.pad(gain_ffn[:, None], ((0, 0), (0, tail - 1))),
        ],
        axis=1,
    )
    total_qkv, total_ffn = pack_qkv.shape[1], pack_ffn.shape[1]
    cut = total_ffn * 3 // 10 // LANES * LANES
    if fast:
        own_qkv = plane(stack(across_z(pack_qkv)))
        other_qkv = both_cores(own_qkv)
        pack_c, pack_f = pack_ffn[:, :cut], pack_ffn[:, cut:]
        came_x, came_y = exchange(pack_c, X), exchange(pack_c, Y)
        stack_c = stack([pack_c, came_x, came_y, exchange(came_y, X)])
        own_c = across_z(stack_c)
        own_f = plane(stack(across_z(pack_f)))
        own_ffn = own_c + own_f
        other_ffn = both_cores(own_c) + both_cores(own_f)
        layout_qkv = [(d, 0, total_qkv) for d in PLANE_PIECES]
        layout_ffn = [(d, 0, cut) for d in LINE_PIECES]
        layout_ffn += [(d, cut, total_ffn) for d in PLANE_PIECES]
    else:
        own_qkv = [lax.all_gather(pack_qkv, "dp", axis=0, tiled=True)]
        own_ffn = [lax.all_gather(pack_ffn, "dp", axis=0, tiled=True)]
        other_qkv, other_ffn = both_cores(own_qkv), both_cores(own_ffn)
        layout_qkv, layout_ffn = [(None, 0, total_qkv)], [(None, 0, total_ffn)]

    seg = lax.dynamic_slice_in_dim(segments, core, 1, axis=0)
    length = lax.dynamic_slice_in_dim(lengths, core, 1, axis=0)
    live = ((jnp.arange(seq, dtype=jnp.int32) < length) & (core < counts[0])).astype(F32)
    seg_row, seg_col = seg, seg.reshape(seq, 1)
    live_row, live_col = live.reshape(1, seq), live.reshape(seq, 1)
    earlier = jnp.sum((seg_row < seg_col).astype(jnp.int32), axis=1)
    position = (jnp.arange(seq, dtype=jnp.int32) - earlier).astype(F32)
    frequency = jnp.power(F32(THETA_BASE), -(jnp.arange(HD // 2, dtype=F32) * (2.0 / HD)))
    angle = position[:, None] * frequency[None, :]
    cosine, sine = jnp.cos(angle), jnp.sin(angle)
    repeats = LANES // HD
    cosine = jnp.concatenate([cosine, cosine] * repeats, axis=1)
    sine = jnp.concatenate([-sine, sine] * repeats, axis=1)
    me_vec = me.astype(jnp.int32).reshape(1)

    cfg = dict(half=half, rows=rows, layout=layout_qkv, units=units, main=main, model=model)
    width = 2 * half
    w_full, qkv, att, logt, n1, gain1 = call(
        functools.partial(attn_forward_kernel, cfg, len(own_qkv)),
        [me_vec, inputs, *own_qkv, *other_qkv, seg_row, seg_col, live_row, cosine, sine],
        [
            shape(model, 3 * width),
            shape(tokens, 3 * width),
            shape(tokens, width),
            shape(tokens, LANES, dtype=F32),
            shape(tokens, model),
            shape(8, model, dtype=F32),
        ],
        [pltpu.VMEM((model, LANES), BF16)],
        flops=2 * tokens * model * 3 * width,
    )
    ffn_cfg = dict(cfg, layout=layout_ffn)
    side = 2 * units + half + main + LANES
    output, grad_hidden, wo_full, swap1, keep1 = call(
        functools.partial(ffn_kernel, ffn_cfg, len(own_ffn)),
        [me_vec, inputs, att, cotangent, live_col, *own_ffn, *other_ffn],
        [
            shape(tokens, model),
            shape(tokens, model, dtype=F32),
            shape(model, width),
            shape(tokens + 16, 3 * model + side),
            shape(tokens, side),
        ],
        [pltpu.VMEM((model, 2 * units), BF16)] * 3 + [pltpu.VMEM((model, LANES), BF16)],
        flops=2 * tokens * model * 12 * units,
    )

    def grads(sections, swap_mine, keep, cfg):
        total = cfg["total"]
        outs = [shape(model, total, dtype=F32)]
        if fast:
            outs = [shape(8, rows, last - first) for _, (first, last) in cfg["emit"] for _ in "ks"]
        theirs = swap_cores(swap_mine)
        return call(
            functools.partial(grads_kernel, cfg, sections, fast),
            [me_vec, swap_mine, keep, theirs],
            outs,
            [pltpu.VMEM((model, total), F32)],
            flops=4 * tokens * model * total,
        )

    sections1 = [
        (0, 0, 2 * units),
        (2 * model, 2 * units, half),
        (model, 2 * units + half, main + LANES),
    ]
    mid = cut + (side - cut) // 2 // LANES * LANES
    emit1 = [(GRAD_C, (0, cut)), (GRAD_A, (cut, mid)), (GRAD_B, (mid, side))]
    cfg1 = dict(ffn_cfg, base=3 * model, total=side, gain_lane=tail, emit=emit1)
    pieces1 = grads(sections1, swap1, keep1, cfg1)
    grad_inputs, swap2, keep2 = call(
        functools.partial(attn_backward_kernel, cfg),
        [
            inputs, grad_hidden, wo_full, w_full, qkv, att, logt, gain1,
            seg_row, seg_col, live_row, cosine, sine, n1,
        ],
        [
            shape(tokens, model, dtype=F32),
            shape(tokens + 16, model + 3 * half),
            shape(tokens, 3 * half),
        ],
        [pltpu.VMEM((tokens, width), BF16), pltpu.VMEM((tokens, 3 * width), BF16)],
        scalars=0,
        flops=2 * tokens * model * 5 * width,
    )
    total2 = 3 * half + LANES
    emit2 = [(GRAD_A, (0, total2 // 2)), (GRAD_B, (total2 // 2, total2))]
    cfg2 = dict(cfg, base=model, total=total2, gain_lane=0, emit=emit2)
    pieces2 = grads([(0, 0, 3 * half)], swap2, keep2, cfg2)

    if fast:
        keep_c, send_c, keep_a, send_a, keep_b, send_b = pieces1
        keep_a, send_a, keep_b, send_b = combine(
            False, keep_a, exchange(send_a, X), keep_b, exchange(send_b, Y)
        )
        keep_c, send_c = combine(False, keep_c, exchange(send_c, Z))
        keep_c, send_c = combine(False, keep_c, exchange(send_c, ZZ))
        keep, send = combine(True, keep_a, exchange(send_a, Y), keep_b, exchange(send_b, X))
        keep_c, send_c = combine(False, keep_c, exchange(send_c, X))
        keep, send = combine(False, keep, exchange(send, Z))
        came_c, came = exchange(send_c, Y), exchange(send, ZZ)
        share1 = call(
            final_ffn_kernel,
            [keep_c, came_c, keep, came],
            [shape(rows, side, dtype=F32)],
            [],
            scalars=0,
        )[0]
        keep_a, send_a, keep_b, send_b = pieces2
        keep_a, send_a, keep_b, send_b = combine(
            False, keep_a, exchange(send_a, X), keep_b, exchange(send_b, Y)
        )
        keep, send = combine(True, keep_a, exchange(send_a, Y), keep_b, exchange(send_b, X))
        keep, send = combine(False, keep, exchange(send, Z))
        grad_qkv, gain1_share = call(
            final_qkv_kernel,
            [keep, exchange(send, ZZ)],
            [shape(3, rows, half, dtype=F32), shape(rows, LANES, dtype=F32)],
            [],
            scalars=0,
        )
        grad_gain1 = gain1_share[:, 0]
    else:
        share1, share2 = (
            lax.psum_scatter(pieces[0], "dp", scatter_dimension=0, tiled=True)
            for pieces in (pieces1, pieces2)
        )
        grad_qkv = jnp.stack([share2[:, c * half : (c + 1) * half] for c in range(3)])
        grad_gain1 = share2[:, 3 * half]
    heads = share1[:, : 2 * main].reshape(rows, 2, main)
    tails = share1[:, 2 * main : 2 * units].reshape(rows, 2, tail)
    grad_in = jnp.concatenate([heads, tails], axis=2)
    grad_out = share1[:, 2 * units : 2 * units + half].T
    grad_down = share1[:, 2 * units + half : 2 * units + half + units].T
    grad_gain2 = share1[:, 2 * units + half + units]
    return (
        output,
        grad_inputs,
        grad_gain1,
        grad_qkv,
        grad_out,
        grad_gain2,
        grad_in,
        grad_down,
    )


def fast_path(dp):
    return dp == 16


def solution(mesh):
    in_specs = (
        P(("dp", "tensor"), None),
        P("dp"),
        P(None, "dp", "tensor"),
        P("tensor", "dp"),
        P("dp"),
        P("dp", None, "tensor"),
        P("tensor", "dp"),
        P(("dp", "tensor"), None),
        P("dp", None),
        P("dp"),
        P("dp"),
    )
    out_specs = (
        P(("dp", "tensor"), None),
        P(("dp", "tensor"), None),
        P("dp"),
        P(None, "dp", "tensor"),
        P("tensor", "dp"),
        P("dp"),
        P("dp", None, "tensor"),
        P("tensor", "dp"),
    )

    return jax.shard_map(shards, mesh=mesh, in_specs=in_specs, out_specs=out_specs, check_vma=False)
```

```python
import functools
import math

import jax
import jax.numpy as jnp
from jax import lax
from jax.experimental import pallas as pl
from jax.experimental.pallas import tpu as pltpu
from jax.sharding import PartitionSpec as P


HD = 64
LANES = 128

THETA_BASE = 160000.0
EPSILON = 1e-05
SQRT_HALF = 0.7071067811865476
INV_ROOT_TWO_PI = 0.3989422804014327
MASKED_SCORE = -1e30

F32 = jnp.float32
BF16 = jnp.bfloat16


NN = (((1,), (0,)), ((), ()))
NT = (((1,), (1,)), ((), ()))
TN = (((0,), (0,)), ((), ()))

X, Y, Z, ZZ = 1, 2, 4, 8
Z_ALL = (0, Z, ZZ, Z | ZZ)
Z_HALVES = (0, ZZ, Z, Z | ZZ)
XY_ALL = (0, X, Y, X | Y)
XY_HALVES = (0, Y, X, X | Y)


def shift(distances, by):
    return tuple(d ^ by for d in distances)


PLANE_PIECES = (Z_ALL, shift(Z_ALL, X), shift(Z_ALL, Y), (3, 7), (11, 15))
LINE_PIECES = tuple(shift(XY_ALL, z) for z in Z_ALL)

GRAD_A = (tuple(y + z for y in (0, Y) for z in Z_HALVES), X)
GRAD_B = (tuple(x + z for x in (0, X) for z in Z_HALVES), Y)
GRAD_C = (tuple(z + xy for z in (0, ZZ) for xy in XY_HALVES), Z)


def mm(left, right, dims):
    return lax.dot_general(left, right, dims, preferred_element_type=F32)


def norm_parts(rows_in):
    centre = rows_in - jnp.mean(rows_in, axis=-1, keepdims=True)
    inv_std = lax.rsqrt(jnp.mean(centre * centre, axis=-1, keepdims=True) + EPSILON)
    return centre * inv_std, inv_std


def norm_back(grad_normed, normed, inv_std, gain_row):
    scaled = grad_normed * gain_row
    inner_mean = jnp.mean(scaled * normed, axis=-1, keepdims=True)
    grad_rows = inv_std * (scaled - jnp.mean(scaled, axis=-1, keepdims=True) - normed * inner_mean)
    return grad_rows, jnp.sum(grad_normed * normed, axis=0, keepdims=True)


def lane_index(shape):
    return lax.broadcasted_iota(jnp.int32, shape, 1)


def swap_halves(chunk):
    half = HD // 2
    return jnp.where(
        lane_index(chunk.shape) % HD < half,
        pltpu.roll(chunk, LANES - half, 1),
        pltpu.roll(chunk, half, 1),
    )


def column_to_row(columns, lane):
    pick = (lane_index((8, LANES)) == lane).astype(BF16)
    return mm(pick, columns, NT)[0:1]


def row_to_columns(row):
    return jnp.transpose(jnp.broadcast_to(row, (LANES, row.shape[1])), (1, 0))


class Pieces:
    def __init__(self, me, refs, rows, layout):
        self.me, self.refs, self.rows, self.layout = me, refs, rows, layout

    def copy(self, dst, dst_col, src_col, width):
        for ref, (distances, first, last) in zip(self.refs, self.layout):
            low, high = max(first, src_col), min(last, src_col + width)
            if low >= high:
                continue
            at = slice(dst_col + low - src_col, dst_col + high - src_col)
            cols = slice(low - first, high - first)
            if distances is None:
                dst[:, at] = ref[:, cols]
                continue
            for i, distance in enumerate(distances):
                base = pl.multiple_of((self.me ^ distance) * self.rows, self.rows)
                dst[pl.ds(base, self.rows), at] = ref[i, :, cols]


def attn_mask(seg_row, seg_col, live_row):
    same = seg_col == seg_row
    shape = same.shape
    diagonal = lax.broadcasted_iota(jnp.int32, shape, 0) == lane_index(shape)
    return (same & (live_row > 0)) | diagonal


def attn_forward_kernel(cfg, n_pieces, *refs):
    me_ref, x_ref = refs[:2]
    own = refs[2 : 2 + n_pieces]
    other = refs[2 + n_pieces : 2 + 2 * n_pieces]
    seg_row, seg_col, live_row, cos_ref, sin_ref = refs[2 + 2 * n_pieces : 7 + 2 * n_pieces]
    w_ref, qkv_ref, att_ref, logt_ref, n1_ref, gain_ref, gcol = refs[7 + 2 * n_pieces :]
    me = me_ref[0]
    half, width = cfg["half"], 2 * cfg["half"]
    for which, pieces in enumerate((own, other)):
        part = Pieces(me, pieces, cfg["rows"], cfg["layout"])
        for c in range(3):
            part.copy(w_ref, c * width + which * half, c * half, half)
        if which == 0:
            part.copy(gcol, 0, 3 * half, LANES)
    gain_row = column_to_row(gcol[...], 0)
    gain_ref[...] = jnp.broadcast_to(gain_row, gain_ref.shape)
    normed, _ = norm_parts(x_ref[...].astype(F32))
    n1 = (normed * gain_row).astype(BF16)
    n1_ref[...] = n1
    cosine, sine = cos_ref[...], sin_ref[...]
    step = 2 * LANES
    for at in range(0, 3 * width, step):
        product = mm(n1, w_ref[:, at : at + step], NN)
        for sub in range(0, step, LANES):
            chunk = product[:, sub : sub + LANES]
            if at < 2 * width:
                chunk = chunk * cosine + swap_halves(chunk) * sine
            qkv_ref[:, at + sub : at + sub + LANES] = chunk.astype(BF16)
    mask = attn_mask(seg_row[...], seg_col[...], live_row[...])
    scale = HD ** (-0.5)
    rows = x_ref.shape[0]
    low = lane_index((rows, LANES)) < HD
    lanes = lane_index((rows, LANES))
    totals = jnp.zeros((rows, LANES), F32)
    for pair in range(width // LANES):
        at = pair * LANES
        queries = qkv_ref[:, at : at + LANES]
        keys = qkv_ref[:, width + at : width + at + LANES]
        values = qkv_ref[:, 2 * width + at : 2 * width + at + LANES]
        outs = []
        for side in range(2):
            picked = jnp.where(low if side == 0 else ~low, queries, jnp.zeros_like(queries))
            scores = jnp.where(mask, mm(picked, keys, NT) * scale, MASKED_SCORE)
            row_max = jnp.max(scores, axis=-1, keepdims=True)
            weights = jnp.exp(scores - row_max)
            total = jnp.sum(weights, axis=-1, keepdims=True)
            prob = (weights * (1.0 / total)).astype(BF16)
            outs.append(mm(prob, values, NN))
            totals = jnp.where(lanes == 2 * pair + side, row_max + jnp.log(total), totals)
        att_ref[:, at : at + LANES] = jnp.where(low, outs[0], outs[1]).astype(BF16)
    logt_ref[...] = totals


def ffn_kernel(cfg, n_pieces, *refs):
    me_ref, x_ref, att_ref, cot_ref, live_ref = refs[:5]
    own = refs[5 : 5 + n_pieces]
    other = refs[5 + n_pieces : 5 + 2 * n_pieces]
    rest = refs[5 + 2 * n_pieces :]
    out_ref, gh_ref, wo_ref, swap_ref, keep_ref = rest[:5]
    win_ref, wgate_ref, wdown_ref, gcol = rest[5:]
    me = me_ref[0]
    half, units, main = cfg["half"], cfg["units"], cfg["main"]
    tail = units - main
    model = x_ref.shape[1]
    out_at = 2 * units
    for which, pieces in enumerate((own, other)):
        part = Pieces(me, pieces, cfg["rows"], cfg["layout"])
        part.copy(win_ref, which * main, 0, main)
        part.copy(wgate_ref, which * main, main, main)
        part.copy(win_ref, 2 * main + which * tail, 2 * main, tail)
        part.copy(wgate_ref, 2 * main + which * tail, 2 * main + tail, tail)
        part.copy(wo_ref, which * half, out_at, half)
        part.copy(wdown_ref, which * main, out_at + half, main)
        part.copy(wdown_ref, 2 * main + which * tail, out_at + half + main, tail)
        if which == 0:
            part.copy(gcol, 0, out_at + half + main, LANES)
    lanes8 = lane_index((8, LANES))
    pick = (lanes8 == tail).astype(BF16)
    gain_row = mm(pick, gcol[...], NT)[0:1]
    att = att_ref[...]
    hidden = x_ref[...].astype(F32) + mm(att, wo_ref[...], NT)
    normed, inv_std = norm_parts(hidden)
    n2 = (normed * gain_row).astype(BF16)
    live = live_ref[...]
    grad_mixed = live * cot_ref[...].astype(F32)
    grad_mixed_bf = grad_mixed.astype(BF16)
    rows = x_ref.shape[0]
    swap_ref[0:rows, 0:model] = n2
    swap_ref[0:rows, model : 2 * model] = grad_mixed_bf
    base = 3 * model
    step = 3 * LANES
    mixed = hidden
    grad_normed = jnp.zeros((rows, model), F32)
    for at in range(0, 2 * units, step):
        unit_in = mm(n2, win_ref[:, at : at + step], NN)
        unit_gate = mm(n2, wgate_ref[:, at : at + step], NN)
        grad_act = mm(grad_mixed_bf, wdown_ref[:, at : at + step], NN)
        cdf = 0.5 * (1.0 + lax.erf(unit_in * SQRT_HALF))
        gelu = unit_in * cdf
        slope = cdf + unit_in * INV_ROOT_TWO_PI * jnp.exp(-0.5 * unit_in * unit_in)
        activated = (gelu * unit_gate).astype(BF16)
        grad_in = (grad_act * unit_gate * slope).astype(BF16)
        grad_gate = (grad_act * gelu).astype(BF16)
        mixed = mixed + mm(activated, wdown_ref[:, at : at + step], NT)
        grad_normed = (
            grad_normed
            + mm(grad_in, win_ref[:, at : at + step], NT)
            + mm(grad_gate, wgate_ref[:, at : at + step], NT)
        )
        for sub in range(0, step, LANES):
            lo = at + sub
            a, gi, gg = (v[:, sub : sub + LANES] for v in (activated, grad_in, grad_gate))
            if lo < 2 * main:
                which, col = divmod(lo, main)
                ref, off = (keep_ref, 0) if which == 0 else (swap_ref, base)
                ref[0:rows, off + col : off + col + LANES] = gi
                ref[0:rows, off + main + col : off + main + col + LANES] = gg
                col = off + 2 * units + half + col
                ref[0:rows, col : col + LANES] = a
            else:
                low = lane_index((rows, LANES)) < tail
                gi, gg, a = gi.astype(F32), gg.astype(F32), a.astype(F32)
                mine = jnp.where(low, gi, pltpu.roll(gg, tail, 1)).astype(BF16)
                theirs = jnp.where(low, pltpu.roll(gi, tail, 1), gg).astype(BF16)
                at_tail = 2 * main
                keep_ref[0:rows, at_tail : at_tail + LANES] = mine
                swap_ref[0:rows, base + at_tail : base + at_tail + LANES] = theirs
                at_tail = 2 * units + half + main
                keep_ref[0:rows, at_tail : at_tail + LANES] = a.astype(BF16)
                swap_ref[0:rows, base + at_tail : base + at_tail + LANES] = pltpu.roll(
                    a, tail, 1
                ).astype(BF16)
    out_ref[...] = (live * mixed).astype(BF16)
    grad_rows, gain_term = norm_back(grad_normed, normed, inv_std, gain_row)
    grad_hidden = grad_mixed + grad_rows
    gh_ref[...] = grad_hidden
    swap_ref[0:rows, 2 * model : base] = grad_hidden.astype(BF16)
    keep_ref[0:rows, 2 * units : 2 * units + half] = att[:, 0:half]
    swap_ref[0:rows, base + 2 * units : base + 2 * units + half] = att[:, half:]
    put_gain(swap_ref, gain_term, rows)


def put_gain(ref, gain_term, rows):
    model = gain_term.shape[1]
    extra = ref.shape[0] - rows
    high = gain_term.astype(BF16).astype(F32)
    first = lax.broadcasted_iota(jnp.int32, (extra, model), 0)
    block = jnp.where(first == 0, high, jnp.where(first == 1, gain_term - high, 0.0))
    ref[rows:, 0:model] = block.astype(BF16)
    ref[rows:, model:] = jnp.zeros((extra, ref.shape[1] - model), BF16)


def attn_backward_kernel(cfg, *refs):
    (x_ref, gh_ref, wo_ref, w_ref, qkv_ref, att_ref, logt_ref, gain_ref) = refs[:8]
    seg_row, seg_col, live_row, cos_ref, sin_ref, n1_ref = refs[8:14]
    gin_ref, swap_ref, keep_ref, gatt_ref, gqkv_ref = refs[14:]
    half, width = cfg["half"], 2 * cfg["half"]
    rows, model = x_ref.shape
    gatt_ref[...] = mm(gh_ref[...].astype(BF16), wo_ref[...], NN).astype(BF16)
    mask = attn_mask(seg_row[...], seg_col[...], live_row[...])
    scale = HD ** (-0.5)
    low = lane_index((rows, LANES)) < HD
    cosine, sine = cos_ref[...], sin_ref[...]
    for pair in range(width // LANES):
        at = pair * LANES
        queries = qkv_ref[:, at : at + LANES]
        keys = qkv_ref[:, width + at : width + at + LANES]
        values = qkv_ref[:, 2 * width + at : 2 * width + at + LANES]
        grad_att = gatt_ref[:, at : at + LANES]
        products = grad_att.astype(F32) * att_ref[:, at : at + LANES].astype(F32)
        grads_q, grad_k, grad_v = [], 0.0, 0.0
        for side in range(2):
            on = low if side == 0 else ~low
            q_side = jnp.where(on, queries, jnp.zeros_like(queries))
            g_side = jnp.where(on, grad_att, jnp.zeros_like(grad_att))
            head = 2 * pair + side
            scores = jnp.where(mask, mm(q_side, keys, NT) * scale, MASKED_SCORE)
            prob = jnp.exp(scores - logt_ref[:, head : head + 1])
            row_inner = jnp.sum(jnp.where(on, products, 0.0), axis=-1, keepdims=True)
            grad_prob = mm(g_side, values, NT)
            grad_scores = (prob * (grad_prob - row_inner)).astype(BF16)
            grad_v = grad_v + mm(prob.astype(BF16), g_side, TN)
            grads_q.append(mm(grad_scores, keys, NN))
            grad_k = grad_k + mm(grad_scores, q_side, TN)
        grad_q = jnp.where(low, grads_q[0], grads_q[1]) * scale
        grad_k = grad_k * scale
        grad_q = grad_q * cosine - swap_halves(grad_q) * sine
        grad_k = grad_k * cosine - swap_halves(grad_k) * sine
        for c, value in enumerate((grad_q, grad_k, grad_v)):
            value = value.astype(BF16)
            gqkv_ref[:, c * width + at : c * width + at + LANES] = value
            if at < half:
                keep_ref[0:rows, c * half + at : c * half + at + LANES] = value
            else:
                col = model + c * half + at - half
                swap_ref[0:rows, col : col + LANES] = value
    swap_ref[0:rows, 0:model] = n1_ref[...]
    grad_normed = mm(gqkv_ref[...], w_ref[...], NT)
    normed, inv_std = norm_parts(x_ref[...].astype(F32))
    grad_rows, gain_term = norm_back(grad_normed, normed, inv_std, gain_ref[0:1])
    gin_ref[...] = gh_ref[...] + grad_rows
    put_gain(swap_ref, gain_term, rows)


def grads_kernel(cfg, sections, fast, me_ref, mine, keep, theirs, *refs):
    grad_ref = refs[-1]
    outs = refs[:-1]
    tokens = keep.shape[0]
    base = cfg["base"]
    for left, at, size in sections:
        l_mine = mine[0:tokens, left : left + cfg["model"]]
        l_theirs = theirs[0:tokens, left : left + cfg["model"]]
        grad_ref[:, at : at + size] = mm(l_mine, keep[:, at : at + size], TN) + mm(
            l_theirs, theirs[0:tokens, base + at : base + at + size], TN
        )
    gain = jnp.zeros((1, cfg["model"]), F32)
    for ref in (mine, theirs):
        block = ref[tokens:, 0 : cfg["model"]].astype(F32)
        gain = gain + block[0:1] + block[1:2]
    columns = row_to_columns(gain)
    total = grad_ref.shape[1]
    last = slice(total - LANES, total)
    if cfg["gain_lane"]:
        keep_low = lane_index(columns.shape) < cfg["gain_lane"]
        columns = jnp.where(keep_low, grad_ref[:, last], columns)
    grad_ref[:, last] = columns
    if not fast:
        outs[0][...] = grad_ref[...]
        return
    me, rows = me_ref[0], cfg["rows"]
    at = 0
    for (order, bit), (first, last) in cfg["emit"]:
        for which in (0, 1):
            for i, distance in enumerate(order):
                start = pl.multiple_of((me ^ distance ^ (bit * which)) * rows, rows)
                outs[at + which][i] = grad_ref[pl.ds(start, rows), first:last].astype(BF16)
        at += 2


def stack_kernel(*refs):
    for i, ref in enumerate(refs[:-1]):
        refs[-1][i] = ref[...]


def combine_kernel(joined, *refs):
    n = (len(refs) - 2) // 2 if joined else len(refs) // 4
    ins, outs = refs[: 2 * n], refs[2 * n :]
    at = 0
    for i in range(n):
        kept, came = ins[2 * i], ins[2 * i + 1]
        blocks, _, cols = kept.shape
        keep, send = (outs[0], outs[1]) if joined else (outs[2 * i], outs[2 * i + 1])
        for j in range(blocks):
            total = kept[j].astype(F32) + came[j].astype(F32)
            ref, k = (keep, j) if j < blocks // 2 else (send, j - blocks // 2)
            ref[k, :, at : at + cols] = total.astype(ref.dtype)
        at += cols if joined else 0


def final_ffn_kernel(kept_c, came_c, kept_ab, came_ab, share):
    cut = kept_c.shape[2]
    share[:, :cut] = kept_c[0] + came_c[0].astype(F32)
    share[:, cut:] = kept_ab[0] + came_ab[0].astype(F32)


def final_qkv_kernel(kept, came, grad, gain):
    half = grad.shape[2]
    for c in range(3):
        cols = slice(c * half, (c + 1) * half)
        grad[c] = kept[0, :, cols] + came[0, :, cols].astype(F32)
    gain[...] = kept[0, :, 3 * half :] + came[0, :, 3 * half :].astype(F32)


VMEM = pl.BlockSpec(memory_space=pltpu.VMEM)
SMEM = pl.BlockSpec(memory_space=pltpu.SMEM)


def call(kernel, operands, outs, scratch, scalars=1, flops=0, spare=1 << 20):
    moved = sum(o.size * o.dtype.itemsize for o in operands)
    moved += sum(s.size * s.dtype.itemsize for s in outs)
    held = sum(math.prod(s.shape) * jnp.dtype(s.dtype).itemsize for s in scratch)
    return pl.pallas_call(
        kernel,
        out_shape=outs,
        in_specs=[SMEM] * scalars + [VMEM] * (len(operands) - scalars),
        out_specs=[VMEM] * len(outs),
        scratch_shapes=scratch,
        cost_estimate=pl.CostEstimate(flops=flops, bytes_accessed=moved, transcendentals=0),
        compiler_params=pltpu.CompilerParams(vmem_limit_bytes=moved + held + spare),
    )(*operands)


def shape(*dims, dtype=BF16):
    return jax.ShapeDtypeStruct(dims, dtype)


def stack(planes):
    outs = [shape(len(planes), *planes[0].shape)]
    return call(stack_kernel, list(planes), outs, [], scalars=0)[0]


def combine(joined, *arrays):
    outs = []
    for kept in arrays[::2]:
        blocks, rows, cols = kept.shape
        outs += [shape(blocks // 2, rows, cols, dtype=F32), shape(blocks // 2, rows, cols)]
    if joined:
        blocks, rows = outs[0].shape[:2]
        cols = sum(o.shape[2] for o in outs[::2])
        outs = [shape(blocks, rows, cols, dtype=F32), shape(blocks, rows, cols)]
    kernel = functools.partial(combine_kernel, joined)
    return call(kernel, list(arrays), outs, [], scalars=0)


def shards(
    inputs, gain_attn, w_qkv, w_out, gain_ffn, w_in, w_down, cotangent, segments, lengths, counts
):
    dp, cores = lax.axis_size("dp"), lax.axis_size("tensor")
    me, core = lax.axis_index("dp"), lax.axis_index("tensor")
    seq = segments.shape[1]
    tokens, model = inputs.shape
    rows, half, units = gain_attn.shape[0], w_qkv.shape[2], w_in.shape[2]
    main = units // LANES * LANES
    tail = units - main
    if cores != 2 or tokens != seq or segments.shape[0] != cores or 2 * tail != LANES:
        raise ValueError("unsupported shapes")
    fast = fast_path(dp) and rows % 16 == 0

    def swap_cores(value):
        return lax.ppermute(value, "tensor", [(0, 1), (1, 0)])

    def exchange(value, distance):
        pairs = [(i, i ^ distance) for i in range(dp)]
        return lax.ppermute(value, "dp", pairs)

    def across_z(value):
        return [value] + [exchange(value, z) for z in Z_ALL[1:]]

    def plane(stacked):
        came_x = exchange(stacked, X)
        came_y = exchange(stacked, Y)
        far_a = exchange(came_y[:2], X)
        far_b = exchange(came_x[2:], Y)
        return [stacked, came_x, came_y, far_a, far_b]

    def both_cores(pieces):
        return [swap_cores(piece) for piece in pieces]

    pack_qkv = jnp.concatenate(
        [w_qkv[0], w_qkv[1], w_qkv[2], jnp.pad(gain_attn[:, None], ((0, 0), (0, LANES - 1)))],
        axis=1,
    )
    out_t, down_t = w_out.T, w_down.T
    pack_ffn = jnp.concatenate(
        [
            w_in[:, 0, :main],
            w_in[:, 1, :main],
            w_in[:, 0, main:],
            w_in[:, 1, main:],
            out_t,
            down_t,
            jnp.pad(gain_ffn[:, None], ((0, 0), (0, tail - 1))),
        ],
        axis=1,
    )
    total_qkv, total_ffn = pack_qkv.shape[1], pack_ffn.shape[1]
    cut = total_ffn * 3 // 10 // LANES * LANES
    if fast:
        own_qkv = plane(stack(across_z(pack_qkv)))
        other_qkv = both_cores(own_qkv)
        pack_c, pack_f = pack_ffn[:, :cut], pack_ffn[:, cut:]
        came_x, came_y = exchange(pack_c, X), exchange(pack_c, Y)
        stack_c = stack([pack_c, came_x, came_y, exchange(came_y, X)])
        own_c = across_z(stack_c)
        own_f = plane(stack(across_z(pack_f)))
        own_ffn = own_c + own_f
        other_ffn = both_cores(own_c) + both_cores(own_f)
        layout_qkv = [(d, 0, total_qkv) for d in PLANE_PIECES]
        layout_ffn = [(d, 0, cut) for d in LINE_PIECES]
        layout_ffn += [(d, cut, total_ffn) for d in PLANE_PIECES]
    else:
        own_qkv = [lax.all_gather(pack_qkv, "dp", axis=0, tiled=True)]
        own_ffn = [lax.all_gather(pack_ffn, "dp", axis=0, tiled=True)]
        other_qkv, other_ffn = both_cores(own_qkv), both_cores(own_ffn)
        layout_qkv, layout_ffn = [(None, 0, total_qkv)], [(None, 0, total_ffn)]

    seg = lax.dynamic_slice_in_dim(segments, core, 1, axis=0)
    length = lax.dynamic_slice_in_dim(lengths, core, 1, axis=0)
    live = ((jnp.arange(seq, dtype=jnp.int32) < length) & (core < counts[0])).astype(F32)
    seg_row, seg_col = seg, seg.reshape(seq, 1)
    live_row, live_col = live.reshape(1, seq), live.reshape(seq, 1)
    earlier = jnp.sum((seg_row < seg_col).astype(jnp.int32), axis=1)
    position = (jnp.arange(seq, dtype=jnp.int32) - earlier).astype(F32)
    frequency = jnp.power(F32(THETA_BASE), -(jnp.arange(HD // 2, dtype=F32) * (2.0 / HD)))
    angle = position[:, None] * frequency[None, :]
    cosine, sine = jnp.cos(angle), jnp.sin(angle)
    repeats = LANES // HD
    cosine = jnp.concatenate([cosine, cosine] * repeats, axis=1)
    sine = jnp.concatenate([-sine, sine] * repeats, axis=1)
    me_vec = me.astype(jnp.int32).reshape(1)

    cfg = dict(half=half, rows=rows, layout=layout_qkv, units=units, main=main, model=model)
    width = 2 * half
    w_full, qkv, att, logt, n1, gain1 = call(
        functools.partial(attn_forward_kernel, cfg, len(own_qkv)),
        [me_vec, inputs, *own_qkv, *other_qkv, seg_row, seg_col, live_row, cosine, sine],
        [
            shape(model, 3 * width),
            shape(tokens, 3 * width),
            shape(tokens, width),
            shape(tokens, LANES, dtype=F32),
            shape(tokens, model),
            shape(8, model, dtype=F32),
        ],
        [pltpu.VMEM((model, LANES), BF16)],
        flops=2 * tokens * model * 3 * width,
        spare=6 << 20,
    )
    ffn_cfg = dict(cfg, layout=layout_ffn)
    side = 2 * units + half + main + LANES
    output, grad_hidden, wo_full, swap1, keep1 = call(
        functools.partial(ffn_kernel, ffn_cfg, len(own_ffn)),
        [me_vec, inputs, att, cotangent, live_col, *own_ffn, *other_ffn],
        [
            shape(tokens, model),
            shape(tokens, model, dtype=F32),
            shape(model, width),
            shape(tokens + 16, 3 * model + side),
            shape(tokens, side),
        ],
        [pltpu.VMEM((model, 2 * units), BF16)] * 3 + [pltpu.VMEM((model, LANES), BF16)],
        flops=2 * tokens * model * 12 * units,
        spare=6 << 20,
    )

    def grads(sections, swap_mine, keep, cfg):
        total = cfg["total"]
        outs = [shape(model, total, dtype=F32)]
        if fast:
            outs = [shape(8, rows, last - first) for _, (first, last) in cfg["emit"] for _ in "ks"]
        theirs = swap_cores(swap_mine)
        return call(
            functools.partial(grads_kernel, cfg, sections, fast),
            [me_vec, swap_mine, keep, theirs],
            outs,
            [pltpu.VMEM((model, total), F32)],
            flops=4 * tokens * model * total,
            spare=6 << 20,
        )

    sections1 = [
        (0, 0, 2 * units),
        (2 * model, 2 * units, half),
        (model, 2 * units + half, main + LANES),
    ]
    mid = cut + (side - cut) // 2 // LANES * LANES
    emit1 = [(GRAD_C, (0, cut)), (GRAD_A, (cut, mid)), (GRAD_B, (mid, side))]
    cfg1 = dict(ffn_cfg, base=3 * model, total=side, gain_lane=tail, emit=emit1)
    pieces1 = grads(sections1, swap1, keep1, cfg1)
    grad_inputs, swap2, keep2 = call(
        functools.partial(attn_backward_kernel, cfg),
        [
            inputs, grad_hidden, wo_full, w_full, qkv, att, logt, gain1,
            seg_row, seg_col, live_row, cosine, sine, n1,
        ],
        [
            shape(tokens, model, dtype=F32),
            shape(tokens + 16, model + 3 * half),
            shape(tokens, 3 * half),
        ],
        [pltpu.VMEM((tokens, width), BF16), pltpu.VMEM((tokens, 3 * width), BF16)],
        scalars=0,
        flops=2 * tokens * model * 5 * width,
        spare=6 << 20,
    )
    total2 = 3 * half + LANES
    emit2 = [(GRAD_A, (0, total2 // 2)), (GRAD_B, (total2 // 2, total2))]
    cfg2 = dict(cfg, base=model, total=total2, gain_lane=0, emit=emit2)
    pieces2 = grads([(0, 0, 3 * half)], swap2, keep2, cfg2)

    if fast:
        keep_c, send_c, keep_a, send_a, keep_b, send_b = pieces1
        keep_a, send_a, keep_b, send_b = combine(
            False, keep_a, exchange(send_a, X), keep_b, exchange(send_b, Y)
        )
        keep_c, send_c = combine(False, keep_c, exchange(send_c, Z))
        keep_c, send_c = combine(False, keep_c, exchange(send_c, ZZ))
        keep, send = combine(True, keep_a, exchange(send_a, Y), keep_b, exchange(send_b, X))
        keep_c, send_c = combine(False, keep_c, exchange(send_c, X))
        keep, send = combine(False, keep, exchange(send, Z))
        came_c, came = exchange(send_c, Y), exchange(send, ZZ)
        share1 = call(
            final_ffn_kernel,
            [keep_c, came_c, keep, came],
            [shape(rows, side, dtype=F32)],
            [],
            scalars=0,
        )[0]
        keep_a, send_a, keep_b, send_b = pieces2
        keep_a, send_a, keep_b, send_b = combine(
            False, keep_a, exchange(send_a, X), keep_b, exchange(send_b, Y)
        )
        keep, send = combine(True, keep_a, exchange(send_a, Y), keep_b, exchange(send_b, X))
        keep, send = combine(False, keep, exchange(send, Z))
        grad_qkv, gain1_share = call(
            final_qkv_kernel,
            [keep, exchange(send, ZZ)],
            [shape(3, rows, half, dtype=F32), shape(rows, LANES, dtype=F32)],
            [],
            scalars=0,
        )
        grad_gain1 = gain1_share[:, 0]
    else:
        share1, share2 = (
            lax.psum_scatter(pieces[0], "dp", scatter_dimension=0, tiled=True)
            for pieces in (pieces1, pieces2)
        )
        grad_qkv = jnp.stack([share2[:, c * half : (c + 1) * half] for c in range(3)])
        grad_gain1 = share2[:, 3 * half]
    heads = share1[:, : 2 * main].reshape(rows, 2, main)
    tails = share1[:, 2 * main : 2 * units].reshape(rows, 2, tail)
    grad_in = jnp.concatenate([heads, tails], axis=2)
    grad_out = share1[:, 2 * units : 2 * units + half].T
    grad_down = share1[:, 2 * units + half : 2 * units + half + units].T
    grad_gain2 = share1[:, 2 * units + half + units]
    return (
        output,
        grad_inputs,
        grad_gain1,
        grad_qkv,
        grad_out,
        grad_gain2,
        grad_in,
        grad_down,
    )


def fast_path(dp):
    return dp == 16


def solution(mesh):
    in_specs = (
        P(("dp", "tensor"), None),
        P("dp"),
        P(None, "dp", "tensor"),
        P("tensor", "dp"),
        P("dp"),
        P("dp", None, "tensor"),
        P("tensor", "dp"),
        P(("dp", "tensor"), None),
        P("dp", None),
        P("dp"),
        P("dp"),
    )
    out_specs = (
        P(("dp", "tensor"), None),
        P(("dp", "tensor"), None),
        P("dp"),
        P(None, "dp", "tensor"),
        P("tensor", "dp"),
        P("dp"),
        P("dp", None, "tensor"),
        P("tensor", "dp"),
    )

    return jax.shard_map(shards, mesh=mesh, in_specs=in_specs, out_specs=out_specs, check_vma=False)
```

```python
import functools
import math

import jax
import jax.numpy as jnp
from jax import lax
from jax.experimental import pallas as pl
from jax.experimental.pallas import tpu as pltpu
from jax.sharding import PartitionSpec as P


HD = 64
LANES = 128

THETA_BASE = 160000.0
EPSILON = 1e-05
SQRT_HALF = 0.7071067811865476
INV_ROOT_TWO_PI = 0.3989422804014327
MASKED_SCORE = -1e30

F32 = jnp.float32
BF16 = jnp.bfloat16


NN = (((1,), (0,)), ((), ()))
NT = (((1,), (1,)), ((), ()))
TN = (((0,), (0,)), ((), ()))

X, Y, Z, ZZ = 1, 2, 4, 8
Z_ALL = (0, Z, ZZ, Z | ZZ)
Z_HALVES = (0, ZZ, Z, Z | ZZ)
XY_ALL = (0, X, Y, X | Y)
XY_HALVES = (0, Y, X, X | Y)


def shift(distances, by):
    return tuple(d ^ by for d in distances)


PLANE_PIECES = (Z_ALL, shift(Z_ALL, X), shift(Z_ALL, Y), (3, 7), (11, 15))
LINE_PIECES = tuple(shift(XY_ALL, z) for z in Z_ALL)

GRAD_A = (tuple(y + z for y in (0, Y) for z in Z_HALVES), X)
GRAD_B = (tuple(x + z for x in (0, X) for z in Z_HALVES), Y)
GRAD_C = (tuple(z + xy for z in (0, ZZ) for xy in XY_HALVES), Z)


def mm(left, right, dims):
    return lax.dot_general(left, right, dims, preferred_element_type=F32)


def norm_parts(rows_in):
    centre = rows_in - jnp.mean(rows_in, axis=-1, keepdims=True)
    inv_std = lax.rsqrt(jnp.mean(centre * centre, axis=-1, keepdims=True) + EPSILON)
    return centre * inv_std, inv_std


def norm_back(grad_normed, normed, inv_std, gain_row):
    scaled = grad_normed * gain_row
    inner_mean = jnp.mean(scaled * normed, axis=-1, keepdims=True)
    grad_rows = inv_std * (scaled - jnp.mean(scaled, axis=-1, keepdims=True) - normed * inner_mean)
    return grad_rows, jnp.sum(grad_normed * normed, axis=0, keepdims=True)


def lane_index(shape):
    return lax.broadcasted_iota(jnp.int32, shape, 1)


def swap_halves(chunk):
    half = HD // 2
    return jnp.where(
        lane_index(chunk.shape) % HD < half,
        pltpu.roll(chunk, LANES - half, 1),
        pltpu.roll(chunk, half, 1),
    )


def column_to_row(columns, lane):
    pick = (lane_index((8, LANES)) == lane).astype(BF16)
    return mm(pick, columns, NT)[0:1]


def row_to_columns(row):
    return jnp.transpose(jnp.broadcast_to(row, (LANES, row.shape[1])), (1, 0))


class Pieces:
    def __init__(self, me, refs, rows, layout):
        self.me, self.refs, self.rows, self.layout = me, refs, rows, layout

    def copy(self, dst, dst_col, src_col, width):
        for ref, (distances, first, last) in zip(self.refs, self.layout):
            low, high = max(first, src_col), min(last, src_col + width)
            if low >= high:
                continue
            at = slice(dst_col + low - src_col, dst_col + high - src_col)
            cols = slice(low - first, high - first)
            if distances is None:
                dst[:, at] = ref[:, cols]
                continue
            for i, distance in enumerate(distances):
                base = pl.multiple_of((self.me ^ distance) * self.rows, self.rows)
                dst[pl.ds(base, self.rows), at] = ref[i, :, cols]


def attn_mask(seg_row, seg_col, live_row):
    same = seg_col == seg_row
    shape = same.shape
    diagonal = lax.broadcasted_iota(jnp.int32, shape, 0) == lane_index(shape)
    return (same & (live_row > 0)) | diagonal


def attn_forward_kernel(cfg, n_pieces, *refs):
    me_ref, x_ref = refs[:2]
    own = refs[2 : 2 + n_pieces]
    other = refs[2 + n_pieces : 2 + 2 * n_pieces]
    seg_row, seg_col, live_row, cos_ref, sin_ref = refs[2 + 2 * n_pieces : 7 + 2 * n_pieces]
    w_ref, qkv_ref, att_ref, far_ref, logt_ref, n1_ref, gain_ref, gcol = refs[7 + 2 * n_pieces :]
    me = me_ref[0]
    half, width = cfg["half"], 2 * cfg["half"]
    for which, pieces in enumerate((own, other)):
        part = Pieces(me, pieces, cfg["rows"], cfg["layout"])
        for c in range(3):
            part.copy(w_ref, c * width + which * half, c * half, half)
        if which == 0:
            part.copy(gcol, 0, 3 * half, LANES)
    gain_row = column_to_row(gcol[...], 0)
    gain_ref[...] = jnp.broadcast_to(gain_row, gain_ref.shape)
    normed, _ = norm_parts(x_ref[...].astype(F32))
    n1 = (normed * gain_row).astype(BF16)
    n1_ref[...] = n1
    cosine, sine = cos_ref[...], sin_ref[...]
    step = 2 * LANES
    for at in range(0, 3 * width, step):
        product = mm(n1, w_ref[:, at : at + step], NN)
        for sub in range(0, step, LANES):
            chunk = product[:, sub : sub + LANES]
            if at < 2 * width:
                chunk = chunk * cosine + swap_halves(chunk) * sine
            qkv_ref[:, at + sub : at + sub + LANES] = chunk.astype(BF16)
    mask = attn_mask(seg_row[...], seg_col[...], live_row[...])
    scale = HD ** (-0.5)
    rows = x_ref.shape[0]
    low = lane_index((rows, LANES)) < HD
    lanes = lane_index((rows, LANES))
    totals = jnp.zeros((rows, LANES), F32)
    for pair in range(width // LANES):
        at = pair * LANES
        queries = qkv_ref[:, at : at + LANES]
        keys = qkv_ref[:, width + at : width + at + LANES]
        values = qkv_ref[:, 2 * width + at : 2 * width + at + LANES]
        outs = []
        for side in range(2):
            picked = jnp.where(low if side == 0 else ~low, queries, jnp.zeros_like(queries))
            scores = jnp.where(mask, mm(picked, keys, NT) * scale, MASKED_SCORE)
            row_max = jnp.max(scores, axis=-1, keepdims=True)
            weights = jnp.exp(scores - row_max)
            total = jnp.sum(weights, axis=-1, keepdims=True)
            prob = (weights * (1.0 / total)).astype(BF16)
            outs.append(mm(prob, values, NN))
            totals = jnp.where(lanes == 2 * pair + side, row_max + jnp.log(total), totals)
        attended = jnp.where(low, outs[0], outs[1]).astype(BF16)
        att_ref[:, at : at + LANES] = attended
        if at >= half:
            far_ref[:, at - half : at - half + LANES] = attended
    logt_ref[...] = totals


def ffn_kernel(cfg, n_pieces, *refs):
    me_ref, x_ref, att_ref, gm_ref, live_ref = refs[:5]
    own = refs[5 : 5 + n_pieces]
    other = refs[5 + n_pieces : 5 + 2 * n_pieces]
    rest = refs[5 + 2 * n_pieces :]
    out_ref, hidden_ref, gain_ref, wo_ref, win_ref, wgate_ref, gi_ref, gg_ref = rest[:8]
    swap_ref, keep_ref, wdown_ref, gcol = rest[8:]
    me = me_ref[0]
    half, units, main = cfg["half"], cfg["units"], cfg["main"]
    tail = units - main
    rows, model = x_ref.shape
    out_at = 2 * units
    for which, pieces in enumerate((own, other)):
        part = Pieces(me, pieces, cfg["rows"], cfg["layout"])
        part.copy(win_ref, which * main, 0, main)
        part.copy(wgate_ref, which * main, main, main)
        part.copy(win_ref, 2 * main + which * tail, 2 * main, tail)
        part.copy(wgate_ref, 2 * main + which * tail, 2 * main + tail, tail)
        part.copy(wo_ref, which * half, out_at, half)
        part.copy(wdown_ref, which * main, out_at + half, main)
        part.copy(wdown_ref, 2 * main + which * tail, out_at + half + main, tail)
        if which == 0:
            part.copy(gcol, 0, out_at + half + main, LANES)
    gain_row = column_to_row(gcol[...], tail)
    gain_ref[...] = jnp.broadcast_to(gain_row, gain_ref.shape)
    hidden = x_ref[...].astype(F32) + mm(att_ref[...], wo_ref[...], NT)
    hidden_ref[...] = hidden
    n2 = (norm_parts(hidden)[0] * gain_row).astype(BF16)
    swap_ref[:, 0:model] = n2
    grad_mixed = gm_ref[...]
    step = 3 * LANES
    mixed = hidden
    for at in range(0, 2 * units, step):
        unit_in = mm(n2, win_ref[:, at : at + step], NN)
        unit_gate = mm(n2, wgate_ref[:, at : at + step], NN)
        grad_act = mm(grad_mixed, wdown_ref[:, at : at + step], NN)
        cdf = 0.5 * (1.0 + lax.erf(unit_in * SQRT_HALF))
        gelu = unit_in * cdf
        slope = cdf + unit_in * INV_ROOT_TWO_PI * jnp.exp(-0.5 * unit_in * unit_in)
        activated = (gelu * unit_gate).astype(BF16)
        grad_in = (grad_act * unit_gate * slope).astype(BF16)
        grad_gate = (grad_act * gelu).astype(BF16)
        gi_ref[:, at : at + step] = grad_in
        gg_ref[:, at : at + step] = grad_gate
        mixed = mixed + mm(activated, wdown_ref[:, at : at + step], NT)
        for sub in range(0, step, LANES):
            lo = at + sub
            a, gi, gg = (v[:, sub : sub + LANES] for v in (activated, grad_in, grad_gate))
            if lo < 2 * main:
                which, col = divmod(lo, main)
                ref, off = (keep_ref, 0) if which == 0 else (swap_ref, model)
                for value, start in ((gi, 0), (gg, main), (a, 2 * units)):
                    ref[:, off + start + col : off + start + col + LANES] = value
            else:
                low = lane_index((rows, LANES)) < tail
                gi, gg, a = gi.astype(F32), gg.astype(F32), a.astype(F32)
                mine = jnp.where(low, gi, pltpu.roll(gg, tail, 1))
                theirs = jnp.where(low, pltpu.roll(gi, tail, 1), gg)
                for start, here, there in (
                    (2 * main, mine, theirs),
                    (2 * units + main, a, pltpu.roll(a, tail, 1)),
                ):
                    keep_ref[:, start : start + LANES] = here.astype(BF16)
                    start += model
                    swap_ref[:, start : start + LANES] = there.astype(BF16)
    out_ref[...] = (live_ref[...] * mixed).astype(BF16)


def ffn_backward_kernel(hidden_ref, gm_ref, gain_ref, win_ref, wgate_ref, gi_ref, gg_ref, *outs):
    gh_ref, swap_ref = outs
    rows, _ = hidden_ref.shape
    grad_normed = mm(gi_ref[...], win_ref[...], NT) + mm(gg_ref[...], wgate_ref[...], NT)
    normed, inv_std = norm_parts(hidden_ref[...])
    grad_rows, gain_term = norm_back(grad_normed, normed, inv_std, gain_ref[0:1])
    grad_hidden = gm_ref[...].astype(F32) + grad_rows
    gh_ref[...] = grad_hidden
    swap_ref[0:rows, :] = grad_hidden.astype(BF16)
    put_gain(swap_ref, gain_term, rows)


def put_gain(ref, gain_term, rows):
    model = gain_term.shape[1]
    extra = ref.shape[0] - rows
    high = gain_term.astype(BF16).astype(F32)
    first = lax.broadcasted_iota(jnp.int32, (extra, model), 0)
    block = jnp.where(first == 0, high, jnp.where(first == 1, gain_term - high, 0.0))
    ref[rows:, 0:model] = block.astype(BF16)
    if ref.shape[1] > model:
        ref[rows:, model:] = jnp.zeros((extra, ref.shape[1] - model), BF16)


def attn_backward_kernel(cfg, *refs):
    (x_ref, gh_ref, wo_ref, w_ref, qkv_ref, att_ref, logt_ref, gain_ref) = refs[:8]
    seg_row, seg_col, live_row, cos_ref, sin_ref, n1_ref = refs[8:14]
    gin_ref, swap_ref, keep_ref, gatt_ref, gqkv_ref = refs[14:]
    half, width = cfg["half"], 2 * cfg["half"]
    rows, model = x_ref.shape
    gatt_ref[...] = mm(gh_ref[...].astype(BF16), wo_ref[...], NN).astype(BF16)
    mask = attn_mask(seg_row[...], seg_col[...], live_row[...])
    scale = HD ** (-0.5)
    low = lane_index((rows, LANES)) < HD
    cosine, sine = cos_ref[...], sin_ref[...]
    for pair in range(width // LANES):
        at = pair * LANES
        queries = qkv_ref[:, at : at + LANES]
        keys = qkv_ref[:, width + at : width + at + LANES]
        values = qkv_ref[:, 2 * width + at : 2 * width + at + LANES]
        grad_att = gatt_ref[:, at : at + LANES]
        products = grad_att.astype(F32) * att_ref[:, at : at + LANES].astype(F32)
        grads_q, grad_k, grad_v = [], 0.0, 0.0
        for side in range(2):
            on = low if side == 0 else ~low
            q_side = jnp.where(on, queries, jnp.zeros_like(queries))
            g_side = jnp.where(on, grad_att, jnp.zeros_like(grad_att))
            head = 2 * pair + side
            scores = jnp.where(mask, mm(q_side, keys, NT) * scale, MASKED_SCORE)
            prob = jnp.exp(scores - logt_ref[:, head : head + 1])
            row_inner = jnp.sum(jnp.where(on, products, 0.0), axis=-1, keepdims=True)
            grad_prob = mm(g_side, values, NT)
            grad_scores = (prob * (grad_prob - row_inner)).astype(BF16)
            grad_v = grad_v + mm(prob.astype(BF16), g_side, TN)
            grads_q.append(mm(grad_scores, keys, NN))
            grad_k = grad_k + mm(grad_scores, q_side, TN)
        grad_q = jnp.where(low, grads_q[0], grads_q[1]) * scale
        grad_k = grad_k * scale
        grad_q = grad_q * cosine - swap_halves(grad_q) * sine
        grad_k = grad_k * cosine - swap_halves(grad_k) * sine
        for c, value in enumerate((grad_q, grad_k, grad_v)):
            value = value.astype(BF16)
            gqkv_ref[:, c * width + at : c * width + at + LANES] = value
            if at < half:
                keep_ref[0:rows, c * half + at : c * half + at + LANES] = value
            else:
                col = model + c * half + at - half
                swap_ref[0:rows, col : col + LANES] = value
    swap_ref[0:rows, 0:model] = n1_ref[...]
    grad_normed = mm(gqkv_ref[...], w_ref[...], NT)
    normed, inv_std = norm_parts(x_ref[...].astype(F32))
    grad_rows, gain_term = norm_back(grad_normed, normed, inv_std, gain_ref[0:1])
    gin_ref[...] = gh_ref[...] + grad_rows
    put_gain(swap_ref, gain_term, rows)


def grads_kernel(cfg, sections, n_in, fast, me_ref, *refs):
    ins, outs, grad_ref = refs[:n_in], refs[n_in:-1], refs[-1]
    model = cfg["model"]
    tokens = cfg["tokens"]
    for pairs, at, size in sections:
        total = 0.0
        for (left, left_at), (right, right_at) in pairs:
            total = total + mm(
                ins[left][0:tokens, left_at : left_at + model],
                ins[right][0:tokens, right_at : right_at + size],
                TN,
            )
        grad_ref[:, at : at + size] = total
    gain = jnp.zeros((1, model), F32)
    for which in cfg["gain_from"]:
        block = ins[which][tokens:, 0:model].astype(F32)
        gain = gain + block[0:1] + block[1:2]
    columns = row_to_columns(gain)
    total = grad_ref.shape[1]
    last = slice(total - LANES, total)
    if cfg["gain_lane"]:
        keep_low = lane_index(columns.shape) < cfg["gain_lane"]
        columns = jnp.where(keep_low, grad_ref[:, last], columns)
    grad_ref[:, last] = columns
    if not fast:
        outs[0][...] = grad_ref[...]
        return
    me, rows = me_ref[0], cfg["rows"]
    at = 0
    for (order, bit), (first, last) in cfg["emit"]:
        for which in (0, 1):
            for i, distance in enumerate(order):
                start = pl.multiple_of((me ^ distance ^ (bit * which)) * rows, rows)
                outs[at + which][i] = grad_ref[pl.ds(start, rows), first:last].astype(BF16)
        at += 2


def stack_kernel(*refs):
    for i, ref in enumerate(refs[:-1]):
        refs[-1][i] = ref[...]


def combine_kernel(joined, *refs):
    n = (len(refs) - 2) // 2 if joined else len(refs) // 4
    ins, outs = refs[: 2 * n], refs[2 * n :]
    at = 0
    for i in range(n):
        kept, came = ins[2 * i], ins[2 * i + 1]
        blocks, _, cols = kept.shape
        keep, send = (outs[0], outs[1]) if joined else (outs[2 * i], outs[2 * i + 1])
        for j in range(blocks):
            total = kept[j].astype(F32) + came[j].astype(F32)
            ref, k = (keep, j) if j < blocks // 2 else (send, j - blocks // 2)
            ref[k, :, at : at + cols] = total.astype(ref.dtype)
        at += cols if joined else 0


def final_ffn_kernel(kept_c, came_c, kept_ab, came_ab, share):
    cut = kept_c.shape[2]
    share[:, :cut] = kept_c[0] + came_c[0].astype(F32)
    share[:, cut:] = kept_ab[0] + came_ab[0].astype(F32)


def final_qkv_kernel(kept, came, grad, gain):
    half = grad.shape[2]
    for c in range(3):
        cols = slice(c * half, (c + 1) * half)
        grad[c] = kept[0, :, cols] + came[0, :, cols].astype(F32)
    gain[...] = kept[0, :, 3 * half :] + came[0, :, 3 * half :].astype(F32)


VMEM = pl.BlockSpec(memory_space=pltpu.VMEM)
SMEM = pl.BlockSpec(memory_space=pltpu.SMEM)


def call(kernel, operands, outs, scratch, scalars=1, flops=0, spare=1 << 20):
    moved = sum(o.size * o.dtype.itemsize for o in operands)
    moved += sum(s.size * s.dtype.itemsize for s in outs)
    held = sum(math.prod(s.shape) * jnp.dtype(s.dtype).itemsize for s in scratch)
    return pl.pallas_call(
        kernel,
        out_shape=outs,
        in_specs=[SMEM] * scalars + [VMEM] * (len(operands) - scalars),
        out_specs=[VMEM] * len(outs),
        scratch_shapes=scratch,
        cost_estimate=pl.CostEstimate(flops=flops, bytes_accessed=moved, transcendentals=0),
        compiler_params=pltpu.CompilerParams(vmem_limit_bytes=moved + held + spare),
    )(*operands)


def shape(*dims, dtype=BF16):
    return jax.ShapeDtypeStruct(dims, dtype)


def stack(planes):
    outs = [shape(len(planes), *planes[0].shape)]
    return call(stack_kernel, list(planes), outs, [], scalars=0)[0]


def combine(joined, *arrays):
    outs = []
    for kept in arrays[::2]:
        blocks, rows, cols = kept.shape
        outs += [shape(blocks // 2, rows, cols, dtype=F32), shape(blocks // 2, rows, cols)]
    if joined:
        blocks, rows = outs[0].shape[:2]
        cols = sum(o.shape[2] for o in outs[::2])
        outs = [shape(blocks, rows, cols, dtype=F32), shape(blocks, rows, cols)]
    kernel = functools.partial(combine_kernel, joined)
    return call(kernel, list(arrays), outs, [], scalars=0)


def shards(
    inputs, gain_attn, w_qkv, w_out, gain_ffn, w_in, w_down, cotangent, segments, lengths, counts
):
    dp, cores = lax.axis_size("dp"), lax.axis_size("tensor")
    me, core = lax.axis_index("dp"), lax.axis_index("tensor")
    seq = segments.shape[1]
    tokens, model = inputs.shape
    rows, half, units = gain_attn.shape[0], w_qkv.shape[2], w_in.shape[2]
    main = units // LANES * LANES
    tail = units - main
    if cores != 2 or tokens != seq or segments.shape[0] != cores or 2 * tail != LANES:
        raise ValueError("unsupported shapes")
    fast = fast_path(dp) and rows % 16 == 0

    def swap_cores(value):
        return lax.ppermute(value, "tensor", [(0, 1), (1, 0)])

    def exchange(value, distance):
        pairs = [(i, i ^ distance) for i in range(dp)]
        return lax.ppermute(value, "dp", pairs)

    def across_z(value):
        return [value] + [exchange(value, z) for z in Z_ALL[1:]]

    def plane(stacked):
        came_x = exchange(stacked, X)
        came_y = exchange(stacked, Y)
        far_a = exchange(came_y[:2], X)
        far_b = exchange(came_x[2:], Y)
        return [stacked, came_x, came_y, far_a, far_b]

    def both_cores(pieces):
        return [swap_cores(piece) for piece in pieces]

    pack_qkv = jnp.concatenate(
        [w_qkv[0], w_qkv[1], w_qkv[2], jnp.pad(gain_attn[:, None], ((0, 0), (0, LANES - 1)))],
        axis=1,
    )
    out_t, down_t = w_out.T, w_down.T
    pack_ffn = jnp.concatenate(
        [
            w_in[:, 0, :main],
            w_in[:, 1, :main],
            w_in[:, 0, main:],
            w_in[:, 1, main:],
            out_t,
            down_t,
            jnp.pad(gain_ffn[:, None], ((0, 0), (0, tail - 1))),
        ],
        axis=1,
    )
    total_qkv, total_ffn = pack_qkv.shape[1], pack_ffn.shape[1]
    cut = total_ffn * 9 // 25 // LANES * LANES
    if fast:
        own_qkv = plane(stack(across_z(pack_qkv)))
        other_qkv = both_cores(own_qkv)
        pack_c, pack_f = pack_ffn[:, :cut], pack_ffn[:, cut:]
        came_x, came_y = exchange(pack_c, X), exchange(pack_c, Y)
        stack_c = stack([pack_c, came_x, came_y, exchange(came_y, X)])
        own_c = across_z(stack_c)
        own_f = plane(stack(across_z(pack_f)))
        own_ffn = own_c + own_f
        other_ffn = both_cores(own_c) + both_cores(own_f)
        layout_qkv = [(d, 0, total_qkv) for d in PLANE_PIECES]
        layout_ffn = [(d, 0, cut) for d in LINE_PIECES]
        layout_ffn += [(d, cut, total_ffn) for d in PLANE_PIECES]
    else:
        own_qkv = [lax.all_gather(pack_qkv, "dp", axis=0, tiled=True)]
        own_ffn = [lax.all_gather(pack_ffn, "dp", axis=0, tiled=True)]
        other_qkv, other_ffn = both_cores(own_qkv), both_cores(own_ffn)
        layout_qkv, layout_ffn = [(None, 0, total_qkv)], [(None, 0, total_ffn)]

    seg = lax.dynamic_slice_in_dim(segments, core, 1, axis=0)
    length = lax.dynamic_slice_in_dim(lengths, core, 1, axis=0)
    live = ((jnp.arange(seq, dtype=jnp.int32) < length) & (core < counts[0])).astype(F32)
    seg_row, seg_col = seg, seg.reshape(seq, 1)
    live_row, live_col = live.reshape(1, seq), live.reshape(seq, 1)
    earlier = jnp.sum((seg_row < seg_col).astype(jnp.int32), axis=1)
    position = (jnp.arange(seq, dtype=jnp.int32) - earlier).astype(F32)
    frequency = jnp.power(F32(THETA_BASE), -(jnp.arange(HD // 2, dtype=F32) * (2.0 / HD)))
    angle = position[:, None] * frequency[None, :]
    cosine, sine = jnp.cos(angle), jnp.sin(angle)
    repeats = LANES // HD
    cosine = jnp.concatenate([cosine, cosine] * repeats, axis=1)
    sine = jnp.concatenate([-sine, sine] * repeats, axis=1)
    grad_mixed = (live_col * cotangent.astype(F32)).astype(BF16)
    their_mixed = swap_cores(grad_mixed)
    me_vec = me.astype(jnp.int32).reshape(1)

    cfg = dict(half=half, rows=rows, layout=layout_qkv, units=units, main=main, model=model)
    width = 2 * half
    w_full, qkv, att, far, logt, n1, gain1 = call(
        functools.partial(attn_forward_kernel, cfg, len(own_qkv)),
        [me_vec, inputs, *own_qkv, *other_qkv, seg_row, seg_col, live_row, cosine, sine],
        [
            shape(model, 3 * width),
            shape(tokens, 3 * width),
            shape(tokens, width),
            shape(tokens, half),
            shape(tokens, LANES, dtype=F32),
            shape(tokens, model),
            shape(8, model, dtype=F32),
        ],
        [pltpu.VMEM((model, LANES), BF16)],
        flops=2 * tokens * model * 3 * width,
        spare=6 << 20,
    )
    their_far = swap_cores(far)
    ffn_cfg = dict(cfg, layout=layout_ffn)
    side = 2 * units + main + LANES
    output, hidden, gain2, wo_full, win_full, wgate_full, gi, gg, swap_b, keep1 = call(
        functools.partial(ffn_kernel, ffn_cfg, len(own_ffn)),
        [me_vec, inputs, att, grad_mixed, live_col, *own_ffn, *other_ffn],
        [
            shape(tokens, model),
            shape(tokens, model, dtype=F32),
            shape(8, model, dtype=F32),
            shape(model, width),
            shape(model, 2 * units),
            shape(model, 2 * units),
            shape(tokens, 2 * units),
            shape(tokens, 2 * units),
            shape(tokens, model + side),
            shape(tokens, side),
        ],
        [pltpu.VMEM((model, 2 * units), BF16), pltpu.VMEM((model, LANES), BF16)],
        flops=2 * tokens * model * 8 * units,
        spare=6 << 20,
    )
    their_b = swap_cores(swap_b)
    grad_hidden, swap_h = call(
        ffn_backward_kernel,
        [hidden, grad_mixed, gain2, win_full, wgate_full, gi, gg],
        [shape(tokens, model, dtype=F32), shape(tokens + 16, model)],
        [],
        scalars=0,
        flops=2 * tokens * model * 4 * units,
        spare=6 << 20,
    )
    their_h = swap_cores(swap_h)

    def grads(sections, operands, cfg):
        total = cfg["total"]
        outs = [shape(model, total, dtype=F32)]
        if fast:
            outs = [shape(8, rows, last - first) for _, (first, last) in cfg["emit"] for _ in "ks"]
        return call(
            functools.partial(grads_kernel, cfg, sections, len(operands), fast),
            [me_vec, *operands],
            outs,
            [pltpu.VMEM((model, total), F32)],
            flops=4 * tokens * model * total,
            spare=6 << 20,
        )

    total1 = 2 * units + half + main + LANES
    sections1 = [
        ((((0, 0), (1, 0)), ((2, 0), (2, model))), 0, 2 * units),
        ((((3, 0), (4, 0)), ((5, 0), (6, 0))), 2 * units, half),
        (
            (((7, 0), (1, 2 * units)), ((8, 0), (2, model + 2 * units))),
            2 * units + half,
            main + LANES,
        ),
    ]
    operands1 = [
        swap_b, keep1, their_b, swap_h, att, their_h, their_far, grad_mixed, their_mixed,
    ]
    cut1 = total1 * 9 // 25 // LANES * LANES
    mid = cut1 + (total1 - cut1) // 2 // LANES * LANES
    emit1 = [(GRAD_C, (0, cut1)), (GRAD_A, (cut1, mid)), (GRAD_B, (mid, total1))]
    cfg1 = dict(
        ffn_cfg, tokens=tokens, total=total1, gain_lane=tail, emit=emit1, gain_from=(3, 5)
    )
    pieces1 = grads(sections1, operands1, cfg1)
    grad_inputs, swap2, keep2 = call(
        functools.partial(attn_backward_kernel, cfg),
        [
            inputs, grad_hidden, wo_full, w_full, qkv, att, logt, gain1,
            seg_row, seg_col, live_row, cosine, sine, n1,
        ],
        [
            shape(tokens, model, dtype=F32),
            shape(tokens + 16, model + 3 * half),
            shape(tokens, 3 * half),
        ],
        [pltpu.VMEM((tokens, width), BF16), pltpu.VMEM((tokens, 3 * width), BF16)],
        scalars=0,
        flops=2 * tokens * model * 5 * width,
        spare=6 << 20,
    )
    total2 = 3 * half + LANES
    emit2 = [(GRAD_A, (0, total2 // 2)), (GRAD_B, (total2 // 2, total2))]
    cfg2 = dict(cfg, tokens=tokens, total=total2, gain_lane=0, emit=emit2, gain_from=(0, 2))
    sections2 = [((((0, 0), (1, 0)), ((2, 0), (2, model))), 0, 3 * half)]
    operands2 = [swap2, keep2, swap_cores(swap2)]
    pieces2 = grads(sections2, operands2, cfg2)

    if fast:
        keep_c, send_c, keep_a, send_a, keep_b, send_b = pieces1
        keep_a, send_a, keep_b, send_b = combine(
            False, keep_a, exchange(send_a, X), keep_b, exchange(send_b, Y)
        )
        keep_c, send_c = combine(False, keep_c, exchange(send_c, Z))
        keep_c, send_c = combine(False, keep_c, exchange(send_c, ZZ))
        keep, send = combine(True, keep_a, exchange(send_a, Y), keep_b, exchange(send_b, X))
        keep_c, send_c = combine(False, keep_c, exchange(send_c, X))
        keep, send = combine(False, keep, exchange(send, Z))
        came_c, came = exchange(send_c, Y), exchange(send, ZZ)
        share1 = call(
            final_ffn_kernel,
            [keep_c, came_c, keep, came],
            [shape(rows, total1, dtype=F32)],
            [],
            scalars=0,
        )[0]
        keep_a, send_a, keep_b, send_b = pieces2
        keep_a, send_a, keep_b, send_b = combine(
            False, keep_a, exchange(send_a, X), keep_b, exchange(send_b, Y)
        )
        keep, send = combine(True, keep_a, exchange(send_a, Y), keep_b, exchange(send_b, X))
        keep, send = combine(False, keep, exchange(send, Z))
        grad_qkv, gain1_share = call(
            final_qkv_kernel,
            [keep, exchange(send, ZZ)],
            [shape(3, rows, half, dtype=F32), shape(rows, LANES, dtype=F32)],
            [],
            scalars=0,
        )
        grad_gain1 = gain1_share[:, 0]
    else:
        share1, share2 = (
            lax.psum_scatter(pieces[0], "dp", scatter_dimension=0, tiled=True)
            for pieces in (pieces1, pieces2)
        )
        grad_qkv = jnp.stack([share2[:, c * half : (c + 1) * half] for c in range(3)])
        grad_gain1 = share2[:, 3 * half]
    heads = share1[:, : 2 * main].reshape(rows, 2, main)
    tails = share1[:, 2 * main : 2 * units].reshape(rows, 2, tail)
    grad_in = jnp.concatenate([heads, tails], axis=2)
    grad_out = share1[:, 2 * units : 2 * units + half].T
    grad_down = share1[:, 2 * units + half : 2 * units + half + units].T
    grad_gain2 = share1[:, 2 * units + half + units]
    return (
        output,
        grad_inputs,
        grad_gain1,
        grad_qkv,
        grad_out,
        grad_gain2,
        grad_in,
        grad_down,
    )


def fast_path(dp):
    return dp == 16


def solution(mesh):
    in_specs = (
        P(("dp", "tensor"), None),
        P("dp"),
        P(None, "dp", "tensor"),
        P("tensor", "dp"),
        P("dp"),
        P("dp", None, "tensor"),
        P("tensor", "dp"),
        P(("dp", "tensor"), None),
        P("dp", None),
        P("dp"),
        P("dp"),
    )
    out_specs = (
        P(("dp", "tensor"), None),
        P(("dp", "tensor"), None),
        P("dp"),
        P(None, "dp", "tensor"),
        P("tensor", "dp"),
        P("dp"),
        P("dp", None, "tensor"),
        P("tensor", "dp"),
    )

    return jax.shard_map(shards, mesh=mesh, in_specs=in_specs, out_specs=out_specs, check_vma=False)
```

```python
import functools
import math

import jax
import jax.numpy as jnp
from jax import lax
from jax.experimental import pallas as pl
from jax.experimental.pallas import tpu as pltpu
from jax.sharding import PartitionSpec as P


HD = 64
LANES = 128

THETA_BASE = 160000.0
EPSILON = 1e-05
SQRT_HALF = 0.7071067811865476
INV_ROOT_TWO_PI = 0.3989422804014327
MASKED_SCORE = -1e30

F32 = jnp.float32
BF16 = jnp.bfloat16


NN = (((1,), (0,)), ((), ()))
NT = (((1,), (1,)), ((), ()))
TN = (((0,), (0,)), ((), ()))

X, Y, Z, ZZ = 1, 2, 4, 8
Z_ALL = (0, Z, ZZ, Z | ZZ)
Z_HALVES = (0, ZZ, Z, Z | ZZ)
XY_ALL = (0, X, Y, X | Y)
XY_HALVES = (0, Y, X, X | Y)


def shift(distances, by):
    return tuple(d ^ by for d in distances)


PLANE_PIECES = (Z_ALL, shift(Z_ALL, X), shift(Z_ALL, Y), (3, 7), (11, 15))
LINE_PIECES = tuple(shift(XY_ALL, z) for z in Z_ALL)

GRAD_A = (tuple(y + z for y in (0, Y) for z in Z_HALVES), X)
GRAD_B = (tuple(x + z for x in (0, X) for z in Z_HALVES), Y)
GRAD_C = (tuple(z + xy for z in (0, ZZ) for xy in XY_HALVES), Z)


def mm(left, right, dims):
    return lax.dot_general(left, right, dims, preferred_element_type=F32)


def norm_parts(rows_in):
    centre = rows_in - jnp.mean(rows_in, axis=-1, keepdims=True)
    inv_std = lax.rsqrt(jnp.mean(centre * centre, axis=-1, keepdims=True) + EPSILON)
    return centre * inv_std, inv_std


def norm_back(grad_normed, normed, inv_std, gain_row):
    scaled = grad_normed * gain_row
    inner_mean = jnp.mean(scaled * normed, axis=-1, keepdims=True)
    grad_rows = inv_std * (scaled - jnp.mean(scaled, axis=-1, keepdims=True) - normed * inner_mean)
    return grad_rows, jnp.sum(grad_normed * normed, axis=0, keepdims=True)


def lane_index(shape):
    return lax.broadcasted_iota(jnp.int32, shape, 1)


def swap_halves(chunk):
    half = HD // 2
    return jnp.where(
        lane_index(chunk.shape) % HD < half,
        pltpu.roll(chunk, LANES - half, 1),
        pltpu.roll(chunk, half, 1),
    )


def column_to_row(columns, lane):
    pick = (lane_index((8, LANES)) == lane).astype(BF16)
    return mm(pick, columns, NT)[0:1]


def row_to_columns(row):
    return jnp.transpose(jnp.broadcast_to(row, (LANES, row.shape[1])), (1, 0))


class Pieces:
    def __init__(self, me, refs, rows, layout):
        self.me, self.refs, self.rows, self.layout = me, refs, rows, layout

    def copy(self, dst, dst_col, src_col, width):
        for ref, (distances, first, last) in zip(self.refs, self.layout):
            low, high = max(first, src_col), min(last, src_col + width)
            if low >= high:
                continue
            at = slice(dst_col + low - src_col, dst_col + high - src_col)
            cols = slice(low - first, high - first)
            if distances is None:
                dst[:, at] = ref[:, cols]
                continue
            for i, distance in enumerate(distances):
                base = pl.multiple_of((self.me ^ distance) * self.rows, self.rows)
                dst[pl.ds(base, self.rows), at] = ref[i, :, cols]


def attn_mask(seg_row, seg_col, live_row):
    same = seg_col == seg_row
    shape = same.shape
    diagonal = lax.broadcasted_iota(jnp.int32, shape, 0) == lane_index(shape)
    return (same & (live_row > 0)) | diagonal


def attn_forward_kernel(cfg, n_pieces, *refs):
    me_ref, x_ref = refs[:2]
    own = refs[2 : 2 + n_pieces]
    other = refs[2 + n_pieces : 2 + 2 * n_pieces]
    seg_row, seg_col, live_row, cos_ref, sin_ref = refs[2 + 2 * n_pieces : 7 + 2 * n_pieces]
    w_ref, qkv_ref, att_ref, far_ref, logt_ref, n1_ref = refs[7 + 2 * n_pieces :]
    me = me_ref[0]
    half, width = cfg["half"], 2 * cfg["half"]
    for which, pieces in enumerate((own, other)):
        part = Pieces(me, pieces, cfg["rows"], cfg["layout"])
        for c in range(3):
            part.copy(w_ref, c * width + which * half, c * half, half)
    normed, _ = norm_parts(x_ref[...].astype(F32))
    n1 = normed.astype(BF16)
    n1_ref[...] = n1
    cosine, sine = cos_ref[...], sin_ref[...]
    step = 2 * LANES
    for at in range(0, 3 * width, step):
        product = mm(n1, w_ref[:, at : at + step], NN)
        for sub in range(0, step, LANES):
            chunk = product[:, sub : sub + LANES]
            if at < 2 * width:
                chunk = chunk * cosine + swap_halves(chunk) * sine
            qkv_ref[:, at + sub : at + sub + LANES] = chunk.astype(BF16)
    mask = attn_mask(seg_row[...], seg_col[...], live_row[...])
    scale = HD ** (-0.5)
    rows = x_ref.shape[0]
    low = lane_index((rows, LANES)) < HD
    lanes = lane_index((rows, LANES))
    totals = jnp.zeros((rows, LANES), F32)
    for pair in range(width // LANES):
        at = pair * LANES
        queries = qkv_ref[:, at : at + LANES]
        keys = qkv_ref[:, width + at : width + at + LANES]
        values = qkv_ref[:, 2 * width + at : 2 * width + at + LANES]
        outs = []
        for side in range(2):
            picked = jnp.where(low if side == 0 else ~low, queries, jnp.zeros_like(queries))
            scores = jnp.where(mask, mm(picked, keys, NT) * scale, MASKED_SCORE)
            row_max = jnp.max(scores, axis=-1, keepdims=True)
            weights = jnp.exp(scores - row_max)
            total = jnp.sum(weights, axis=-1, keepdims=True)
            prob = (weights * (1.0 / total)).astype(BF16)
            outs.append(mm(prob, values, NN))
            totals = jnp.where(lanes == 2 * pair + side, row_max + jnp.log(total), totals)
        attended = jnp.where(low, outs[0], outs[1]).astype(BF16)
        att_ref[:, at : at + LANES] = attended
        if at >= half:
            far_ref[:, at - half : at - half + LANES] = attended
    logt_ref[...] = totals


def ffn_kernel(cfg, n_pieces, *refs):
    me_ref, x_ref, att_ref, gm_ref, live_ref = refs[:5]
    own = refs[5 : 5 + n_pieces]
    other = refs[5 + n_pieces : 5 + 2 * n_pieces]
    rest = refs[5 + 2 * n_pieces :]
    out_ref, hidden_ref, gain_ref, wo_ref, win_ref, wgate_ref, gi_ref, gg_ref = rest[:8]
    swap_ref, keep_ref, wdown_ref, gcol = rest[8:]
    me = me_ref[0]
    half, units, main = cfg["half"], cfg["units"], cfg["main"]
    tail = units - main
    rows, model = x_ref.shape
    out_at = 2 * units
    for which, pieces in enumerate((own, other)):
        part = Pieces(me, pieces, cfg["rows"], cfg["layout"])
        part.copy(win_ref, which * main, 0, main)
        part.copy(wgate_ref, which * main, main, main)
        part.copy(win_ref, 2 * main + which * tail, 2 * main, tail)
        part.copy(wgate_ref, 2 * main + which * tail, 2 * main + tail, tail)
        part.copy(wo_ref, which * half, out_at, half)
        part.copy(wdown_ref, which * main, out_at + half, main)
        part.copy(wdown_ref, 2 * main + which * tail, out_at + half + main, tail)
        if which == 0:
            part.copy(gcol, 0, out_at + half + main, LANES)
    gain_row = column_to_row(gcol[...], tail)
    gain_ref[...] = jnp.broadcast_to(gain_row, gain_ref.shape)
    hidden = x_ref[...].astype(F32) + mm(att_ref[...], wo_ref[...], NT)
    hidden_ref[...] = hidden
    n2 = (norm_parts(hidden)[0] * gain_row).astype(BF16)
    swap_ref[:, 0:model] = n2
    grad_mixed = gm_ref[...]
    step = 3 * LANES
    mixed = hidden
    for at in range(0, 2 * units, step):
        unit_in = mm(n2, win_ref[:, at : at + step], NN)
        unit_gate = mm(n2, wgate_ref[:, at : at + step], NN)
        grad_act = mm(grad_mixed, wdown_ref[:, at : at + step], NN)
        cdf = 0.5 * (1.0 + lax.erf(unit_in * SQRT_HALF))
        gelu = unit_in * cdf
        slope = cdf + unit_in * INV_ROOT_TWO_PI * jnp.exp(-0.5 * unit_in * unit_in)
        activated = (gelu * unit_gate).astype(BF16)
        grad_in = (grad_act * unit_gate * slope).astype(BF16)
        grad_gate = (grad_act * gelu).astype(BF16)
        gi_ref[:, at : at + step] = grad_in
        gg_ref[:, at : at + step] = grad_gate
        mixed = mixed + mm(activated, wdown_ref[:, at : at + step], NT)
        for sub in range(0, step, LANES):
            lo = at + sub
            a, gi, gg = (v[:, sub : sub + LANES] for v in (activated, grad_in, grad_gate))
            if lo < 2 * main:
                which, col = divmod(lo, main)
                ref, off = (keep_ref, 0) if which == 0 else (swap_ref, model)
                for value, start in ((gi, 0), (gg, main), (a, 2 * units)):
                    ref[:, off + start + col : off + start + col + LANES] = value
            else:
                low = lane_index((rows, LANES)) < tail
                gi, gg, a = gi.astype(F32), gg.astype(F32), a.astype(F32)
                mine = jnp.where(low, gi, pltpu.roll(gg, tail, 1))
                theirs = jnp.where(low, pltpu.roll(gi, tail, 1), gg)
                for start, here, there in (
                    (2 * main, mine, theirs),
                    (2 * units + main, a, pltpu.roll(a, tail, 1)),
                ):
                    keep_ref[:, start : start + LANES] = here.astype(BF16)
                    start += model
                    swap_ref[:, start : start + LANES] = there.astype(BF16)
    out_ref[...] = (live_ref[...] * mixed).astype(BF16)


def ffn_backward_kernel(hidden_ref, gm_ref, gain_ref, win_ref, wgate_ref, gi_ref, gg_ref, *outs):
    gh_ref, swap_ref = outs
    rows, _ = hidden_ref.shape
    grad_normed = mm(gi_ref[...], win_ref[...], NT) + mm(gg_ref[...], wgate_ref[...], NT)
    normed, inv_std = norm_parts(hidden_ref[...])
    grad_rows, gain_term = norm_back(grad_normed, normed, inv_std, gain_ref[0:1])
    grad_hidden = gm_ref[...].astype(F32) + grad_rows
    gh_ref[...] = grad_hidden
    swap_ref[0:rows, :] = grad_hidden.astype(BF16)
    put_gain(swap_ref, gain_term, rows)


def put_gain(ref, gain_term, rows):
    model = gain_term.shape[1]
    extra = ref.shape[0] - rows
    high = gain_term.astype(BF16).astype(F32)
    first = lax.broadcasted_iota(jnp.int32, (extra, model), 0)
    block = jnp.where(first == 0, high, jnp.where(first == 1, gain_term - high, 0.0))
    ref[rows:, 0:model] = block.astype(BF16)
    if ref.shape[1] > model:
        ref[rows:, model:] = jnp.zeros((extra, ref.shape[1] - model), BF16)


def attn_backward_kernel(cfg, *refs):
    (x_ref, gh_ref, wo_ref, w_ref, qkv_ref, att_ref, logt_ref) = refs[:7]
    seg_row, seg_col, live_row, cos_ref, sin_ref, n1_ref = refs[7:13]
    gin_ref, swap_ref, keep_ref, gatt_ref, gqkv_ref = refs[13:]
    half, width = cfg["half"], 2 * cfg["half"]
    rows, model = x_ref.shape
    gatt_ref[...] = mm(gh_ref[...].astype(BF16), wo_ref[...], NN).astype(BF16)
    mask = attn_mask(seg_row[...], seg_col[...], live_row[...])
    scale = HD ** (-0.5)
    low = lane_index((rows, LANES)) < HD
    cosine, sine = cos_ref[...], sin_ref[...]
    for pair in range(width // LANES):
        at = pair * LANES
        queries = qkv_ref[:, at : at + LANES]
        keys = qkv_ref[:, width + at : width + at + LANES]
        values = qkv_ref[:, 2 * width + at : 2 * width + at + LANES]
        grad_att = gatt_ref[:, at : at + LANES]
        products = grad_att.astype(F32) * att_ref[:, at : at + LANES].astype(F32)
        grads_q, grad_k, grad_v = [], 0.0, 0.0
        for side in range(2):
            on = low if side == 0 else ~low
            q_side = jnp.where(on, queries, jnp.zeros_like(queries))
            g_side = jnp.where(on, grad_att, jnp.zeros_like(grad_att))
            head = 2 * pair + side
            scores = jnp.where(mask, mm(q_side, keys, NT) * scale, MASKED_SCORE)
            prob = jnp.exp(scores - logt_ref[:, head : head + 1])
            row_inner = jnp.sum(jnp.where(on, products, 0.0), axis=-1, keepdims=True)
            grad_prob = mm(g_side, values, NT)
            grad_scores = (prob * (grad_prob - row_inner)).astype(BF16)
            grad_v = grad_v + mm(prob.astype(BF16), g_side, TN)
            grads_q.append(mm(grad_scores, keys, NN))
            grad_k = grad_k + mm(grad_scores, q_side, TN)
        grad_q = jnp.where(low, grads_q[0], grads_q[1]) * scale
        grad_k = grad_k * scale
        grad_q = grad_q * cosine - swap_halves(grad_q) * sine
        grad_k = grad_k * cosine - swap_halves(grad_k) * sine
        for c, value in enumerate((grad_q, grad_k, grad_v)):
            value = value.astype(BF16)
            gqkv_ref[:, c * width + at : c * width + at + LANES] = value
            if at < half:
                keep_ref[0:rows, c * half + at : c * half + at + LANES] = value
            else:
                col = model + c * half + at - half
                swap_ref[0:rows, col : col + LANES] = value
    swap_ref[0:rows, 0:model] = n1_ref[...]
    scaled = mm(gqkv_ref[...], w_ref[...], NT)
    normed, inv_std = norm_parts(x_ref[...].astype(F32))
    grad_rows, gain_term = norm_back(scaled, normed, inv_std, 1.0)
    gin_ref[...] = gh_ref[...] + grad_rows
    put_gain(swap_ref, gain_term, rows)


def grads_kernel(cfg, sections, n_in, fast, me_ref, *refs):
    ins, outs, grad_ref = refs[:n_in], refs[n_in:-1], refs[-1]
    model = cfg["model"]
    tokens = cfg["tokens"]
    for pairs, at, size in sections:
        total = 0.0
        for (left, left_at), (right, right_at) in pairs:
            total = total + mm(
                ins[left][0:tokens, left_at : left_at + model],
                ins[right][0:tokens, right_at : right_at + size],
                TN,
            )
        grad_ref[:, at : at + size] = total
    gain = jnp.zeros((1, model), F32)
    for which in cfg["gain_from"]:
        block = ins[which][tokens:, 0:model].astype(F32)
        gain = gain + block[0:1] + block[1:2]
    columns = row_to_columns(gain)
    total = grad_ref.shape[1]
    last = slice(total - LANES, total)
    if cfg["gain_lane"]:
        keep_low = lane_index(columns.shape) < cfg["gain_lane"]
        columns = jnp.where(keep_low, grad_ref[:, last], columns)
    grad_ref[:, last] = columns
    if not fast:
        outs[0][...] = grad_ref[...]
        return
    me, rows = me_ref[0], cfg["rows"]
    at = 0
    for (order, bit), (first, last) in cfg["emit"]:
        for which in (0, 1):
            for i, distance in enumerate(order):
                start = pl.multiple_of((me ^ distance ^ (bit * which)) * rows, rows)
                outs[at + which][i] = grad_ref[pl.ds(start, rows), first:last].astype(BF16)
        at += 2


def stack_kernel(*refs):
    for i, ref in enumerate(refs[:-1]):
        refs[-1][i] = ref[...]


def take_kernel(first, source, taken):
    for i in range(taken.shape[0]):
        taken[i] = source[first + i]


def combine_kernel(joined, *refs):
    n = (len(refs) - 2) // 2 if joined else len(refs) // 4
    ins, outs = refs[: 2 * n], refs[2 * n :]
    at = 0
    for i in range(n):
        kept, came = ins[2 * i], ins[2 * i + 1]
        blocks, _, cols = kept.shape
        keep, send = (outs[0], outs[1]) if joined else (outs[2 * i], outs[2 * i + 1])
        for j in range(blocks):
            total = kept[j].astype(F32) + came[j].astype(F32)
            ref, k = (keep, j) if j < blocks // 2 else (send, j - blocks // 2)
            ref[k, :, at : at + cols] = total.astype(ref.dtype)
        at += cols if joined else 0


def final_ffn_kernel(kept_c, came_c, kept_ab, came_ab, share):
    cut = kept_c.shape[2]
    share[:, :cut] = kept_c[0] + came_c[0].astype(F32)
    share[:, cut:] = kept_ab[0] + came_ab[0].astype(F32)


def final_qkv_kernel(kept, came, gain_ref, grad, gain_grad):
    half = grad.shape[2]
    gain = gain_ref[...]
    for c in range(3):
        cols = slice(c * half, (c + 1) * half)
        grad[c] = (kept[0, :, cols] + came[0, :, cols].astype(F32)) * gain
    gain_grad[...] = (kept[0, :, 3 * half :] + came[0, :, 3 * half :].astype(F32)) / gain


VMEM = pl.BlockSpec(memory_space=pltpu.VMEM)
SMEM = pl.BlockSpec(memory_space=pltpu.SMEM)


def call(kernel, operands, outs, scratch, scalars=1, flops=0, spare=1 << 20):
    moved = sum(o.size * o.dtype.itemsize for o in operands)
    moved += sum(s.size * s.dtype.itemsize for s in outs)
    held = sum(math.prod(s.shape) * jnp.dtype(s.dtype).itemsize for s in scratch)
    return pl.pallas_call(
        kernel,
        out_shape=outs,
        in_specs=[SMEM] * scalars + [VMEM] * (len(operands) - scalars),
        out_specs=[VMEM] * len(outs),
        scratch_shapes=scratch,
        cost_estimate=pl.CostEstimate(flops=flops, bytes_accessed=moved, transcendentals=0),
        compiler_params=pltpu.CompilerParams(vmem_limit_bytes=moved + held + spare),
    )(*operands)


def shape(*dims, dtype=BF16):
    return jax.ShapeDtypeStruct(dims, dtype)


def stack(planes):
    outs = [shape(len(planes), *planes[0].shape)]
    return call(stack_kernel, list(planes), outs, [], scalars=0)[0]


def take(source, first, count):
    kernel = functools.partial(take_kernel, first)
    outs = [shape(count, *source.shape[1:])]
    return call(kernel, [source], outs, [], scalars=0)[0]


def combine(joined, *arrays):
    outs = []
    for kept in arrays[::2]:
        blocks, rows, cols = kept.shape
        outs += [shape(blocks // 2, rows, cols, dtype=F32), shape(blocks // 2, rows, cols)]
    if joined:
        blocks, rows = outs[0].shape[:2]
        cols = sum(o.shape[2] for o in outs[::2])
        outs = [shape(blocks, rows, cols, dtype=F32), shape(blocks, rows, cols)]
    kernel = functools.partial(combine_kernel, joined)
    return call(kernel, list(arrays), outs, [], scalars=0)


def shards(
    inputs, gain_attn, w_qkv, w_out, gain_ffn, w_in, w_down, cotangent, segments, lengths, counts
):
    dp, cores = lax.axis_size("dp"), lax.axis_size("tensor")
    me, core = lax.axis_index("dp"), lax.axis_index("tensor")
    seq = segments.shape[1]
    tokens, model = inputs.shape
    rows, half, units = gain_attn.shape[0], w_qkv.shape[2], w_in.shape[2]
    main = units // LANES * LANES
    tail = units - main
    if cores != 2 or tokens != seq or segments.shape[0] != cores or 2 * tail != LANES:
        raise ValueError("unsupported shapes")
    fast = fast_path(dp) and rows % 16 == 0

    def swap_cores(value):
        return lax.ppermute(value, "tensor", [(0, 1), (1, 0)])

    def exchange(value, distance):
        pairs = [(i, i ^ distance) for i in range(dp)]
        return lax.ppermute(value, "dp", pairs)

    def across_z(value):
        return [value] + [exchange(value, z) for z in Z_ALL[1:]]

    def plane(stacked):
        came_x = exchange(stacked, X)
        came_y = exchange(stacked, Y)
        far_a = exchange(take(came_y, 0, 2), X)
        far_b = exchange(take(came_x, 2, 2), Y)
        return [stacked, came_x, came_y, far_a, far_b]

    def both_cores(pieces):
        return [swap_cores(piece) for piece in pieces]

    gain_col = gain_attn.astype(F32)[:, None]
    pack_qkv = jnp.concatenate(
        [(w_qkv[c].astype(F32) * gain_col).astype(BF16) for c in range(3)], axis=1
    )
    out_t, down_t = w_out.T, w_down.T
    pack_ffn = jnp.concatenate(
        [
            w_in[:, 0, :main],
            w_in[:, 1, :main],
            w_in[:, 0, main:],
            w_in[:, 1, main:],
            out_t,
            down_t,
            jnp.pad(gain_ffn[:, None], ((0, 0), (0, tail - 1))),
        ],
        axis=1,
    )
    total_qkv, total_ffn = pack_qkv.shape[1], pack_ffn.shape[1]
    cut = total_ffn * 3 // 10 // LANES * LANES
    if fast:
        own_qkv = plane(stack(across_z(pack_qkv)))
        other_qkv = both_cores(own_qkv)
        pack_c, pack_f = pack_ffn[:, :cut], pack_ffn[:, cut:]
        came_x, came_y = exchange(pack_c, X), exchange(pack_c, Y)
        stack_c = stack([pack_c, came_x, came_y, exchange(came_y, X)])
        own_c = across_z(stack_c)
        own_f = plane(stack(across_z(pack_f)))
        own_ffn = own_c + own_f
        other_ffn = both_cores(own_c) + both_cores(own_f)
        layout_qkv = [(d, 0, total_qkv) for d in PLANE_PIECES]
        layout_ffn = [(d, 0, cut) for d in LINE_PIECES]
        layout_ffn += [(d, cut, total_ffn) for d in PLANE_PIECES]
    else:
        own_qkv = [lax.all_gather(pack_qkv, "dp", axis=0, tiled=True)]
        own_ffn = [lax.all_gather(pack_ffn, "dp", axis=0, tiled=True)]
        other_qkv, other_ffn = both_cores(own_qkv), both_cores(own_ffn)
        layout_qkv, layout_ffn = [(None, 0, total_qkv)], [(None, 0, total_ffn)]

    seg = lax.dynamic_slice_in_dim(segments, core, 1, axis=0)
    length = lax.dynamic_slice_in_dim(lengths, core, 1, axis=0)
    live = ((jnp.arange(seq, dtype=jnp.int32) < length) & (core < counts[0])).astype(F32)
    seg_row, seg_col = seg, seg.reshape(seq, 1)
    live_row, live_col = live.reshape(1, seq), live.reshape(seq, 1)
    earlier = jnp.sum((seg_row < seg_col).astype(jnp.int32), axis=1)
    position = (jnp.arange(seq, dtype=jnp.int32) - earlier).astype(F32)
    frequency = jnp.power(F32(THETA_BASE), -(jnp.arange(HD // 2, dtype=F32) * (2.0 / HD)))
    angle = position[:, None] * frequency[None, :]
    cosine, sine = jnp.cos(angle), jnp.sin(angle)
    repeats = LANES // HD
    cosine = jnp.concatenate([cosine, cosine] * repeats, axis=1)
    sine = jnp.concatenate([-sine, sine] * repeats, axis=1)
    grad_mixed = (live_col * cotangent.astype(F32)).astype(BF16)
    their_mixed = swap_cores(grad_mixed)
    me_vec = me.astype(jnp.int32).reshape(1)

    cfg = dict(half=half, rows=rows, layout=layout_qkv, units=units, main=main, model=model)
    width = 2 * half
    w_full, qkv, att, far, logt, n1 = call(
        functools.partial(attn_forward_kernel, cfg, len(own_qkv)),
        [me_vec, inputs, *own_qkv, *other_qkv, seg_row, seg_col, live_row, cosine, sine],
        [
            shape(model, 3 * width),
            shape(tokens, 3 * width),
            shape(tokens, width),
            shape(tokens, half),
            shape(tokens, LANES, dtype=F32),
            shape(tokens, model),
        ],
        [],
        flops=2 * tokens * model * 3 * width,
        spare=6 << 20,
    )
    their_far = swap_cores(far)
    ffn_cfg = dict(cfg, layout=layout_ffn)
    side = 2 * units + main + LANES
    output, hidden, gain2, wo_full, win_full, wgate_full, gi, gg, swap_b, keep1 = call(
        functools.partial(ffn_kernel, ffn_cfg, len(own_ffn)),
        [me_vec, inputs, att, grad_mixed, live_col, *own_ffn, *other_ffn],
        [
            shape(tokens, model),
            shape(tokens, model, dtype=F32),
            shape(8, model, dtype=F32),
            shape(model, width),
            shape(model, 2 * units),
            shape(model, 2 * units),
            shape(tokens, 2 * units),
            shape(tokens, 2 * units),
            shape(tokens, model + side),
            shape(tokens, side),
        ],
        [pltpu.VMEM((model, 2 * units), BF16), pltpu.VMEM((model, LANES), BF16)],
        flops=2 * tokens * model * 8 * units,
        spare=6 << 20,
    )
    their_b = swap_cores(swap_b)
    grad_hidden, swap_h = call(
        ffn_backward_kernel,
        [hidden, grad_mixed, gain2, win_full, wgate_full, gi, gg],
        [shape(tokens, model, dtype=F32), shape(tokens + 16, model)],
        [],
        scalars=0,
        flops=2 * tokens * model * 4 * units,
        spare=6 << 20,
    )
    their_h = swap_cores(swap_h)

    def grads(sections, operands, cfg):
        total = cfg["total"]
        outs = [shape(model, total, dtype=F32)]
        if fast:
            outs = [shape(8, rows, last - first) for _, (first, last) in cfg["emit"] for _ in "ks"]
        return call(
            functools.partial(grads_kernel, cfg, sections, len(operands), fast),
            [me_vec, *operands],
            outs,
            [pltpu.VMEM((model, total), F32)],
            flops=4 * tokens * model * total,
            spare=6 << 20,
        )

    total1 = 2 * units + half + main + LANES
    sections1 = [
        ((((0, 0), (1, 0)), ((2, 0), (2, model))), 0, 2 * units),
        ((((3, 0), (4, 0)), ((5, 0), (6, 0))), 2 * units, half),
        (
            (((7, 0), (1, 2 * units)), ((8, 0), (2, model + 2 * units))),
            2 * units + half,
            main + LANES,
        ),
    ]
    operands1 = [
        swap_b, keep1, their_b, swap_h, att, their_h, their_far, grad_mixed, their_mixed,
    ]
    cut1 = total1 * 21 // 50 // LANES * LANES
    mid = cut1 + (total1 - cut1) // 2 // LANES * LANES
    emit1 = [(GRAD_C, (0, cut1)), (GRAD_A, (cut1, mid)), (GRAD_B, (mid, total1))]
    cfg1 = dict(
        ffn_cfg, tokens=tokens, total=total1, gain_lane=tail, emit=emit1, gain_from=(3, 5)
    )
    pieces1 = grads(sections1, operands1, cfg1)
    grad_inputs, swap2, keep2 = call(
        functools.partial(attn_backward_kernel, cfg),
        [
            inputs, grad_hidden, wo_full, w_full, qkv, att, logt,
            seg_row, seg_col, live_row, cosine, sine, n1,
        ],
        [
            shape(tokens, model, dtype=F32),
            shape(tokens + 16, model + 3 * half),
            shape(tokens, 3 * half),
        ],
        [pltpu.VMEM((tokens, width), BF16), pltpu.VMEM((tokens, 3 * width), BF16)],
        scalars=0,
        flops=2 * tokens * model * 5 * width,
        spare=6 << 20,
    )
    total2 = 3 * half + LANES
    emit2 = [(GRAD_A, (0, total2 // 2)), (GRAD_B, (total2 // 2, total2))]
    cfg2 = dict(cfg, tokens=tokens, total=total2, gain_lane=0, emit=emit2, gain_from=(0, 2))
    sections2 = [((((0, 0), (1, 0)), ((2, 0), (2, model))), 0, 3 * half)]
    operands2 = [swap2, keep2, swap_cores(swap2)]
    pieces2 = grads(sections2, operands2, cfg2)

    if fast:
        keep_c, send_c, keep_a, send_a, keep_b, send_b = pieces1
        keep_a, send_a, keep_b, send_b = combine(
            False, keep_a, exchange(send_a, X), keep_b, exchange(send_b, Y)
        )
        keep_c, send_c = combine(False, keep_c, exchange(send_c, Z))
        keep_c, send_c = combine(False, keep_c, exchange(send_c, ZZ))
        keep, send = combine(True, keep_a, exchange(send_a, Y), keep_b, exchange(send_b, X))
        keep_c, send_c = combine(False, keep_c, exchange(send_c, X))
        keep, send = combine(False, keep, exchange(send, Z))
        came_c, came = exchange(send_c, Y), exchange(send, ZZ)
        share1 = call(
            final_ffn_kernel,
            [keep_c, came_c, keep, came],
            [shape(rows, total1, dtype=F32)],
            [],
            scalars=0,
        )[0]
        keep_a, send_a, keep_b, send_b = pieces2
        keep_a, send_a, keep_b, send_b = combine(
            False, keep_a, exchange(send_a, X), keep_b, exchange(send_b, Y)
        )
        keep, send = combine(True, keep_a, exchange(send_a, Y), keep_b, exchange(send_b, X))
        keep, send = combine(False, keep, exchange(send, Z))
        grad_qkv, gain1_share = call(
            final_qkv_kernel,
            [keep, exchange(send, ZZ), gain_col],
            [shape(3, rows, half, dtype=F32), shape(rows, LANES, dtype=F32)],
            [],
            scalars=0,
        )
        grad_gain1 = gain1_share[:, 0]
    else:
        share1, share2 = (
            lax.psum_scatter(pieces[0], "dp", scatter_dimension=0, tiled=True)
            for pieces in (pieces1, pieces2)
        )
        grad_qkv = jnp.stack([share2[:, c * half : (c + 1) * half] * gain_col for c in range(3)])
        grad_gain1 = share2[:, 3 * half] / gain_col[:, 0]
    heads = share1[:, : 2 * main].reshape(rows, 2, main)
    tails = share1[:, 2 * main : 2 * units].reshape(rows, 2, tail)
    grad_in = jnp.concatenate([heads, tails], axis=2)
    grad_out = share1[:, 2 * units : 2 * units + half].T
    grad_down = share1[:, 2 * units + half : 2 * units + half + units].T
    grad_gain2 = share1[:, 2 * units + half + units]
    return (
        output,
        grad_inputs,
        grad_gain1,
        grad_qkv,
        grad_out,
        grad_gain2,
        grad_in,
        grad_down,
    )


def fast_path(dp):
    return dp == 16


def solution(mesh):
    in_specs = (
        P(("dp", "tensor"), None),
        P("dp"),
        P(None, "dp", "tensor"),
        P("tensor", "dp"),
        P("dp"),
        P("dp", None, "tensor"),
        P("tensor", "dp"),
        P(("dp", "tensor"), None),
        P("dp", None),
        P("dp"),
        P("dp"),
    )
    out_specs = (
        P(("dp", "tensor"), None),
        P(("dp", "tensor"), None),
        P("dp"),
        P(None, "dp", "tensor"),
        P("tensor", "dp"),
        P("dp"),
        P("dp", None, "tensor"),
        P("tensor", "dp"),
    )

    return jax.shard_map(shards, mesh=mesh, in_specs=in_specs, out_specs=out_specs, check_vma=False)
```

```python
import functools
import math

import jax
import jax.numpy as jnp
from jax import lax
from jax.experimental import pallas as pl
from jax.experimental.pallas import tpu as pltpu
from jax.sharding import PartitionSpec as P


HD = 64
LANES = 128

THETA_BASE = 160000.0
EPSILON = 1e-05
SQRT_HALF = 0.7071067811865476
INV_ROOT_TWO_PI = 0.3989422804014327
MASKED_SCORE = -1e30

F32 = jnp.float32
BF16 = jnp.bfloat16


NN = (((1,), (0,)), ((), ()))
NT = (((1,), (1,)), ((), ()))
TN = (((0,), (0,)), ((), ()))

X, Y, Z, ZZ = 1, 2, 4, 8
Z_ALL = (0, Z, ZZ, Z | ZZ)
Z_HALVES = (0, ZZ, Z, Z | ZZ)
XY_ALL = (0, X, Y, X | Y)
XY_HALVES = (0, Y, X, X | Y)


def shift(distances, by):
    return tuple(d ^ by for d in distances)


PLANE_PIECES = (Z_ALL, shift(Z_ALL, X), shift(Z_ALL, Y), (3, 7), (11, 15))
LINE_PIECES = tuple(shift(XY_ALL, z) for z in Z_ALL)

GRAD_A = (tuple(y + z for y in (0, Y) for z in Z_HALVES), X)
GRAD_B = (tuple(x + z for x in (0, X) for z in Z_HALVES), Y)
GRAD_C = (tuple(z + xy for z in (0, ZZ) for xy in XY_HALVES), Z)


def mm(left, right, dims):
    return lax.dot_general(left, right, dims, preferred_element_type=F32)


def norm_parts(rows_in):
    centre = rows_in - jnp.mean(rows_in, axis=-1, keepdims=True)
    inv_std = lax.rsqrt(jnp.mean(centre * centre, axis=-1, keepdims=True) + EPSILON)
    return centre * inv_std, inv_std


def norm_back(grad_normed, normed, inv_std, gain_row):
    scaled = grad_normed * gain_row
    inner_mean = jnp.mean(scaled * normed, axis=-1, keepdims=True)
    grad_rows = inv_std * (scaled - jnp.mean(scaled, axis=-1, keepdims=True) - normed * inner_mean)
    return grad_rows, jnp.sum(grad_normed * normed, axis=0, keepdims=True)


def lane_index(shape):
    return lax.broadcasted_iota(jnp.int32, shape, 1)


def swap_halves(chunk):
    half = HD // 2
    return jnp.where(
        lane_index(chunk.shape) % HD < half,
        pltpu.roll(chunk, LANES - half, 1),
        pltpu.roll(chunk, half, 1),
    )


def column_to_row(columns, lane):
    pick = (lane_index((8, LANES)) == lane).astype(BF16)
    return mm(pick, columns, NT)[0:1]


def row_to_columns(row):
    return jnp.transpose(jnp.broadcast_to(row, (LANES, row.shape[1])), (1, 0))


class Pieces:
    def __init__(self, me, refs, rows, layout):
        self.me, self.refs, self.rows, self.layout = me, refs, rows, layout

    def copy(self, dst, dst_col, src_col, width):
        for ref, (distances, first, last) in zip(self.refs, self.layout):
            low, high = max(first, src_col), min(last, src_col + width)
            if low >= high:
                continue
            at = slice(dst_col + low - src_col, dst_col + high - src_col)
            cols = slice(low - first, high - first)
            if distances is None:
                dst[:, at] = ref[:, cols]
                continue
            for i, distance in enumerate(distances):
                base = pl.multiple_of((self.me ^ distance) * self.rows, self.rows)
                dst[pl.ds(base, self.rows), at] = ref[i, :, cols]


def attn_mask(seg_row, seg_col, live_row):
    same = seg_col == seg_row
    shape = same.shape
    diagonal = lax.broadcasted_iota(jnp.int32, shape, 0) == lane_index(shape)
    return (same & (live_row > 0)) | diagonal


def attn_forward_kernel(cfg, n_pieces, *refs):
    me_ref, x_ref = refs[:2]
    own = refs[2 : 2 + n_pieces]
    other = refs[2 + n_pieces : 2 + 2 * n_pieces]
    seg_row, seg_col, live_row, cos_ref, sin_ref = refs[2 + 2 * n_pieces : 7 + 2 * n_pieces]
    w_ref, qkv_ref, att_ref, far_ref, logt_ref, n1_ref = refs[7 + 2 * n_pieces :]
    me = me_ref[0]
    half, width = cfg["half"], 2 * cfg["half"]
    for which, pieces in enumerate((own, other)):
        part = Pieces(me, pieces, cfg["rows"], cfg["layout"])
        for c in range(3):
            part.copy(w_ref, c * width + which * half, c * half, half)
    normed, _ = norm_parts(x_ref[...].astype(F32))
    n1 = normed.astype(BF16)
    n1_ref[...] = n1
    cosine, sine = cos_ref[...], sin_ref[...]
    step = 2 * LANES
    for at in range(0, 3 * width, step):
        product = mm(n1, w_ref[:, at : at + step], NN)
        for sub in range(0, step, LANES):
            chunk = product[:, sub : sub + LANES]
            if at < 2 * width:
                chunk = chunk * cosine + swap_halves(chunk) * sine
            qkv_ref[:, at + sub : at + sub + LANES] = chunk.astype(BF16)
    mask = attn_mask(seg_row[...], seg_col[...], live_row[...])
    scale = HD ** (-0.5)
    rows = x_ref.shape[0]
    low = lane_index((rows, LANES)) < HD
    lanes = lane_index((rows, LANES))
    totals = jnp.zeros((rows, LANES), F32)
    for pair in range(width // LANES):
        at = pair * LANES
        queries = qkv_ref[:, at : at + LANES]
        keys = qkv_ref[:, width + at : width + at + LANES]
        values = qkv_ref[:, 2 * width + at : 2 * width + at + LANES]
        outs = []
        for side in range(2):
            picked = jnp.where(low if side == 0 else ~low, queries, jnp.zeros_like(queries))
            scores = jnp.where(mask, mm(picked, keys, NT) * scale, MASKED_SCORE)
            row_max = jnp.max(scores, axis=-1, keepdims=True)
            weights = jnp.exp(scores - row_max)
            total = jnp.sum(weights, axis=-1, keepdims=True)
            prob = (weights * (1.0 / total)).astype(BF16)
            outs.append(mm(prob, values, NN))
            totals = jnp.where(lanes == 2 * pair + side, row_max + jnp.log(total), totals)
        attended = jnp.where(low, outs[0], outs[1]).astype(BF16)
        att_ref[:, at : at + LANES] = attended
        if at >= half:
            far_ref[:, at - half : at - half + LANES] = attended
    logt_ref[...] = totals


def ffn_kernel(cfg, n_pieces, *refs):
    me_ref, x_ref, att_ref, gm_ref, live_ref = refs[:5]
    own = refs[5 : 5 + n_pieces]
    other = refs[5 + n_pieces : 5 + 2 * n_pieces]
    rest = refs[5 + 2 * n_pieces :]
    out_ref, hidden_ref, gain_ref, wo_ref, win_ref, wgate_ref, gi_ref, gg_ref = rest[:8]
    swap_ref, keep_ref, wdown_ref, gcol = rest[8:]
    me = me_ref[0]
    half, units, main = cfg["half"], cfg["units"], cfg["main"]
    tail = units - main
    rows, model = x_ref.shape
    out_at = 2 * units
    for which, pieces in enumerate((own, other)):
        part = Pieces(me, pieces, cfg["rows"], cfg["layout"])
        part.copy(win_ref, which * main, 0, main)
        part.copy(wgate_ref, which * main, main, main)
        part.copy(win_ref, 2 * main + which * tail, 2 * main, tail)
        part.copy(wgate_ref, 2 * main + which * tail, 2 * main + tail, tail)
        part.copy(wo_ref, which * half, out_at, half)
        part.copy(wdown_ref, which * main, out_at + half, main)
        part.copy(wdown_ref, 2 * main + which * tail, out_at + half + main, tail)
        if which == 0:
            part.copy(gcol, 0, out_at + half + main, LANES)
    gain_row = column_to_row(gcol[...], tail)
    gain_ref[...] = jnp.broadcast_to(gain_row, gain_ref.shape)
    hidden = x_ref[...].astype(F32) + mm(att_ref[...], wo_ref[...], NT)
    hidden_ref[...] = hidden
    n2 = (norm_parts(hidden)[0] * gain_row).astype(BF16)
    swap_ref[:, 0:model] = n2
    grad_mixed = gm_ref[...]
    step = 3 * LANES
    mixed = hidden
    for at in range(0, 2 * units, step):
        unit_in = mm(n2, win_ref[:, at : at + step], NN)
        unit_gate = mm(n2, wgate_ref[:, at : at + step], NN)
        grad_act = mm(grad_mixed, wdown_ref[:, at : at + step], NN)
        cdf = 0.5 * (1.0 + lax.erf(unit_in * SQRT_HALF))
        gelu = unit_in * cdf
        slope = cdf + unit_in * INV_ROOT_TWO_PI * jnp.exp(-0.5 * unit_in * unit_in)
        activated = (gelu * unit_gate).astype(BF16)
        grad_in = (grad_act * unit_gate * slope).astype(BF16)
        grad_gate = (grad_act * gelu).astype(BF16)
        gi_ref[:, at : at + step] = grad_in
        gg_ref[:, at : at + step] = grad_gate
        mixed = mixed + mm(activated, wdown_ref[:, at : at + step], NT)
        for sub in range(0, step, LANES):
            lo = at + sub
            a, gi, gg = (v[:, sub : sub + LANES] for v in (activated, grad_in, grad_gate))
            if lo < 2 * main:
                which, col = divmod(lo, main)
                ref, off = (keep_ref, 0) if which == 0 else (swap_ref, model)
                for value, start in ((gi, 0), (gg, main), (a, 2 * units)):
                    ref[:, off + start + col : off + start + col + LANES] = value
            else:
                low = lane_index((rows, LANES)) < tail
                gi, gg, a = gi.astype(F32), gg.astype(F32), a.astype(F32)
                mine = jnp.where(low, gi, pltpu.roll(gg, tail, 1))
                theirs = jnp.where(low, pltpu.roll(gi, tail, 1), gg)
                for start, here, there in (
                    (2 * main, mine, theirs),
                    (2 * units + main, a, pltpu.roll(a, tail, 1)),
                ):
                    keep_ref[:, start : start + LANES] = here.astype(BF16)
                    start += model
                    swap_ref[:, start : start + LANES] = there.astype(BF16)
    out_ref[...] = (live_ref[...] * mixed).astype(BF16)


def ffn_backward_kernel(hidden_ref, gm_ref, gain_ref, win_ref, wgate_ref, gi_ref, gg_ref, *outs):
    gh_ref, swap_ref = outs
    rows, _ = hidden_ref.shape
    grad_normed = mm(gi_ref[...], win_ref[...], NT) + mm(gg_ref[...], wgate_ref[...], NT)
    normed, inv_std = norm_parts(hidden_ref[...])
    grad_rows, gain_term = norm_back(grad_normed, normed, inv_std, gain_ref[0:1])
    grad_hidden = gm_ref[...].astype(F32) + grad_rows
    gh_ref[...] = grad_hidden
    swap_ref[0:rows, :] = grad_hidden.astype(BF16)
    put_gain(swap_ref, gain_term, rows)


def put_gain(ref, gain_term, rows):
    model = gain_term.shape[1]
    extra = ref.shape[0] - rows
    high = gain_term.astype(BF16).astype(F32)
    first = lax.broadcasted_iota(jnp.int32, (extra, model), 0)
    block = jnp.where(first == 0, high, jnp.where(first == 1, gain_term - high, 0.0))
    ref[rows:, 0:model] = block.astype(BF16)
    if ref.shape[1] > model:
        ref[rows:, model:] = jnp.zeros((extra, ref.shape[1] - model), BF16)


def attn_backward_kernel(cfg, *refs):
    (x_ref, gh_ref, wo_ref, w_ref, qkv_ref, att_ref, logt_ref) = refs[:7]
    seg_row, seg_col, live_row, cos_ref, sin_ref, n1_ref = refs[7:13]
    gin_ref, swap_ref, keep_ref, gatt_ref, gqkv_ref = refs[13:]
    half, width = cfg["half"], 2 * cfg["half"]
    rows, model = x_ref.shape
    gatt_ref[...] = mm(gh_ref[...].astype(BF16), wo_ref[...], NN).astype(BF16)
    mask = attn_mask(seg_row[...], seg_col[...], live_row[...])
    scale = HD ** (-0.5)
    low = lane_index((rows, LANES)) < HD
    cosine, sine = cos_ref[...], sin_ref[...]
    for pair in range(width // LANES):
        at = pair * LANES
        queries = qkv_ref[:, at : at + LANES]
        keys = qkv_ref[:, width + at : width + at + LANES]
        values = qkv_ref[:, 2 * width + at : 2 * width + at + LANES]
        grad_att = gatt_ref[:, at : at + LANES]
        products = grad_att.astype(F32) * att_ref[:, at : at + LANES].astype(F32)
        grads_q, grad_k, grad_v = [], 0.0, 0.0
        for side in range(2):
            on = low if side == 0 else ~low
            q_side = jnp.where(on, queries, jnp.zeros_like(queries))
            g_side = jnp.where(on, grad_att, jnp.zeros_like(grad_att))
            head = 2 * pair + side
            scores = jnp.where(mask, mm(q_side, keys, NT) * scale, MASKED_SCORE)
            prob = jnp.exp(scores - logt_ref[:, head : head + 1])
            row_inner = jnp.sum(jnp.where(on, products, 0.0), axis=-1, keepdims=True)
            grad_prob = mm(g_side, values, NT)
            grad_scores = (prob * (grad_prob - row_inner)).astype(BF16)
            grad_v = grad_v + mm(prob.astype(BF16), g_side, TN)
            grads_q.append(mm(grad_scores, keys, NN))
            grad_k = grad_k + mm(grad_scores, q_side, TN)
        grad_q = jnp.where(low, grads_q[0], grads_q[1]) * scale
        grad_k = grad_k * scale
        grad_q = grad_q * cosine - swap_halves(grad_q) * sine
        grad_k = grad_k * cosine - swap_halves(grad_k) * sine
        for c, value in enumerate((grad_q, grad_k, grad_v)):
            value = value.astype(BF16)
            gqkv_ref[:, c * width + at : c * width + at + LANES] = value
            if at < half:
                keep_ref[0:rows, c * half + at : c * half + at + LANES] = value
            else:
                col = model + c * half + at - half
                swap_ref[0:rows, col : col + LANES] = value
    swap_ref[0:rows, 0:model] = n1_ref[...]
    scaled = mm(gqkv_ref[...], w_ref[...], NT)
    normed, inv_std = norm_parts(x_ref[...].astype(F32))
    grad_rows, gain_term = norm_back(scaled, normed, inv_std, 1.0)
    gin_ref[...] = gh_ref[...] + grad_rows
    put_gain(swap_ref, gain_term, rows)


def grads_kernel(cfg, sections, n_in, fast, me_ref, *refs):
    ins, outs, grad_ref = refs[:n_in], refs[n_in:-1], refs[-1]
    model = cfg["model"]
    tokens = cfg["tokens"]
    for pairs, at, size in sections:
        total = 0.0
        for (left, left_at), (right, right_at) in pairs:
            total = total + mm(
                ins[left][0:tokens, left_at : left_at + model],
                ins[right][0:tokens, right_at : right_at + size],
                TN,
            )
        grad_ref[:, at : at + size] = total
    gain = jnp.zeros((1, model), F32)
    for which in cfg["gain_from"]:
        block = ins[which][tokens:, 0:model].astype(F32)
        gain = gain + block[0:1] + block[1:2]
    columns = row_to_columns(gain)
    total = grad_ref.shape[1]
    last = slice(total - LANES, total)
    if cfg["gain_lane"]:
        keep_low = lane_index(columns.shape) < cfg["gain_lane"]
        columns = jnp.where(keep_low, grad_ref[:, last], columns)
    grad_ref[:, last] = columns
    if not fast:
        outs[0][...] = grad_ref[...]
        return
    me, rows = me_ref[0], cfg["rows"]
    at = 0
    for (order, bit), (first, last) in cfg["emit"]:
        for which in (0, 1):
            for i, distance in enumerate(order):
                start = pl.multiple_of((me ^ distance ^ (bit * which)) * rows, rows)
                outs[at + which][i] = grad_ref[pl.ds(start, rows), first:last].astype(BF16)
        at += 2


def stack_kernel(*refs):
    for i, ref in enumerate(refs[:-1]):
        refs[-1][i] = ref[...]


def combine_kernel(joined, *refs):
    n = (len(refs) - 2) // 2 if joined else len(refs) // 4
    ins, outs = refs[: 2 * n], refs[2 * n :]
    at = 0
    for i in range(n):
        kept, came = ins[2 * i], ins[2 * i + 1]
        blocks, _, cols = kept.shape
        keep, send = (outs[0], outs[1]) if joined else (outs[2 * i], outs[2 * i + 1])
        for j in range(blocks):
            total = kept[j].astype(F32) + came[j].astype(F32)
            ref, k = (keep, j) if j < blocks // 2 else (send, j - blocks // 2)
            ref[k, :, at : at + cols] = total.astype(ref.dtype)
        at += cols if joined else 0


def final_ffn_kernel(kept_c, came_c, kept_ab, came_ab, share):
    cut = kept_c.shape[2]
    share[:, :cut] = kept_c[0] + came_c[0].astype(F32)
    share[:, cut:] = kept_ab[0] + came_ab[0].astype(F32)


def final_qkv_kernel(kept, came, gain_ref, grad, gain_grad):
    half = grad.shape[2]
    gain = gain_ref[...]
    for c in range(3):
        cols = slice(c * half, (c + 1) * half)
        grad[c] = (kept[0, :, cols] + came[0, :, cols].astype(F32)) * gain
    gain_grad[...] = (kept[0, :, 3 * half :] + came[0, :, 3 * half :].astype(F32)) / gain


VMEM = pl.BlockSpec(memory_space=pltpu.VMEM)
SMEM = pl.BlockSpec(memory_space=pltpu.SMEM)


def call(kernel, operands, outs, scratch, scalars=1, flops=0, spare=1 << 20):
    moved = sum(o.size * o.dtype.itemsize for o in operands)
    moved += sum(s.size * s.dtype.itemsize for s in outs)
    held = sum(math.prod(s.shape) * jnp.dtype(s.dtype).itemsize for s in scratch)
    return pl.pallas_call(
        kernel,
        out_shape=outs,
        in_specs=[SMEM] * scalars + [VMEM] * (len(operands) - scalars),
        out_specs=[VMEM] * len(outs),
        scratch_shapes=scratch,
        cost_estimate=pl.CostEstimate(flops=flops, bytes_accessed=moved, transcendentals=0),
        compiler_params=pltpu.CompilerParams(vmem_limit_bytes=moved + held + spare),
    )(*operands)


def shape(*dims, dtype=BF16):
    return jax.ShapeDtypeStruct(dims, dtype)


def stack(planes):
    outs = [shape(len(planes), *planes[0].shape)]
    return call(stack_kernel, list(planes), outs, [], scalars=0)[0]


def combine(joined, *arrays):
    outs = []
    for kept in arrays[::2]:
        blocks, rows, cols = kept.shape
        outs += [shape(blocks // 2, rows, cols, dtype=F32), shape(blocks // 2, rows, cols)]
    if joined:
        blocks, rows = outs[0].shape[:2]
        cols = sum(o.shape[2] for o in outs[::2])
        outs = [shape(blocks, rows, cols, dtype=F32), shape(blocks, rows, cols)]
    kernel = functools.partial(combine_kernel, joined)
    return call(kernel, list(arrays), outs, [], scalars=0)


def shards(
    inputs, gain_attn, w_qkv, w_out, gain_ffn, w_in, w_down, cotangent, segments, lengths, counts
):
    dp, cores = lax.axis_size("dp"), lax.axis_size("tensor")
    me, core = lax.axis_index("dp"), lax.axis_index("tensor")
    seq = segments.shape[1]
    tokens, model = inputs.shape
    rows, half, units = gain_attn.shape[0], w_qkv.shape[2], w_in.shape[2]
    main = units // LANES * LANES
    tail = units - main
    if cores != 2 or tokens != seq or segments.shape[0] != cores or 2 * tail != LANES:
        raise ValueError("unsupported shapes")
    fast = fast_path(dp) and rows % 16 == 0

    def swap_cores(value):
        return lax.ppermute(value, "tensor", [(0, 1), (1, 0)])

    def exchange(value, distance):
        pairs = [(i, i ^ distance) for i in range(dp)]
        return lax.ppermute(value, "dp", pairs)

    def across_z(value):
        return [value] + [exchange(value, z) for z in Z_ALL[1:]]

    def plane(stacked):
        came_x = exchange(stacked, X)
        came_y = exchange(stacked, Y)
        far_a = exchange(came_y[:2], X)
        far_b = exchange(came_x[2:], Y)
        return [stacked, came_x, came_y, far_a, far_b]

    def both_cores(pieces):
        return [swap_cores(piece) for piece in pieces]

    gain_col = gain_attn.astype(F32)[:, None]
    pack_qkv = jnp.concatenate(
        [(w_qkv[c].astype(F32) * gain_col).astype(BF16) for c in range(3)], axis=1
    )
    out_t, down_t = w_out.T, w_down.T
    pack_ffn = jnp.concatenate(
        [
            w_in[:, 0, :main],
            w_in[:, 1, :main],
            w_in[:, 0, main:],
            w_in[:, 1, main:],
            out_t,
            down_t,
            jnp.pad(gain_ffn[:, None], ((0, 0), (0, tail - 1))),
        ],
        axis=1,
    )
    total_qkv, total_ffn = pack_qkv.shape[1], pack_ffn.shape[1]
    cut = total_ffn * 3 // 10 // LANES * LANES
    if fast:
        own_qkv = plane(stack(across_z(pack_qkv)))
        other_qkv = both_cores(own_qkv)
        pack_c, pack_f = pack_ffn[:, :cut], pack_ffn[:, cut:]
        came_x, came_y = exchange(pack_c, X), exchange(pack_c, Y)
        stack_c = stack([pack_c, came_x, came_y, exchange(came_y, X)])
        own_c = across_z(stack_c)
        own_f = plane(stack(across_z(pack_f)))
        own_ffn = own_c + own_f
        other_ffn = both_cores(own_c) + both_cores(own_f)
        layout_qkv = [(d, 0, total_qkv) for d in PLANE_PIECES]
        layout_ffn = [(d, 0, cut) for d in LINE_PIECES]
        layout_ffn += [(d, cut, total_ffn) for d in PLANE_PIECES]
    else:
        own_qkv = [lax.all_gather(pack_qkv, "dp", axis=0, tiled=True)]
        own_ffn = [lax.all_gather(pack_ffn, "dp", axis=0, tiled=True)]
        other_qkv, other_ffn = both_cores(own_qkv), both_cores(own_ffn)
        layout_qkv, layout_ffn = [(None, 0, total_qkv)], [(None, 0, total_ffn)]

    seg = lax.dynamic_slice_in_dim(segments, core, 1, axis=0)
    length = lax.dynamic_slice_in_dim(lengths, core, 1, axis=0)
    live = ((jnp.arange(seq, dtype=jnp.int32) < length) & (core < counts[0])).astype(F32)
    seg_row, seg_col = seg, seg.reshape(seq, 1)
    live_row, live_col = live.reshape(1, seq), live.reshape(seq, 1)
    earlier = jnp.sum((seg_row < seg_col).astype(jnp.int32), axis=1)
    position = (jnp.arange(seq, dtype=jnp.int32) - earlier).astype(F32)
    frequency = jnp.power(F32(THETA_BASE), -(jnp.arange(HD // 2, dtype=F32) * (2.0 / HD)))
    angle = position[:, None] * frequency[None, :]
    cosine, sine = jnp.cos(angle), jnp.sin(angle)
    repeats = LANES // HD
    cosine = jnp.concatenate([cosine, cosine] * repeats, axis=1)
    sine = jnp.concatenate([-sine, sine] * repeats, axis=1)
    grad_mixed = (live_col * cotangent.astype(F32)).astype(BF16)
    their_mixed = swap_cores(grad_mixed)
    me_vec = me.astype(jnp.int32).reshape(1)

    cfg = dict(half=half, rows=rows, layout=layout_qkv, units=units, main=main, model=model)
    width = 2 * half
    w_full, qkv, att, far, logt, n1 = call(
        functools.partial(attn_forward_kernel, cfg, len(own_qkv)),
        [me_vec, inputs, *own_qkv, *other_qkv, seg_row, seg_col, live_row, cosine, sine],
        [
            shape(model, 3 * width),
            shape(tokens, 3 * width),
            shape(tokens, width),
            shape(tokens, half),
            shape(tokens, LANES, dtype=F32),
            shape(tokens, model),
        ],
        [],
        flops=2 * tokens * model * 3 * width,
        spare=6 << 20,
    )
    their_far = swap_cores(far)
    ffn_cfg = dict(cfg, layout=layout_ffn)
    side = 2 * units + main + LANES
    output, hidden, gain2, wo_full, win_full, wgate_full, gi, gg, swap_b, keep1 = call(
        functools.partial(ffn_kernel, ffn_cfg, len(own_ffn)),
        [me_vec, inputs, att, grad_mixed, live_col, *own_ffn, *other_ffn],
        [
            shape(tokens, model),
            shape(tokens, model, dtype=F32),
            shape(8, model, dtype=F32),
            shape(model, width),
            shape(model, 2 * units),
            shape(model, 2 * units),
            shape(tokens, 2 * units),
            shape(tokens, 2 * units),
            shape(tokens, model + side),
            shape(tokens, side),
        ],
        [pltpu.VMEM((model, 2 * units), BF16), pltpu.VMEM((model, LANES), BF16)],
        flops=2 * tokens * model * 8 * units,
        spare=6 << 20,
    )
    their_b = swap_cores(swap_b)
    grad_hidden, swap_h = call(
        ffn_backward_kernel,
        [hidden, grad_mixed, gain2, win_full, wgate_full, gi, gg],
        [shape(tokens, model, dtype=F32), shape(tokens + 16, model)],
        [],
        scalars=0,
        flops=2 * tokens * model * 4 * units,
        spare=6 << 20,
    )
    their_h = swap_cores(swap_h)

    def grads(sections, operands, cfg):
        total = cfg["total"]
        outs = [shape(model, total, dtype=F32)]
        if fast:
            outs = [shape(8, rows, last - first) for _, (first, last) in cfg["emit"] for _ in "ks"]
        return call(
            functools.partial(grads_kernel, cfg, sections, len(operands), fast),
            [me_vec, *operands],
            outs,
            [pltpu.VMEM((model, total), F32)],
            flops=4 * tokens * model * total,
            spare=6 << 20,
        )

    total1 = 2 * units + half + main + LANES
    sections1 = [
        ((((0, 0), (1, 0)), ((2, 0), (2, model))), 0, 2 * units),
        ((((3, 0), (4, 0)), ((5, 0), (6, 0))), 2 * units, half),
        (
            (((7, 0), (1, 2 * units)), ((8, 0), (2, model + 2 * units))),
            2 * units + half,
            main + LANES,
        ),
    ]
    operands1 = [
        swap_b, keep1, their_b, swap_h, att, their_h, their_far, grad_mixed, their_mixed,
    ]
    cut1 = total1 * 9 // 25 // LANES * LANES
    mid = cut1 + (total1 - cut1) // 2 // LANES * LANES
    emit1 = [(GRAD_C, (0, cut1)), (GRAD_A, (cut1, mid)), (GRAD_B, (mid, total1))]
    cfg1 = dict(
        ffn_cfg, tokens=tokens, total=total1, gain_lane=tail, emit=emit1, gain_from=(3, 5)
    )
    pieces1 = grads(sections1, operands1, cfg1)
    grad_inputs, swap2, keep2 = call(
        functools.partial(attn_backward_kernel, cfg),
        [
            inputs, grad_hidden, wo_full, w_full, qkv, att, logt,
            seg_row, seg_col, live_row, cosine, sine, n1,
        ],
        [
            shape(tokens, model, dtype=F32),
            shape(tokens + 16, model + 3 * half),
            shape(tokens, 3 * half),
        ],
        [pltpu.VMEM((tokens, width), BF16), pltpu.VMEM((tokens, 3 * width), BF16)],
        scalars=0,
        flops=2 * tokens * model * 5 * width,
        spare=6 << 20,
    )
    total2 = 3 * half + LANES
    emit2 = [(GRAD_A, (0, total2 // 2)), (GRAD_B, (total2 // 2, total2))]
    cfg2 = dict(cfg, tokens=tokens, total=total2, gain_lane=0, emit=emit2, gain_from=(0, 2))
    sections2 = [((((0, 0), (1, 0)), ((2, 0), (2, model))), 0, 3 * half)]
    operands2 = [swap2, keep2, swap_cores(swap2)]
    pieces2 = grads(sections2, operands2, cfg2)

    if fast:
        keep_c, send_c, keep_a, send_a, keep_b, send_b = pieces1
        keep_a, send_a, keep_b, send_b = combine(
            False, keep_a, exchange(send_a, X), keep_b, exchange(send_b, Y)
        )
        keep_c, send_c = combine(False, keep_c, exchange(send_c, Z))
        keep_c, send_c = combine(False, keep_c, exchange(send_c, ZZ))
        keep, send = combine(True, keep_a, exchange(send_a, Y), keep_b, exchange(send_b, X))
        keep_c, send_c = combine(False, keep_c, exchange(send_c, X))
        keep, send = combine(False, keep, exchange(send, Z))
        came_c, came = exchange(send_c, Y), exchange(send, ZZ)
        share1 = call(
            final_ffn_kernel,
            [keep_c, came_c, keep, came],
            [shape(rows, total1, dtype=F32)],
            [],
            scalars=0,
        )[0]
        keep_a, send_a, keep_b, send_b = pieces2
        keep_a, send_a, keep_b, send_b = combine(
            False, keep_a, exchange(send_a, X), keep_b, exchange(send_b, Y)
        )
        keep, send = combine(True, keep_a, exchange(send_a, Y), keep_b, exchange(send_b, X))
        keep, send = combine(False, keep, exchange(send, Z))
        grad_qkv, gain1_share = call(
            final_qkv_kernel,
            [keep, exchange(send, ZZ), gain_col],
            [shape(3, rows, half, dtype=F32), shape(rows, LANES, dtype=F32)],
            [],
            scalars=0,
        )
        grad_gain1 = gain1_share[:, 0]
    else:
        share1, share2 = (
            lax.psum_scatter(pieces[0], "dp", scatter_dimension=0, tiled=True)
            for pieces in (pieces1, pieces2)
        )
        grad_qkv = jnp.stack([share2[:, c * half : (c + 1) * half] * gain_col for c in range(3)])
        grad_gain1 = share2[:, 3 * half] / gain_col[:, 0]
    heads = share1[:, : 2 * main].reshape(rows, 2, main)
    tails = share1[:, 2 * main : 2 * units].reshape(rows, 2, tail)
    grad_in = jnp.concatenate([heads, tails], axis=2)
    grad_out = share1[:, 2 * units : 2 * units + half].T
    grad_down = share1[:, 2 * units + half : 2 * units + half + units].T
    grad_gain2 = share1[:, 2 * units + half + units]
    return (
        output,
        grad_inputs,
        grad_gain1,
        grad_qkv,
        grad_out,
        grad_gain2,
        grad_in,
        grad_down,
    )


def fast_path(dp):
    return dp == 16


def solution(mesh):
    in_specs = (
        P(("dp", "tensor"), None),
        P("dp"),
        P(None, "dp", "tensor"),
        P("tensor", "dp"),
        P("dp"),
        P("dp", None, "tensor"),
        P("tensor", "dp"),
        P(("dp", "tensor"), None),
        P("dp", None),
        P("dp"),
        P("dp"),
    )
    out_specs = (
        P(("dp", "tensor"), None),
        P(("dp", "tensor"), None),
        P("dp"),
        P(None, "dp", "tensor"),
        P("tensor", "dp"),
        P("dp"),
        P("dp", None, "tensor"),
        P("tensor", "dp"),
    )

    return jax.shard_map(shards, mesh=mesh, in_specs=in_specs, out_specs=out_specs, check_vma=False)
```

```python
import functools
import math

import jax
import jax.numpy as jnp
from jax import lax
from jax.experimental import pallas as pl
from jax.experimental.pallas import tpu as pltpu
from jax.sharding import PartitionSpec as P


HD = 64
LANES = 128

THETA_BASE = 160000.0
EPSILON = 1e-05
SQRT_HALF = 0.7071067811865476
INV_ROOT_TWO_PI = 0.3989422804014327
MASKED_SCORE = -1e30

F32 = jnp.float32
BF16 = jnp.bfloat16


NN = (((1,), (0,)), ((), ()))
NT = (((1,), (1,)), ((), ()))
TN = (((0,), (0,)), ((), ()))

X, Y, Z, ZZ = 1, 2, 4, 8
Z_ALL = (0, Z, ZZ, Z | ZZ)
Z_HALVES = (0, ZZ, Z, Z | ZZ)
XY_ALL = (0, X, Y, X | Y)
XY_HALVES = (0, Y, X, X | Y)


def shift(distances, by):
    return tuple(d ^ by for d in distances)


PLANE_PIECES = (Z_ALL, shift(Z_ALL, X), shift(Z_ALL, Y), (3, 7), (11, 15))
LINE_PIECES = tuple(shift(XY_ALL, z) for z in Z_ALL)

GRAD_A = (tuple(y + z for y in (0, Y) for z in Z_HALVES), X)
GRAD_B = (tuple(x + z for x in (0, X) for z in Z_HALVES), Y)
GRAD_C = (tuple(z + xy for z in (0, ZZ) for xy in XY_HALVES), Z)


def mm(left, right, dims):
    return lax.dot_general(left, right, dims, preferred_element_type=F32)


def norm_parts(rows_in):
    centre = rows_in - jnp.mean(rows_in, axis=-1, keepdims=True)
    inv_std = lax.rsqrt(jnp.mean(centre * centre, axis=-1, keepdims=True) + EPSILON)
    return centre * inv_std, inv_std


def norm_back(grad_normed, normed, inv_std, gain_row):
    scaled = grad_normed * gain_row
    inner_mean = jnp.mean(scaled * normed, axis=-1, keepdims=True)
    grad_rows = inv_std * (scaled - jnp.mean(scaled, axis=-1, keepdims=True) - normed * inner_mean)
    return grad_rows, jnp.sum(grad_normed * normed, axis=0, keepdims=True)


def lane_index(shape):
    return lax.broadcasted_iota(jnp.int32, shape, 1)


def swap_halves(chunk):
    half = HD // 2
    return jnp.where(
        lane_index(chunk.shape) % HD < half,
        pltpu.roll(chunk, LANES - half, 1),
        pltpu.roll(chunk, half, 1),
    )


def column_to_row(columns, lane):
    pick = (lane_index((8, LANES)) == lane).astype(BF16)
    return mm(pick, columns, NT)[0:1]


def row_to_columns(row):
    return jnp.transpose(jnp.broadcast_to(row, (LANES, row.shape[1])), (1, 0))


class Pieces:
    def __init__(self, me, refs, rows, layout):
        self.me, self.refs, self.rows, self.layout = me, refs, rows, layout

    def copy(self, dst, dst_col, src_col, width):
        for ref, (distances, first, last) in zip(self.refs, self.layout):
            low, high = max(first, src_col), min(last, src_col + width)
            if low >= high:
                continue
            at = slice(dst_col + low - src_col, dst_col + high - src_col)
            cols = slice(low - first, high - first)
            if distances is None:
                dst[:, at] = ref[:, cols]
                continue
            for i, distance in enumerate(distances):
                base = pl.multiple_of((self.me ^ distance) * self.rows, self.rows)
                dst[pl.ds(base, self.rows), at] = ref[i, :, cols]


def attn_mask(seg_row, seg_col, live_row):
    same = seg_col == seg_row
    shape = same.shape
    diagonal = lax.broadcasted_iota(jnp.int32, shape, 0) == lane_index(shape)
    return (same & (live_row > 0)) | diagonal


def attn_forward_kernel(cfg, n_pieces, *refs):
    me_ref, x_ref = refs[:2]
    own = refs[2 : 2 + n_pieces]
    other = refs[2 + n_pieces : 2 + 2 * n_pieces]
    seg_row, seg_col, live_row, cos_ref, sin_ref = refs[2 + 2 * n_pieces : 7 + 2 * n_pieces]
    w_ref, qkv_ref, att_ref, far_ref, logt_ref, n1_ref = refs[7 + 2 * n_pieces :]
    me = me_ref[0]
    half, width = cfg["half"], 2 * cfg["half"]
    for which, pieces in enumerate((own, other)):
        part = Pieces(me, pieces, cfg["rows"], cfg["layout"])
        for c in range(3):
            part.copy(w_ref, c * width + which * half, c * half, half)
    normed, _ = norm_parts(x_ref[...].astype(F32))
    n1 = normed.astype(BF16)
    n1_ref[...] = n1
    cosine, sine = cos_ref[...], sin_ref[...]
    step = 2 * LANES
    for at in range(0, 3 * width, step):
        product = mm(n1, w_ref[:, at : at + step], NN)
        for sub in range(0, step, LANES):
            chunk = product[:, sub : sub + LANES]
            if at < 2 * width:
                chunk = chunk * cosine + swap_halves(chunk) * sine
            chunk = chunk.astype(BF16)
            if at + sub < width:
                chunk = chunk * BF16(HD ** (-0.5))
            qkv_ref[:, at + sub : at + sub + LANES] = chunk
    mask = attn_mask(seg_row[...], seg_col[...], live_row[...])
    rows = x_ref.shape[0]
    low = lane_index((rows, LANES)) < HD
    lanes = lane_index((rows, LANES))
    totals = jnp.zeros((rows, LANES), F32)
    for pair in range(width // LANES):
        at = pair * LANES
        queries = qkv_ref[:, at : at + LANES]
        keys = qkv_ref[:, width + at : width + at + LANES]
        values = qkv_ref[:, 2 * width + at : 2 * width + at + LANES]
        outs = []
        for side in range(2):
            picked = jnp.where(low if side == 0 else ~low, queries, jnp.zeros_like(queries))
            scores = jnp.where(mask, mm(picked, keys, NT), MASKED_SCORE)
            row_max = jnp.max(scores, axis=-1, keepdims=True)
            weights = jnp.exp(scores - row_max)
            total = jnp.sum(weights, axis=-1, keepdims=True)
            prob = (weights * (1.0 / total)).astype(BF16)
            outs.append(mm(prob, values, NN))
            totals = jnp.where(lanes == 2 * pair + side, row_max + jnp.log(total), totals)
        attended = jnp.where(low, outs[0], outs[1]).astype(BF16)
        att_ref[:, at : at + LANES] = attended
        if at >= half:
            far_ref[:, at - half : at - half + LANES] = attended
    logt_ref[...] = totals


def ffn_kernel(cfg, n_pieces, *refs):
    me_ref, x_ref, att_ref, gm_ref, live_ref = refs[:5]
    own = refs[5 : 5 + n_pieces]
    other = refs[5 + n_pieces : 5 + 2 * n_pieces]
    rest = refs[5 + 2 * n_pieces :]
    out_ref, hidden_ref, gain_ref, wo_ref, win_ref, wgate_ref, gi_ref, gg_ref = rest[:8]
    swap_ref, keep_ref, wdown_ref, gcol = rest[8:]
    me = me_ref[0]
    half, units, main = cfg["half"], cfg["units"], cfg["main"]
    tail = units - main
    rows, model = x_ref.shape
    out_at = 2 * units
    for which, pieces in enumerate((own, other)):
        part = Pieces(me, pieces, cfg["rows"], cfg["layout"])
        part.copy(win_ref, which * main, 0, main)
        part.copy(wgate_ref, which * main, main, main)
        part.copy(win_ref, 2 * main + which * tail, 2 * main, tail)
        part.copy(wgate_ref, 2 * main + which * tail, 2 * main + tail, tail)
        part.copy(wo_ref, which * half, out_at, half)
        part.copy(wdown_ref, which * main, out_at + half, main)
        part.copy(wdown_ref, 2 * main + which * tail, out_at + half + main, tail)
        if which == 0:
            part.copy(gcol, 0, out_at + half + main, LANES)
    gain_row = column_to_row(gcol[...], tail)
    gain_ref[...] = jnp.broadcast_to(gain_row, gain_ref.shape)
    hidden = x_ref[...].astype(F32) + mm(att_ref[...], wo_ref[...], NT)
    hidden_ref[...] = hidden
    n2 = (norm_parts(hidden)[0] * gain_row).astype(BF16)
    swap_ref[:, 0:model] = n2
    grad_mixed = gm_ref[...]
    step = 3 * LANES
    mixed = hidden
    for at in range(0, 2 * units, step):
        unit_in = mm(n2, win_ref[:, at : at + step], NN)
        unit_gate = mm(n2, wgate_ref[:, at : at + step], NN)
        grad_act = mm(grad_mixed, wdown_ref[:, at : at + step], NN)
        cdf = 0.5 * (1.0 + lax.erf(unit_in * SQRT_HALF))
        gelu = unit_in * cdf
        slope = cdf + unit_in * INV_ROOT_TWO_PI * jnp.exp(-0.5 * unit_in * unit_in)
        activated = (gelu * unit_gate).astype(BF16)
        grad_in = (grad_act * unit_gate * slope).astype(BF16)
        grad_gate = (grad_act * gelu).astype(BF16)
        gi_ref[:, at : at + step] = grad_in
        gg_ref[:, at : at + step] = grad_gate
        mixed = mixed + mm(activated, wdown_ref[:, at : at + step], NT)
        for sub in range(0, step, LANES):
            lo = at + sub
            a, gi, gg = (v[:, sub : sub + LANES] for v in (activated, grad_in, grad_gate))
            if lo < 2 * main:
                which, col = divmod(lo, main)
                ref, off = (keep_ref, 0) if which == 0 else (swap_ref, model)
                for value, start in ((gi, 0), (gg, main), (a, 2 * units)):
                    ref[:, off + start + col : off + start + col + LANES] = value
            else:
                low = lane_index((rows, LANES)) < tail
                gi, gg, a = gi.astype(F32), gg.astype(F32), a.astype(F32)
                mine = jnp.where(low, gi, pltpu.roll(gg, tail, 1))
                theirs = jnp.where(low, pltpu.roll(gi, tail, 1), gg)
                for start, here, there in (
                    (2 * main, mine, theirs),
                    (2 * units + main, a, pltpu.roll(a, tail, 1)),
                ):
                    keep_ref[:, start : start + LANES] = here.astype(BF16)
                    start += model
                    swap_ref[:, start : start + LANES] = there.astype(BF16)
    out_ref[...] = (live_ref[...] * mixed).astype(BF16)


def ffn_backward_kernel(hidden_ref, gm_ref, gain_ref, win_ref, wgate_ref, gi_ref, gg_ref, *outs):
    gh_ref, swap_ref = outs
    rows, _ = hidden_ref.shape
    grad_normed = mm(gi_ref[...], win_ref[...], NT) + mm(gg_ref[...], wgate_ref[...], NT)
    normed, inv_std = norm_parts(hidden_ref[...])
    grad_rows, gain_term = norm_back(grad_normed, normed, inv_std, gain_ref[0:1])
    grad_hidden = gm_ref[...].astype(F32) + grad_rows
    gh_ref[...] = grad_hidden
    swap_ref[0:rows, :] = grad_hidden.astype(BF16)
    put_gain(swap_ref, gain_term, rows)


def put_gain(ref, gain_term, rows):
    model = gain_term.shape[1]
    extra = ref.shape[0] - rows
    high = gain_term.astype(BF16).astype(F32)
    first = lax.broadcasted_iota(jnp.int32, (extra, model), 0)
    block = jnp.where(first == 0, high, jnp.where(first == 1, gain_term - high, 0.0))
    ref[rows:, 0:model] = block.astype(BF16)
    if ref.shape[1] > model:
        ref[rows:, model:] = jnp.zeros((extra, ref.shape[1] - model), BF16)


def attn_backward_kernel(cfg, *refs):
    (x_ref, gh_ref, wo_ref, w_ref, qkv_ref, att_ref, logt_ref) = refs[:7]
    seg_row, seg_col, live_row, cos_ref, sin_ref, n1_ref = refs[7:13]
    gin_ref, swap_ref, keep_ref, gatt_ref, gqkv_ref = refs[13:]
    half, width = cfg["half"], 2 * cfg["half"]
    rows, model = x_ref.shape
    gatt_ref[...] = mm(gh_ref[...].astype(BF16), wo_ref[...], NN).astype(BF16)
    mask = attn_mask(seg_row[...], seg_col[...], live_row[...])
    scale = HD ** (-0.5)
    low = lane_index((rows, LANES)) < HD
    cosine, sine = cos_ref[...], sin_ref[...]
    for pair in range(width // LANES):
        at = pair * LANES
        queries = qkv_ref[:, at : at + LANES]
        keys = qkv_ref[:, width + at : width + at + LANES]
        values = qkv_ref[:, 2 * width + at : 2 * width + at + LANES]
        grad_att = gatt_ref[:, at : at + LANES]
        products = grad_att.astype(F32) * att_ref[:, at : at + LANES].astype(F32)
        grads_q, grad_k, grad_v = [], 0.0, 0.0
        for side in range(2):
            on = low if side == 0 else ~low
            q_side = jnp.where(on, queries, jnp.zeros_like(queries))
            g_side = jnp.where(on, grad_att, jnp.zeros_like(grad_att))
            head = 2 * pair + side
            scores = jnp.where(mask, mm(q_side, keys, NT), MASKED_SCORE)
            prob = jnp.exp(scores - logt_ref[:, head : head + 1])
            row_inner = jnp.sum(jnp.where(on, products, 0.0), axis=-1, keepdims=True)
            grad_prob = mm(g_side, values, NT)
            grad_scores = (prob * (grad_prob - row_inner)).astype(BF16)
            grad_v = grad_v + mm(prob.astype(BF16), g_side, TN)
            grads_q.append(mm(grad_scores, keys, NN))
            grad_k = grad_k + mm(grad_scores, q_side, TN)
        grad_q = jnp.where(low, grads_q[0], grads_q[1]) * scale
        grad_q = grad_q * cosine - swap_halves(grad_q) * sine
        grad_k = grad_k * cosine - swap_halves(grad_k) * sine
        for c, value in enumerate((grad_q, grad_k, grad_v)):
            value = value.astype(BF16)
            gqkv_ref[:, c * width + at : c * width + at + LANES] = value
            if at < half:
                keep_ref[0:rows, c * half + at : c * half + at + LANES] = value
            else:
                col = model + c * half + at - half
                swap_ref[0:rows, col : col + LANES] = value
    swap_ref[0:rows, 0:model] = n1_ref[...]
    scaled = mm(gqkv_ref[...], w_ref[...], NT)
    normed, inv_std = norm_parts(x_ref[...].astype(F32))
    grad_rows, gain_term = norm_back(scaled, normed, inv_std, 1.0)
    gin_ref[...] = gh_ref[...] + grad_rows
    put_gain(swap_ref, gain_term, rows)


def grads_kernel(cfg, sections, n_in, fast, me_ref, *refs):
    ins, outs, grad_ref = refs[:n_in], refs[n_in:-1], refs[-1]
    model = cfg["model"]
    tokens = cfg["tokens"]
    for pairs, at, size in sections:
        total = 0.0
        for (left, left_at), (right, right_at) in pairs:
            total = total + mm(
                ins[left][0:tokens, left_at : left_at + model],
                ins[right][0:tokens, right_at : right_at + size],
                TN,
            )
        grad_ref[:, at : at + size] = total
    gain = jnp.zeros((1, model), F32)
    for which in cfg["gain_from"]:
        block = ins[which][tokens:, 0:model].astype(F32)
        gain = gain + block[0:1] + block[1:2]
    columns = row_to_columns(gain)
    total = grad_ref.shape[1]
    last = slice(total - LANES, total)
    if cfg["gain_lane"]:
        keep_low = lane_index(columns.shape) < cfg["gain_lane"]
        columns = jnp.where(keep_low, grad_ref[:, last], columns)
    grad_ref[:, last] = columns
    if not fast:
        outs[0][...] = grad_ref[...]
        return
    me, rows = me_ref[0], cfg["rows"]
    at = 0
    for (order, bit), (first, last) in cfg["emit"]:
        for which in (0, 1):
            for i, distance in enumerate(order):
                start = pl.multiple_of((me ^ distance ^ (bit * which)) * rows, rows)
                outs[at + which][i] = grad_ref[pl.ds(start, rows), first:last].astype(BF16)
        at += 2


def stack_kernel(*refs):
    for i, ref in enumerate(refs[:-1]):
        refs[-1][i] = ref[...]


def combine_kernel(joined, *refs):
    n = (len(refs) - 2) // 2 if joined else len(refs) // 4
    ins, outs = refs[: 2 * n], refs[2 * n :]
    at = 0
    for i in range(n):
        kept, came = ins[2 * i], ins[2 * i + 1]
        blocks, _, cols = kept.shape
        keep, send = (outs[0], outs[1]) if joined else (outs[2 * i], outs[2 * i + 1])
        for j in range(blocks):
            total = kept[j].astype(F32) + came[j].astype(F32)
            ref, k = (keep, j) if j < blocks // 2 else (send, j - blocks // 2)
            ref[k, :, at : at + cols] = total.astype(ref.dtype)
        at += cols if joined else 0


def final_ffn_kernel(kept_c, came_c, kept_ab, came_ab, share):
    cut = kept_c.shape[2]
    share[:, :cut] = kept_c[0] + came_c[0].astype(F32)
    share[:, cut:] = kept_ab[0] + came_ab[0].astype(F32)


def final_qkv_kernel(kept, came, gain_ref, grad, gain_grad):
    half = grad.shape[2]
    gain = gain_ref[...]
    for c in range(3):
        cols = slice(c * half, (c + 1) * half)
        grad[c] = (kept[0, :, cols] + came[0, :, cols].astype(F32)) * gain
    columns = (kept[0, :, 3 * half :] + came[0, :, 3 * half :].astype(F32)) / gain
    row = lax.broadcasted_iota(jnp.int32, columns.shape, 0)
    picked = jnp.where(row == lane_index(columns.shape), columns, 0.0)
    gain_grad[...] = jnp.sum(picked, axis=0)[: gain_grad.shape[0]]


VMEM = pl.BlockSpec(memory_space=pltpu.VMEM)
SMEM = pl.BlockSpec(memory_space=pltpu.SMEM)


def call(kernel, operands, outs, scratch, scalars=1, flops=0, spare=1 << 20):
    moved = sum(o.size * o.dtype.itemsize for o in operands)
    moved += sum(s.size * s.dtype.itemsize for s in outs)
    held = sum(math.prod(s.shape) * jnp.dtype(s.dtype).itemsize for s in scratch)
    return pl.pallas_call(
        kernel,
        out_shape=outs,
        in_specs=[SMEM] * scalars + [VMEM] * (len(operands) - scalars),
        out_specs=[VMEM] * len(outs),
        scratch_shapes=scratch,
        cost_estimate=pl.CostEstimate(flops=flops, bytes_accessed=moved, transcendentals=0),
        compiler_params=pltpu.CompilerParams(vmem_limit_bytes=moved + held + spare),
    )(*operands)


def shape(*dims, dtype=BF16):
    return jax.ShapeDtypeStruct(dims, dtype)


def stack(planes):
    outs = [shape(len(planes), *planes[0].shape)]
    return call(stack_kernel, list(planes), outs, [], scalars=0)[0]


def combine(joined, *arrays):
    outs = []
    for kept in arrays[::2]:
        blocks, rows, cols = kept.shape
        outs += [shape(blocks // 2, rows, cols, dtype=F32), shape(blocks // 2, rows, cols)]
    if joined:
        blocks, rows = outs[0].shape[:2]
        cols = sum(o.shape[2] for o in outs[::2])
        outs = [shape(blocks, rows, cols, dtype=F32), shape(blocks, rows, cols)]
    kernel = functools.partial(combine_kernel, joined)
    return call(kernel, list(arrays), outs, [], scalars=0)


def shards(
    inputs, gain_attn, w_qkv, w_out, gain_ffn, w_in, w_down, cotangent, segments, lengths, counts
):
    dp, cores = lax.axis_size("dp"), lax.axis_size("tensor")
    me, core = lax.axis_index("dp"), lax.axis_index("tensor")
    seq = segments.shape[1]
    tokens, model = inputs.shape
    rows, half, units = gain_attn.shape[0], w_qkv.shape[2], w_in.shape[2]
    main = units // LANES * LANES
    tail = units - main
    if cores != 2 or tokens != seq or segments.shape[0] != cores or 2 * tail != LANES:
        raise ValueError("unsupported shapes")
    fast = fast_path(dp) and rows % 16 == 0

    def swap_cores(value):
        return lax.ppermute(value, "tensor", [(0, 1), (1, 0)])

    def exchange(value, distance):
        pairs = [(i, i ^ distance) for i in range(dp)]
        return lax.ppermute(value, "dp", pairs)

    def across_z(value):
        return [value] + [exchange(value, z) for z in Z_ALL[1:]]

    def plane(stacked):
        came_x = exchange(stacked, X)
        came_y = exchange(stacked, Y)
        far_a = exchange(came_y[:2], X)
        far_b = exchange(came_x[2:], Y)
        return [stacked, came_x, came_y, far_a, far_b]

    def both_cores(pieces):
        return [swap_cores(piece) for piece in pieces]

    gain_col = gain_attn.astype(F32)[:, None]
    pack_qkv = jnp.concatenate(
        [(w_qkv[c].astype(F32) * gain_col).astype(BF16) for c in range(3)], axis=1
    )
    out_t, down_t = w_out.T, w_down.T
    pack_ffn = jnp.concatenate(
        [
            w_in[:, 0, :main],
            w_in[:, 1, :main],
            w_in[:, 0, main:],
            w_in[:, 1, main:],
            out_t,
            down_t,
            jnp.pad(gain_ffn[:, None], ((0, 0), (0, tail - 1))),
        ],
        axis=1,
    )
    total_qkv, total_ffn = pack_qkv.shape[1], pack_ffn.shape[1]
    cut = total_ffn // 4 // LANES * LANES
    if fast:
        own_qkv = plane(stack(across_z(pack_qkv)))
        other_qkv = both_cores(own_qkv)
        pack_c, pack_f = pack_ffn[:, :cut], pack_ffn[:, cut:]
        came_x, came_y = exchange(pack_c, X), exchange(pack_c, Y)
        stack_c = stack([pack_c, came_x, came_y, exchange(came_y, X)])
        own_c = across_z(stack_c)
        own_f = plane(stack(across_z(pack_f)))
        own_ffn = own_c + own_f
        other_ffn = both_cores(own_c) + both_cores(own_f)
        layout_qkv = [(d, 0, total_qkv) for d in PLANE_PIECES]
        layout_ffn = [(d, 0, cut) for d in LINE_PIECES]
        layout_ffn += [(d, cut, total_ffn) for d in PLANE_PIECES]
    else:
        own_qkv = [lax.all_gather(pack_qkv, "dp", axis=0, tiled=True)]
        own_ffn = [lax.all_gather(pack_ffn, "dp", axis=0, tiled=True)]
        other_qkv, other_ffn = both_cores(own_qkv), both_cores(own_ffn)
        layout_qkv, layout_ffn = [(None, 0, total_qkv)], [(None, 0, total_ffn)]

    seg = lax.dynamic_slice_in_dim(segments, core, 1, axis=0)
    length = lax.dynamic_slice_in_dim(lengths, core, 1, axis=0)
    live = ((jnp.arange(seq, dtype=jnp.int32) < length) & (core < counts[0])).astype(F32)
    seg_row, seg_col = seg, seg.reshape(seq, 1)
    live_row, live_col = live.reshape(1, seq), live.reshape(seq, 1)
    earlier = jnp.sum((seg_row < seg_col).astype(jnp.int32), axis=1)
    position = (jnp.arange(seq, dtype=jnp.int32) - earlier).astype(F32)
    frequency = jnp.power(F32(THETA_BASE), -(jnp.arange(HD // 2, dtype=F32) * (2.0 / HD)))
    angle = position[:, None] * frequency[None, :]
    cosine, sine = jnp.cos(angle), jnp.sin(angle)
    repeats = LANES // HD
    cosine = jnp.concatenate([cosine, cosine] * repeats, axis=1)
    sine = jnp.concatenate([-sine, sine] * repeats, axis=1)
    grad_mixed = (live_col * cotangent.astype(F32)).astype(BF16)
    their_mixed = swap_cores(grad_mixed)
    me_vec = me.astype(jnp.int32).reshape(1)

    cfg = dict(half=half, rows=rows, layout=layout_qkv, units=units, main=main, model=model)
    width = 2 * half
    w_full, qkv, att, far, logt, n1 = call(
        functools.partial(attn_forward_kernel, cfg, len(own_qkv)),
        [me_vec, inputs, *own_qkv, *other_qkv, seg_row, seg_col, live_row, cosine, sine],
        [
            shape(model, 3 * width),
            shape(tokens, 3 * width),
            shape(tokens, width),
            shape(tokens, half),
            shape(tokens, LANES, dtype=F32),
            shape(tokens, model),
        ],
        [],
        flops=2 * tokens * model * 3 * width,
        spare=6 << 20,
    )
    their_far = swap_cores(far)
    ffn_cfg = dict(cfg, layout=layout_ffn)
    side = 2 * units + main + LANES
    output, hidden, gain2, wo_full, win_full, wgate_full, gi, gg, swap_b, keep1 = call(
        functools.partial(ffn_kernel, ffn_cfg, len(own_ffn)),
        [me_vec, inputs, att, grad_mixed, live_col, *own_ffn, *other_ffn],
        [
            shape(tokens, model),
            shape(tokens, model, dtype=F32),
            shape(8, model, dtype=F32),
            shape(model, width),
            shape(model, 2 * units),
            shape(model, 2 * units),
            shape(tokens, 2 * units),
            shape(tokens, 2 * units),
            shape(tokens, model + side),
            shape(tokens, side),
        ],
        [pltpu.VMEM((model, 2 * units), BF16), pltpu.VMEM((model, LANES), BF16)],
        flops=2 * tokens * model * 8 * units,
        spare=6 << 20,
    )
    their_b = swap_cores(swap_b)
    grad_hidden, swap_h = call(
        ffn_backward_kernel,
        [hidden, grad_mixed, gain2, win_full, wgate_full, gi, gg],
        [shape(tokens, model, dtype=F32), shape(tokens + 16, model)],
        [],
        scalars=0,
        flops=2 * tokens * model * 4 * units,
        spare=6 << 20,
    )
    their_h = swap_cores(swap_h)

    def grads(sections, operands, cfg):
        total = cfg["total"]
        outs = [shape(model, total, dtype=F32)]
        if fast:
            outs = [shape(8, rows, last - first) for _, (first, last) in cfg["emit"] for _ in "ks"]
        return call(
            functools.partial(grads_kernel, cfg, sections, len(operands), fast),
            [me_vec, *operands],
            outs,
            [pltpu.VMEM((model, total), F32)],
            flops=4 * tokens * model * total,
            spare=6 << 20,
        )

    total1 = 2 * units + half + main + LANES
    sections1 = [
        ((((0, 0), (1, 0)), ((2, 0), (2, model))), 0, 2 * units),
        ((((3, 0), (4, 0)), ((5, 0), (6, 0))), 2 * units, half),
        (
            (((7, 0), (1, 2 * units)), ((8, 0), (2, model + 2 * units))),
            2 * units + half,
            main + LANES,
        ),
    ]
    operands1 = [
        swap_b, keep1, their_b, swap_h, att, their_h, their_far, grad_mixed, their_mixed,
    ]
    cut1 = total1 * 9 // 25 // LANES * LANES
    mid = cut1 + (total1 - cut1) // 2 // LANES * LANES
    emit1 = [(GRAD_C, (0, cut1)), (GRAD_A, (cut1, mid)), (GRAD_B, (mid, total1))]
    cfg1 = dict(
        ffn_cfg, tokens=tokens, total=total1, gain_lane=tail, emit=emit1, gain_from=(3, 5)
    )
    pieces1 = grads(sections1, operands1, cfg1)
    grad_inputs, swap2, keep2 = call(
        functools.partial(attn_backward_kernel, cfg),
        [
            inputs, grad_hidden, wo_full, w_full, qkv, att, logt,
            seg_row, seg_col, live_row, cosine, sine, n1,
        ],
        [
            shape(tokens, model, dtype=F32),
            shape(tokens + 16, model + 3 * half),
            shape(tokens, 3 * half),
        ],
        [pltpu.VMEM((tokens, width), BF16), pltpu.VMEM((tokens, 3 * width), BF16)],
        scalars=0,
        flops=2 * tokens * model * 5 * width,
        spare=6 << 20,
    )
    total2 = 3 * half + LANES
    emit2 = [(GRAD_A, (0, total2 // 2)), (GRAD_B, (total2 // 2, total2))]
    cfg2 = dict(cfg, tokens=tokens, total=total2, gain_lane=0, emit=emit2, gain_from=(0, 2))
    sections2 = [((((0, 0), (1, 0)), ((2, 0), (2, model))), 0, 3 * half)]
    operands2 = [swap2, keep2, swap_cores(swap2)]
    pieces2 = grads(sections2, operands2, cfg2)

    if fast:
        keep_c, send_c, keep_a, send_a, keep_b, send_b = pieces1
        keep_a, send_a, keep_b, send_b = combine(
            False, keep_a, exchange(send_a, X), keep_b, exchange(send_b, Y)
        )
        keep_c, send_c = combine(False, keep_c, exchange(send_c, Z))
        keep_c, send_c = combine(False, keep_c, exchange(send_c, ZZ))
        keep, send = combine(True, keep_a, exchange(send_a, Y), keep_b, exchange(send_b, X))
        keep_c, send_c = combine(False, keep_c, exchange(send_c, X))
        keep, send = combine(False, keep, exchange(send, Z))
        came_c, came = exchange(send_c, Y), exchange(send, ZZ)
        share1 = call(
            final_ffn_kernel,
            [keep_c, came_c, keep, came],
            [shape(rows, total1, dtype=F32)],
            [],
            scalars=0,
        )[0]
        keep_a, send_a, keep_b, send_b = pieces2
        keep_a, send_a, keep_b, send_b = combine(
            False, keep_a, exchange(send_a, X), keep_b, exchange(send_b, Y)
        )
        keep, send = combine(True, keep_a, exchange(send_a, Y), keep_b, exchange(send_b, X))
        keep, send = combine(False, keep, exchange(send, Z))
        grad_qkv, grad_gain1 = call(
            final_qkv_kernel,
            [keep, exchange(send, ZZ), gain_col],
            [shape(3, rows, half, dtype=F32), shape(rows, dtype=F32)],
            [],
            scalars=0,
        )
    else:
        share1, share2 = (
            lax.psum_scatter(pieces[0], "dp", scatter_dimension=0, tiled=True)
            for pieces in (pieces1, pieces2)
        )
        grad_qkv = jnp.stack([share2[:, c * half : (c + 1) * half] * gain_col for c in range(3)])
        grad_gain1 = share2[:, 3 * half] / gain_col[:, 0]
    heads = share1[:, : 2 * main].reshape(rows, 2, main)
    tails = share1[:, 2 * main : 2 * units].reshape(rows, 2, tail)
    grad_in = jnp.concatenate([heads, tails], axis=2)
    grad_out = share1[:, 2 * units : 2 * units + half].T
    grad_down = share1[:, 2 * units + half : 2 * units + half + units].T
    grad_gain2 = share1[:, 2 * units + half + units]
    return (
        output,
        grad_inputs,
        grad_gain1,
        grad_qkv,
        grad_out,
        grad_gain2,
        grad_in,
        grad_down,
    )


def fast_path(dp):
    return dp == 16


def solution(mesh):
    in_specs = (
        P(("dp", "tensor"), None),
        P("dp"),
        P(None, "dp", "tensor"),
        P("tensor", "dp"),
        P("dp"),
        P("dp", None, "tensor"),
        P("tensor", "dp"),
        P(("dp", "tensor"), None),
        P("dp", None),
        P("dp"),
        P("dp"),
    )
    out_specs = (
        P(("dp", "tensor"), None),
        P(("dp", "tensor"), None),
        P("dp"),
        P(None, "dp", "tensor"),
        P("tensor", "dp"),
        P("dp"),
        P("dp", None, "tensor"),
        P("tensor", "dp"),
    )

    return jax.shard_map(shards, mesh=mesh, in_specs=in_specs, out_specs=out_specs, check_vma=False)
```
